32 devices in a mesh: dp: 8 (over z, x), tensor: 4 (over y, core).
Axes of the slice: x: 2, y: 2, z: 4, core: 2. Of those that a mesh axis runs over, the one named last changes fastest.
Arguments:
- tokens: bfloat16 [1024, 8192], P('dp', 'tensor'), may hold values from -6 to 6
- key_value_weight: bfloat16 [8192, 2048], P('tensor'), may hold values from -0.0625 to 0.0625
- adapter_down_weight: bfloat16 [24, 64, 8192], P('dp', None, 'tensor'), may hold values from -0.0625 to 0.0625
- adapter_up_weight: bfloat16 [24, 64, 2048], P('dp', None, 'tensor'), may hold values from -0.75 to 0.75
- cotangent: bfloat16 [1024, 2048], P('dp', 'tensor'), may hold values from -3 to 3
- sequence_adapter_index: int32 [32], replicated, may hold values from 0 to 23, as said below
- adapter_storage_row: int32 [24], replicated, may hold values from 0 to 23, as said below
Outputs:
- key_value_output: bfloat16 [1024, 2048], P('dp', 'tensor')
- token_gradient: bfloat16 [1024, 8192], P('dp', 'tensor')
- grad_down: float32 [24, 64, 8192], P('dp', None, 'tensor')
- grad_up: float32 [24, 64, 2048], P('dp', None, 'tensor')
The draws below stay inside these ranges and needn't reach their ends.
Inputs may be any that keep to these rules, and one draw needn't show every extreme that they name: Each value appears once: adapter a is held at row adapter_storage_row[a] of adapter_down_weight, adapter_up_weight, grad_down and grad_up, on index adapter_storage_row[a] // 3 of dp. `sequence_adapter_index`: the 4 sequences i that share one value of i // 4 use adapters held on 4 different indices of dp.
All inputs are finite; a program needn't handle non-finite values.
Results may differ from the reference program's by a relative error of at most 0.02.
Values may be sent and summed in bfloat16 or wider, within the bound.
A program may use at most 64 MiB of HBM per device.

```python
import jax
import jax.numpy as jnp
from jax import lax

MODEL_WIDTH = 8192
ADAPTER_RANK = 64
SEQS_DEV = 4
ADP_DEV = 3
KEY_VALUE_WIDTH = 2048
TOKENS = 1024
ADAPTER_TOTAL = 24
N_DP = 8
N_TENSOR = 4


def adapter_tables(key):
    base_key = jax.random.fold_in(key, 11)
    storage = jax.random.permutation(jax.random.fold_in(base_key, 1), ADP_DEV * N_DP).astype(jnp.int32)
    reader_keys = jax.random.split(jax.random.fold_in(base_key, 2), N_DP)

    def owners_for(reader_key):
        return jax.random.permutation(reader_key, N_DP)[:SEQS_DEV]
    owners = jax.vmap(owners_for)(reader_keys).astype(jnp.int32)
    draw_one = jax.random.randint(jax.random.fold_in(base_key, 3), (N_DP, SEQS_DEV), 0, ADP_DEV)
    draw_two = jax.random.randint(jax.random.fold_in(base_key, 4), (N_DP, SEQS_DEV), 0, ADP_DEV)
    within = jnp.minimum(draw_one, draw_two).astype(jnp.int32)
    held_rows = (owners * ADP_DEV + within).reshape(-1)
    inverse = jnp.argsort(storage).astype(jnp.int32)
    chosen = inverse[held_rows]
    return (storage, chosen.astype(jnp.int32))


def draw_adapter_storage_row(key, part):
    return adapter_tables(key)[0]


def draw_sequence_adapter_index(key, part):
    return adapter_tables(key)[1]


def block_levels(stream_key, shape, cuts, low, top_value):
    factor_of = 1.0
    for axis_at, shards_of in cuts:
        draws = jax.random.uniform(jax.random.fold_in(jax.random.fold_in(stream_key, 6), axis_at), (shards_of,), jnp.float32, low / len(cuts), top_value / len(cuts))
        factor_of = factor_of * jnp.repeat(jnp.exp(draws), shape[axis_at] // shards_of).reshape((-1,) + (1,) * (len(shape) - 1 - axis_at))
    return factor_of


def scatter_about(rng, dims, deviation, bound, cuts=(), held_as=jnp.bfloat16):
    factor_of = block_levels(rng, dims, cuts, -0.22, 0.18) if cuts else 1.0
    array = jax.random.normal(rng, dims, jnp.float32) * deviation * factor_of
    return jnp.minimum(jnp.maximum(array, -bound), bound).astype(held_as)


def setup_inputs(seed: int = 0) -> dict:
    keys = jax.random.split(jax.random.key(seed), 8)
    return {
        "tokens": scatter_about(keys[0], (TOKENS, MODEL_WIDTH), 1.0, 6.0, ((0, 8), (1, 4))),
        "key_value_weight": scatter_about(keys[1], (MODEL_WIDTH, KEY_VALUE_WIDTH), MODEL_WIDTH ** -0.5, 0.0625, ((0, 4),)),
        "adapter_down_weight": scatter_about(keys[2], (ADAPTER_TOTAL, ADAPTER_RANK, MODEL_WIDTH), MODEL_WIDTH ** -0.5, 0.0625, ((0, 8), (2, 4))),
        "adapter_up_weight": scatter_about(keys[3], (ADAPTER_TOTAL, ADAPTER_RANK, KEY_VALUE_WIDTH), ADAPTER_RANK ** -0.5, 0.75, ((0, 8), (2, 4))),
        "cotangent": scatter_about(keys[4], (TOKENS, KEY_VALUE_WIDTH), 0.5, 3.0, ((0, 8), (1, 4))),
        "sequence_adapter_index": draw_sequence_adapter_index(jax.random.fold_in(keys[7], 71), 0),
        "adapter_storage_row": draw_adapter_storage_row(jax.random.fold_in(keys[7], 71), 0),
    }


adapter_scale = 0.25


def reference(tokens, key_value_weight, adapter_down_weight, adapter_up_weight, cotangent, sequence_adapter_index, adapter_storage_row):
    adapters = adapter_storage_row.shape[0]
    seq_total = sequence_adapter_index.shape[0]
    adapter_codes = jnp.arange(adapters, dtype=jnp.int32)
    matches = sequence_adapter_index[:, None] == adapter_codes[None, :]
    seq_rows = jnp.sum(jnp.where(matches, adapter_storage_row[None, :], 0), axis=1).astype(jnp.int32)
    row_hits = seq_rows[:, None] == adapter_codes[None, :]
    usage_count = jnp.sum(row_hits.astype(jnp.float32), axis=0)
    inverse_use = 1.0 / jnp.maximum(usage_count, 1.0)
    feature_width = tokens.shape[1]
    seq_length = tokens.shape[0] // seq_total
    block_span = feature_width // N_TENSOR
    out_width = key_value_weight.shape[1]
    weight_blocks = key_value_weight.reshape(N_TENSOR, block_span, out_width).astype(jnp.float32)
    weight_turned = key_value_weight.T
    token_sequences = tokens.reshape(seq_total, seq_length, feature_width)
    cot_seqs = cotangent.reshape(seq_total, seq_length, out_width)

    def one_sequence(totals, inputs):
        grad_down, grad_up = totals
        sequence_tokens, sequence_cotangent, sequence_row = inputs
        down_matrix_rows = lax.dynamic_index_in_dim(adapter_down_weight, sequence_row, 0, keepdims=False)
        up_matrix_rows = lax.dynamic_index_in_dim(adapter_up_weight, sequence_row, 0, keepdims=False)
        pieces = sequence_tokens.reshape(seq_length, N_TENSOR, block_span).astype(jnp.float32)
        partial_value = jnp.einsum("lnd,ndo->nlo", pieces, weight_blocks)
        partial_round = lax.optimization_barrier(partial_value.astype(jnp.bfloat16)).astype(jnp.float32)
        frozen_backbone = jnp.sum(partial_round, axis=0)
        inner_full = jnp.dot(sequence_tokens, down_matrix_rows.T, preferred_element_type=jnp.float32)
        middle_round = inner_full.astype(jnp.bfloat16)
        back_full = jnp.dot(sequence_cotangent, up_matrix_rows.T, preferred_element_type=jnp.float32)
        backward_round = back_full.astype(jnp.bfloat16)
        output_list = (frozen_backbone + adapter_scale * jnp.dot(middle_round, up_matrix_rows, preferred_element_type=jnp.float32)).astype(jnp.bfloat16)
        grad_in = (jnp.dot(sequence_cotangent, weight_turned, preferred_element_type=jnp.float32)
                   + adapter_scale * jnp.dot(backward_round, down_matrix_rows, preferred_element_type=jnp.float32)).astype(jnp.bfloat16)
        down_term = (adapter_scale * jnp.dot(backward_round.T, sequence_tokens, preferred_element_type=jnp.float32)).astype(jnp.bfloat16)
        up_term = (adapter_scale * jnp.dot(middle_round.T, sequence_cotangent, preferred_element_type=jnp.float32)).astype(jnp.bfloat16)
        grad_down = grad_down.at[sequence_row].add(down_term.astype(jnp.float32))
        grad_up = grad_up.at[sequence_row].add(up_term.astype(jnp.float32))
        return (grad_down, grad_up), (output_list, grad_in)

    down_start_offset = jnp.zeros(adapter_down_weight.shape, jnp.float32)
    up_start_offset = jnp.zeros(adapter_up_weight.shape, jnp.float32)
    (grad_down, grad_up), (output_list, grad_in) = lax.scan(one_sequence, (down_start_offset, up_start_offset), (token_sequences, cot_seqs, seq_rows))
    key_value_output = output_list.reshape(seq_total * seq_length, out_width)
    token_gradient = grad_in.reshape(seq_total * seq_length, feature_width)
    grad_down = grad_down * inverse_use[:, None, None]
    grad_up = grad_up * inverse_use[:, None, None]
    return (key_value_output, token_gradient, grad_down, grad_up)
```

```python
import functools

import jax
import jax.numpy as jnp
from jax import lax
from jax.experimental import pallas as pl
from jax.experimental.pallas import tpu as pltpu
from jax.sharding import PartitionSpec as P

adapter_scale = 0.25
MESH = pl.DeviceIdType.MESH
F32 = jnp.float32
BF16 = jnp.bfloat16


def nt_dot(a, b):
    return lax.dot_general(a, b, (((1,), (1,)), ((), ())), preferred_element_type=F32)


def tn_dot(a, b):
    return lax.dot_general(a, b, (((0,), (0,)), ((), ())), preferred_element_type=F32)


def partner(d, k, dp_count):
    out, bit = d, 1
    while bit < dp_count:
        if k & bit:
            out = out + bit - 2 * bit * lax.rem(lax.div(d, jnp.int32(bit)), jnp.int32(2))
        bit *= 2
    return out


def routes(dp_count, seqs, resident, seq_ref, store_ref, table_ref, weight_ref):
    d = lax.axis_index("dp")
    rows = [store_ref[seq_ref[d * seqs + j]] for j in range(seqs)]
    owners = [lax.div(r, jnp.int32(resident)) for r in rows]
    dist = []
    for j in range(seqs):
        slot = jnp.int32(0)
        for k in range(1, dp_count):
            slot = jnp.where(owners[j] == partner(d, k, dp_count), jnp.int32(k), slot)
        dist.append(slot)
    for j in range(seqs):
        table_ref[2 * dp_count + j] = dist[j]
    for k in range(dp_count):
        pick = jnp.int32(0)
        for j in range(seqs):
            pick = jnp.where(dist[j] == k, jnp.int32(j), pick)
        table_ref[k] = pick
    counts = [jnp.float32(0.0)] * resident
    for k in range(dp_count):
        reader = partner(d, k, dp_count)
        found = jnp.int32(-1)
        for j in range(seqs):
            local = store_ref[seq_ref[reader * seqs + j]] - d * resident
            found = jnp.where((local >= 0) & (local < resident), local, found)
        table_ref[dp_count + k] = jnp.maximum(found, 0)
        for a in range(resident):
            hit = jnp.where(found == a, jnp.float32(1.0), jnp.float32(0.0))
            weight_ref[a * dp_count + k] = hit
            counts[a] = counts[a] + hit
    for a in range(resident):
        weight_ref[resident * dp_count + a] = counts[a]


def slot_groups(dp_count):
    order = list(range(dp_count - 1, -1, -1))
    quarter = dp_count // 4
    return [order[:quarter], order[quarter:2 * quarter], order[2 * quarter:]]


def kernel(
    dp_count,
    tensor_count,
    table_ref,
    weight_ref,
    tok_ref,
    w_ref,
    down_hbm,
    up_hbm,
    cot_ref,
    cot_seq_ref,
    kvo_ref,
    tg_ref,
    gd_hbm,
    gu_hbm,
    down_ref,
    up_ref,
    gd_ref,
    gu_ref,
    w_v,
    slot_out,
    slot_in,
    ret_out,
    ret_in,
    cots,
    parts,
    part_in,
    ranks,
    back_m,
    inner_m,
    acc,
    w_sem,
    local_sem,
    slot_ssem,
    slot_rsem,
    ret_ssem,
    ret_rsem,
    cot_ssem,
    cot_rsem,
    part_ssem,
    part_rsem,
    rank_ssem,
    rank_rsem,
):
    d = lax.axis_index("dp")
    t = lax.axis_index("tensor")
    resident, rank, block = down_ref.shape
    out_block = up_ref.shape[2]
    seqs, length = tok_ref.shape[:2]
    rows = seqs * length
    groups = slot_groups(dp_count)
    starts = [sum(len(g) for g in groups[:i]) for i in range(len(groups))]

    def dp_to(k):
        return partner(d, k, dp_count)

    def t_to(q):
        return lax.rem(t + q, tensor_count)

    def t_from(q):
        return lax.rem(t + tensor_count - q, tensor_count)

    def w_copy(i):
        c = t_to(i)
        return pltpu.make_async_copy(
            w_ref.at[:, pl.ds(pl.multiple_of(c * out_block, out_block), out_block)],
            w_v.at[i],
            w_sem.at[i],
        )

    down_copy = pltpu.make_async_copy(down_hbm, down_ref, local_sem.at[0])
    up_copy = pltpu.make_async_copy(up_hbm, up_ref, local_sem.at[1])
    gd_copy = pltpu.make_async_copy(gd_ref, gd_hbm, local_sem.at[2])
    gu_copy = pltpu.make_async_copy(gu_ref, gu_hbm, local_sem.at[3])
    for i in range(tensor_count):
        w_copy(i).start()
    down_copy.start()
    up_copy.start()

    barrier = pltpu.get_barrier_semaphore()
    for k in range(1, dp_count):
        pl.semaphore_signal(barrier, inc=1, device_id={"dp": dp_to(k)}, device_id_type=MESH)
    for q in range(1, tensor_count):
        pl.semaphore_signal(barrier, inc=1, device_id={"tensor": t_to(q)}, device_id_type=MESH)

    for k in range(dp_count):
        pick = table_ref[k]
        target = slot_in if k == 0 else slot_out
        target[k * length:(k + 1) * length, :block] = tok_ref[pick]
        target[k * length:(k + 1) * length, block:] = cot_seq_ref[pick]

    pl.semaphore_wait(barrier, dp_count + tensor_count - 2)

    def cot_copy(q):
        return pltpu.make_async_remote_copy(
            cot_ref, cots.at[q], cot_ssem.at[q], cot_rsem.at[q],
            device_id={"tensor": t_to(q)}, device_id_type=MESH)

    def slot_copy(k):
        at = pl.ds(k * length, length)
        return pltpu.make_async_remote_copy(
            slot_out.at[at], slot_in.at[at], slot_ssem.at[k], slot_rsem.at[k],
            device_id={"dp": dp_to(k)}, device_id_type=MESH)

    def ret_copy(k):
        return pltpu.make_async_remote_copy(
            ret_out.at[k], ret_in.at[k], ret_ssem.at[k], ret_rsem.at[k],
            device_id={"dp": dp_to(k)}, device_id_type=MESH)

    def part_copy(q):
        return pltpu.make_async_remote_copy(
            parts.at[q], part_in.at[q], part_ssem.at[q], part_rsem.at[q],
            device_id={"tensor": t_to(q)}, device_id_type=MESH)

    def rank_rows(g):
        return pl.ds(starts[g] * length, len(groups[g]) * length)

    def rank_copy(g, q):
        return pltpu.make_async_remote_copy(
            ranks.at[t, rank_rows(g)], ranks.at[t, rank_rows(g)], rank_ssem.at[g, q], rank_rsem.at[g, q],
            device_id={"tensor": t_to(q)}, device_id_type=MESH)

    for k in range(dp_count - 1, 0, -1):
        slot_copy(k).start()
    for q in range(1, tensor_count):
        cot_copy(q).start()

    adapter_of = [table_ref[dp_count + k] for k in range(dp_count)]
    weights = [[weight_ref[a * dp_count + k] for k in range(dp_count)] for a in range(resident)]
    counts = [weight_ref[resident * dp_count + a] for a in range(resident)]

    def frozen_block(i, carry):
        w_copy(i).wait()
        parts[i] = jnp.dot(tok_ref[...].reshape(rows, block), w_v[i], preferred_element_type=F32).astype(BF16)
        return carry

    lax.fori_loop(0, tensor_count, frozen_block, 0)

    def rank_stage(g):
        for m, k in enumerate(groups[g]):
            if k:
                slot_copy(k).wait_recv()
            x = slot_in[k * length:(k + 1) * length, :block]
            c = slot_in[k * length:(k + 1) * length, block:]
            inner = nt_dot(x, down_ref[adapter_of[k]])
            back = nt_dot(c, up_ref[adapter_of[k]])
            ranks[t, (starts[g] + m) * length:(starts[g] + m + 1) * length, :] = jnp.concatenate(
                [inner, back], axis=1).astype(BF16)
        for q in range(1, tensor_count):
            rank_copy(g, q).start()

    def base_block(i, carry):
        q = lax.rem(tensor_count - i, tensor_count)
        acc[...] += nt_dot(cots[q], w_v[i])
        return carry

    def use_stage(g):
        for q in range(1, tensor_count):
            s = t_from(q)
            pltpu.make_async_remote_copy(
                ranks.at[s, rank_rows(g)], ranks.at[s, rank_rows(g)], rank_ssem.at[g, q], rank_rsem.at[g, q],
                device_id={"tensor": t_to(q)}, device_id_type=MESH).wait_recv()
        for q in range(1, tensor_count):
            rank_copy(g, q).wait_send()
        total = ranks[0, rank_rows(g)].astype(F32)
        for s in range(1, tensor_count):
            total = total + ranks[s, rank_rows(g)].astype(F32)
        for m, k in enumerate(groups[g]):
            lines = total[m * length:(m + 1) * length]
            inner = lines[:, :rank].astype(BF16)
            back = lines[:, rank:].astype(BF16)
            target = ret_out if k else ret_in
            target[k, :, :block] = (adapter_scale * jnp.dot(
                back, down_ref[adapter_of[k]], preferred_element_type=F32)).astype(BF16)
            target[k, :, block:] = (adapter_scale * jnp.dot(
                inner, up_ref[adapter_of[k]], preferred_element_type=F32)).astype(BF16)
            for a in range(resident):
                at = slice(k * length, (k + 1) * length)
                back_m[a, at, :] = (back.astype(F32) * weights[a][k]).astype(BF16)
                inner_m[a, at, :] = (inner.astype(F32) * weights[a][k]).astype(BF16)
            if k:
                ret_copy(k).start()

    for q in range(1, tensor_count):
        part_copy(q).start()
    half = max(1, tensor_count // 2)
    acc[...] = nt_dot(cot_ref[...], w_v[0])
    for q in range(1, tensor_count):
        cot_copy(q).wait_recv()
    lax.fori_loop(1, half, base_block, 0)
    down_copy.wait()
    up_copy.wait()
    rank_stage(0)
    lax.fori_loop(half, tensor_count, base_block, 0)
    use_stage(0)
    rank_stage(1)
    use_stage(1)
    rank_stage(2)
    use_stage(2)

    x_all = slot_in[:, :block]
    c_all = slot_in[:, block:]
    for a in range(resident):
        gd_ref[a] = tn_dot(back_m[a], x_all) * (
            adapter_scale / jnp.maximum(jnp.full((1, block), counts[a], F32), 1.0))
        gu_ref[a] = tn_dot(inner_m[a], c_all) * (
            adapter_scale / jnp.maximum(jnp.full((1, out_block), counts[a], F32), 1.0))

    gd_copy.start()
    gu_copy.start()
    for q in range(1, tensor_count):
        part_copy(q).wait_recv()
    backbone = parts[0].astype(F32)
    for q in range(1, tensor_count):
        backbone = backbone + part_in[q].astype(F32)
    for k in range(1, dp_count):
        ret_copy(k).wait_recv()
    for j in range(seqs):
        at = slice(j * length, (j + 1) * length)
        came = ret_in[table_ref[2 * dp_count + j]]
        kvo_ref[at, :] = (backbone[at] + came[:, block:].astype(F32)).astype(BF16)
        tg_ref[at, :] = (acc[at, :] + came[:, :block].astype(F32)).astype(BF16)

    for k in range(1, dp_count):
        slot_copy(k).wait_send()
        ret_copy(k).wait_send()
    for q in range(1, tensor_count):
        cot_copy(q).wait_send()
        part_copy(q).wait_send()
    gd_copy.wait()
    gu_copy.wait()


def mix(first, second, flag):
    return jnp.where(flag > 0, first, second)


def relay_fits(dp_count, seqs):
    return dp_count == 2 * seqs and seqs == 4


def relay_routes(dp_count, seqs, resident, seq_ref, store_ref, table_ref, weight_ref):
    d = lax.axis_index("dp")
    half = dp_count // 2
    xor = lax.bitwise_xor
    level = lax.div(d, jnp.int32(2))
    inner = lax.rem(lax.div(level + 1, jnp.int32(2)), jnp.int32(2))
    home = (2 - lax.div(d, jnp.int32(half))) * 2 + lax.rem(d, jnp.int32(2))
    zero, one = jnp.int32(0), jnp.int32(1)
    worst = zero
    counts = [jnp.float32(0.0)] * resident
    for k in range(dp_count):
        p = xor(d, jnp.int32(k))
        crossing, found = zero, jnp.int32(-1)
        near = [zero] * half
        has, which = [zero] * half, [zero] * half
        apart = []
        for j in range(seqs):
            row = store_ref[seq_ref[p * seqs + j]]
            owner = lax.div(row, jnp.int32(resident))
            away = xor(owner, p)
            crossing = crossing + jnp.where(away >= half, one, zero)
            found = jnp.where(owner == d, row - d * resident, found)
            if k == 0:
                step = xor(owner, home)
                apart.append((away, step))
                for m in range(half):
                    near[m] = jnp.where(away == m, jnp.int32(j), near[m])
            if k in (0, half, half + 2):
                step = xor(owner, home if k == 0 else d)
                for m in range(half):
                    hit = step == half - 1 - m
                    has[m] = jnp.where(hit, one, has[m])
                    which[m] = jnp.where(hit, jnp.int32(j), which[m])
        worst = jnp.maximum(worst, crossing)
        if k == 0:
            for m in range(half):
                table_ref[m] = near[m]
            table_ref[half] = jnp.where(has[0] > 0, which[0], which[1])
            table_ref[half + 1] = jnp.where((has[0] > 0) & (has[1] > 0), which[1], which[2])
            table_ref[half + 2] = jnp.where(has[3] > 0, which[3], which[2])
            place = [zero, jnp.where(has[0] > 0, one, zero), jnp.where(has[3] > 0, one, jnp.int32(2)), jnp.int32(2)]
            for j in range(seqs):
                away, step = apart[j]
                came = away
                for m in range(half):
                    came = jnp.where(step == half - 1 - m, half + place[m], came)
                table_ref[8 + j] = came
        if k in (half, half + 2):
            q = 1 if k == half else 0
            table_ref[20 + 3 * q] = has[0]
            table_ref[21 + 3 * q] = has[0] * has[1]
            table_ref[22 + 3 * q] = has[3]
        s = jnp.int32(k) if k < half else xor(jnp.int32(k), 2 * inner)
        table_ref[12 + s] = jnp.maximum(found, 0)
        for a in range(resident):
            hit = jnp.where(found == a, jnp.float32(1.0), jnp.float32(0.0))
            weight_ref[a * dp_count + s] = hit
            counts[a] = counts[a] + hit
    for a in range(resident):
        weight_ref[resident * dp_count + a] = counts[a]
    table_ref[7] = jnp.where(worst < half, one, zero)


def relay_kernel(
    dp_count,
    tensor_count,
    table_ref,
    weight_ref,
    tok_ref,
    w_ref,
    down_hbm,
    up_hbm,
    cot_ref,
    cot_seq_ref,
    kvo_ref,
    tg_ref,
    gd_hbm,
    gu_hbm,
    down_ref,
    up_ref,
    gd_ref,
    gu_ref,
    w_v,
    near_out,
    cross_out,
    slot_in,
    relay_in,
    relay_out,
    ret_out,
    ret_in,
    relay_ret,
    back_out,
    cots,
    parts,
    part_in,
    ranks,
    back_m,
    inner_m,
    acc,
    w_sem,
    local_sem,
    near_ssem,
    slot_rsem,
    cross_ssem,
    relay_rsem,
    fwd_ssem,
    ret_ssem,
    ret_rsem,
    owner_rsem,
    back_ssem,
    cot_ssem,
    cot_rsem,
    part_ssem,
    part_rsem,
    rank_ssem,
    rank_rsem,
):
    d = lax.axis_index("dp")
    t = lax.axis_index("tensor")
    resident, rank, block = down_ref.shape
    out_block = up_ref.shape[2]
    seqs, length = tok_ref.shape[:2]
    rows = seqs * length
    half = dp_count // 2
    level = lax.div(d, jnp.int32(2))
    inner = lax.rem(lax.div(level + 1, jnp.int32(2)), jnp.int32(2))
    outer = 1 - inner
    home = (2 - lax.div(d, jnp.int32(half))) * 2 + lax.rem(d, jnp.int32(2))
    peer = [partner(d, k, dp_count) for k in range(dp_count)]
    groups = [[0, 1, 2, 3], [4, 5], [6, 7]]
    starts = [0, 4, 6]

    def t_to(q):
        return lax.rem(t + q, tensor_count)

    def t_from(q):
        return lax.rem(t + tensor_count - q, tensor_count)

    def lines(s):
        return slice(s * length, (s + 1) * length)

    def w_copy(i):
        c = t_to(i)
        return pltpu.make_async_copy(
            w_ref.at[:, pl.ds(pl.multiple_of(c * out_block, out_block), out_block)],
            w_v.at[i],
            w_sem.at[i],
        )

    def over(source, target, ssem, rsem, **where):
        return pltpu.make_async_remote_copy(
            source, target, ssem, rsem, device_id=where, device_id_type=MESH)

    def slot_at(s):
        return slot_in.at[pl.ds(s * length, length)]

    def near_copy(k):
        return over(near_out.at[k - 1], slot_at(k), near_ssem.at[k], slot_rsem.at[k], dp=peer[k])

    def cross_copy(i):
        return over(cross_out.at[i], relay_in.at[outer, i], cross_ssem.at[i], relay_rsem.at[outer, i], dp=home)

    def cross_came(q, i):
        return over(cross_out.at[i], relay_in.at[q, i], cross_ssem.at[i], relay_rsem.at[q, i], dp=home)

    def fwd_copy(q, m):
        source = relay_in.at[q, 0] if m == 0 else relay_out.at[q, m - 1]
        s = half + 2 * q + (0 if m == 1 else 1)
        return over(source, slot_at(s), fwd_ssem.at[q, m], slot_rsem.at[s], dp=peer[3 - m])

    def slot_came(s):
        return over(near_out.at[0], slot_at(s), near_ssem.at[0], slot_rsem.at[s], dp=peer[1])

    def ret_near(k):
        return over(ret_out.at[k], ret_in.at[k], ret_ssem.at[k], ret_rsem.at[k], dp=peer[k])

    def ret_same(q):
        s = half + 2 * q
        return over(ret_out.at[s], relay_ret.at[q, 1], ret_ssem.at[s], owner_rsem.at[q, 1], dp=peer[2])

    def ret_other(q):
        s = half + 2 * q + 1
        m = 2 * inner
        return over(ret_out.at[s], relay_ret.at[q, m], ret_ssem.at[s], owner_rsem.at[q, m],
                    dp=inner * peer[1] + outer * peer[3])

    def owner_came(q, m):
        return over(ret_out.at[1], relay_ret.at[q, m], ret_ssem.at[1], owner_rsem.at[q, m], dp=peer[1])

    def back_copy(q, i):
        return over(back_out.at[q, i], ret_in.at[half + i], back_ssem.at[q, i], ret_rsem.at[half + i],
                    dp=peer[half + 2 - 2 * q])

    def ret_came(i):
        return over(ret_out.at[1], ret_in.at[i], ret_ssem.at[1], ret_rsem.at[i], dp=peer[1])

    def cot_copy(q):
        return over(cot_ref, cots.at[q], cot_ssem.at[q], cot_rsem.at[q], tensor=t_to(q))

    def part_copy(q):
        return over(parts.at[q], part_in.at[q], part_ssem.at[q], part_rsem.at[q], tensor=t_to(q))

    def rank_rows(g):
        return pl.ds(starts[g] * length, len(groups[g]) * length)

    def rank_copy(g, q):
        at = ranks.at[t, rank_rows(g)]
        return over(at, at, rank_ssem.at[g, q], rank_rsem.at[g, q], tensor=t_to(q))

    def rank_came(g, q):
        at = ranks.at[t_from(q), rank_rows(g)]
        return over(at, at, rank_ssem.at[g, q], rank_rsem.at[g, q], tensor=t_to(q))

    down_copy = pltpu.make_async_copy(down_hbm, down_ref, local_sem.at[0])
    up_copy = pltpu.make_async_copy(up_hbm, up_ref, local_sem.at[1])
    gd_copy = pltpu.make_async_copy(gd_ref, gd_hbm, local_sem.at[2])
    gu_copy = pltpu.make_async_copy(gu_ref, gu_hbm, local_sem.at[3])

    barrier = pltpu.get_barrier_semaphore()
    for k in range(1, dp_count):
        pl.semaphore_signal(barrier, inc=1, device_id={"dp": peer[k]}, device_id_type=MESH)
    for q in range(1, tensor_count):
        pl.semaphore_signal(barrier, inc=1, device_id={"tensor": t_to(q)}, device_id_type=MESH)
    for i in range(tensor_count):
        w_copy(i).start()
    down_copy.start()
    up_copy.start()

    for i in range(half - 1):
        pick = table_ref[half + i]
        cross_out[i, :, :block] = tok_ref[pick]
        cross_out[i, :, block:] = cot_seq_ref[pick]
    for k in range(half):
        pick = table_ref[k]
        if k == 0:
            slot_in[:length, :block] = tok_ref[pick]
            slot_in[:length, block:] = cot_seq_ref[pick]
        else:
            near_out[k - 1, :, :block] = tok_ref[pick]
            near_out[k - 1, :, block:] = cot_seq_ref[pick]

    pl.semaphore_wait(barrier, dp_count + tensor_count - 2)

    @pl.when(inner == 1)
    def _():
        for i in range(half - 1):
            cross_copy(i).start()
        for k in (3, 2, 1):
            near_copy(k).start()

    @pl.when(inner == 0)
    def _():
        for k in (3, 2, 1):
            near_copy(k).start()
        for i in range(half - 1):
            cross_copy(i).start()

    for q in range(1, tensor_count):
        cot_copy(q).start()

    adapter_of = [table_ref[12 + s] for s in range(dp_count)]
    flags = [[table_ref[20 + 3 * q + i] for i in range(3)] for q in range(2)]
    weights = [[weight_ref[a * dp_count + s] for s in range(dp_count)] for a in range(resident)]
    counts = [weight_ref[resident * dp_count + a] for a in range(resident)]

    def relay(q, i):
        @pl.when(inner == 1)
        def _():
            cross_came(q, i).wait_recv()
            if i == 0:
                fwd_copy(q, 0).start()
            if i == 1:
                relay_out[q, 0] = mix(relay_in[q, 1], relay_in[q, 0], flags[q][0])
                fwd_copy(q, 1).start()
            if i == 2:
                relay_out[q, 1] = mix(relay_in[q, 1], relay_in[q, 2], flags[q][2])
                fwd_copy(q, 2).start()
                slot_in[lines(half + 2 * q), :] = relay_in[q, 2]

    def hand_back(q):
        @pl.when(inner == 1)
        def _():
            owner_came(q, 0).wait_recv()
            owner_came(q, 1).wait_recv()
            back_out[q, 0] = mix(relay_ret[q, 0], relay_ret[q, 1], flags[q][0])
            back_copy(q, 0).start()
            owner_came(q, 2).wait_recv()
            back_out[q, 1] = mix(relay_ret[q, 1], relay_ret[q, 2], flags[q][1])
            back_copy(q, 1).start()
            back_out[q, 2] = mix(ret_out[half + 2 * q], relay_ret[q, 2], flags[q][2])
            back_copy(q, 2).start()

    def frozen_block(i, carry):
        w_copy(i).wait()
        parts[i] = jnp.dot(tok_ref[...].reshape(rows, block), w_v[i], preferred_element_type=F32).astype(BF16)
        return carry

    def base_block(i, carry):
        q = lax.rem(tensor_count - i, tensor_count)
        acc[...] += nt_dot(cots[q], w_v[i])
        return carry

    def rank_stage(g):
        for s in groups[g]:
            if s and s < half:
                slot_came(s).wait_recv()
            if s >= half and s % 2 == 1:
                slot_came(s).wait_recv()
            if s >= half and s % 2 == 0:
                @pl.when(inner == 0)
                def _():
                    slot_came(s).wait_recv()
        for s in groups[g]:
            x = slot_in[lines(s), :block]
            c = slot_in[lines(s), block:]
            inner_s = nt_dot(x, down_ref[adapter_of[s]])
            back_s = nt_dot(c, up_ref[adapter_of[s]])
            ranks[t, lines(s), :] = jnp.concatenate([inner_s, back_s], axis=1).astype(BF16)
        for q in range(1, tensor_count):
            rank_copy(g, q).start()

    def use_stage(g):
        for q in range(1, tensor_count):
            rank_came(g, q).wait_recv()
        for q in range(1, tensor_count):
            rank_copy(g, q).wait_send()
        total = ranks[0, rank_rows(g)].astype(F32)
        for s in range(1, tensor_count):
            total = total + ranks[s, rank_rows(g)].astype(F32)
        for m, s in enumerate(groups[g]):
            part = total[m * length:(m + 1) * length]
            mid = part[:, :rank].astype(BF16)
            back = part[:, rank:].astype(BF16)
            target = ret_out if s else ret_in
            target[s, :, :block] = (adapter_scale * jnp.dot(
                back, down_ref[adapter_of[s]], preferred_element_type=F32)).astype(BF16)
            target[s, :, block:] = (adapter_scale * jnp.dot(
                mid, up_ref[adapter_of[s]], preferred_element_type=F32)).astype(BF16)
            if s and s < half:
                ret_near(s).start()
            if s >= half and s % 2 == 1:
                ret_other((s - half) // 2).start()
            if s >= half and s % 2 == 0:
                @pl.when(inner == 0)
                def _():
                    ret_same((s - half) // 2).start()
            for a in range(resident):
                back_m[a, lines(s), :] = (back.astype(F32) * weights[a][s]).astype(BF16)
                inner_m[a, lines(s), :] = (mid.astype(F32) * weights[a][s]).astype(BF16)

    middle = max(1, tensor_count // 2)
    lax.fori_loop(0, middle, frozen_block, 0)
    relay(0, 0)
    lax.fori_loop(middle, tensor_count, frozen_block, 0)
    for q in range(1, tensor_count):
        part_copy(q).start()
    relay(0, 1)
    acc[...] = nt_dot(cot_ref[...], w_v[0])
    for q in range(1, tensor_count):
        cot_copy(q).wait_recv()
    lax.fori_loop(1, middle, base_block, 0)
    down_copy.wait()
    up_copy.wait()
    rank_stage(0)
    relay(0, 2)
    use_stage(0)
    lax.fori_loop(middle, tensor_count, base_block, 0)
    relay(1, 0)
    rank_stage(1)
    relay(1, 1)
    use_stage(1)
    relay(1, 2)
    hand_back(0)
    rank_stage(2)
    use_stage(2)

    x_all = slot_in[:, :block]
    c_all = slot_in[:, block:]
    for a in range(resident):
        gd_ref[a] = tn_dot(back_m[a], x_all) * (
            adapter_scale / jnp.maximum(jnp.full((1, block), counts[a], F32), 1.0))
        gu_ref[a] = tn_dot(inner_m[a], c_all) * (
            adapter_scale / jnp.maximum(jnp.full((1, out_block), counts[a], F32), 1.0))
    gd_copy.start()
    gu_copy.start()
    hand_back(1)
    for q in range(1, tensor_count):
        part_copy(q).wait_recv()
    backbone = parts[0].astype(F32)
    for q in range(1, tensor_count):
        backbone = backbone + part_in[q].astype(F32)
    for i in range(1, dp_count - 1):
        ret_came(i).wait_recv()
    for j in range(seqs):
        came = ret_in[table_ref[8 + j]]
        kvo_ref[lines(j), :] = (backbone[lines(j)] + came[:, block:].astype(F32)).astype(BF16)
        tg_ref[lines(j), :] = (acc[lines(j), :] + came[:, :block].astype(F32)).astype(BF16)

    for k in range(1, half):
        near_copy(k).wait_send()
        ret_near(k).wait_send()
    for i in range(half - 1):
        cross_copy(i).wait_send()
    for q in range(2):
        ret_other(q).wait_send()

        @pl.when(inner == 0)
        def _():
            ret_same(q).wait_send()

        @pl.when(inner == 1)
        def _():
            for i in range(half - 1):
                fwd_copy(q, i).wait_send()
                back_copy(q, i).wait_send()
    for q in range(1, tensor_count):
        cot_copy(q).wait_send()
        part_copy(q).wait_send()
    gd_copy.wait()
    gu_copy.wait()


def finish(pieces, *refs):
    n = len(pieces)
    given, out, held = refs[:n], refs[n:2 * n], refs[2 * n:3 * n]
    in_sem, out_sem = refs[3 * n:]
    steps = [(i, p) for i in range(n) for p in range(pieces[i])]

    def move(i, p, source, target, sem, at):
        span = source.shape[0] // pieces[i]
        rows = pl.ds(p * span, span)
        return pltpu.make_async_copy(source.at[rows], target.at[rows], sem.at[at])

    for at, (i, p) in enumerate(steps):
        move(i, p, given[i], held[i], in_sem, at).start()
    for at, (i, p) in enumerate(steps):
        move(i, p, given[i], held[i], in_sem, at).wait()
        move(i, p, held[i], out[i], out_sem, at).start()
    for at, (i, p) in enumerate(steps):
        move(i, p, held[i], out[i], out_sem, at).wait()


def shapes_of(rows, block, out_block, resident, rank):
    return (
        jax.ShapeDtypeStruct((rows, out_block), BF16),
        jax.ShapeDtypeStruct((rows, block), BF16),
        jax.ShapeDtypeStruct((resident, rank, block), F32),
        jax.ShapeDtypeStruct((resident, rank, out_block), F32),
    )


def direct(dp_count, tensor_count, tok, w, down, up, cot, seq_index, storage):
    resident, rank, block = down.shape
    out_block = up.shape[2]
    rows = tok.shape[0]
    seqs = seq_index.shape[0] // dp_count
    length = rows // seqs
    groups = len(slot_groups(dp_count))
    anywhere = pl.BlockSpec(memory_space=pl.ANY)
    wide = block + out_block
    vmem = pl.BlockSpec(memory_space=pltpu.VMEM)
    smem = pl.BlockSpec(memory_space=pltpu.SMEM)
    dma = pltpu.SemaphoreType.DMA
    table, weights = pl.pallas_call(
        functools.partial(routes, dp_count, seqs, resident),
        out_shape=(
            jax.ShapeDtypeStruct((2 * dp_count + seqs,), jnp.int32),
            jax.ShapeDtypeStruct((resident * dp_count + resident,), F32),
        ),
        in_specs=[smem, smem],
        out_specs=(smem, smem),
    )(seq_index, storage)
    return pl.pallas_call(
        functools.partial(kernel, dp_count, tensor_count),
        out_shape=shapes_of(rows, block, out_block, resident, rank),
        in_specs=[smem, smem, vmem, anywhere, anywhere, anywhere, vmem, vmem],
        out_specs=(vmem, vmem, anywhere, anywhere),
        scratch_shapes=[
            pltpu.VMEM(down.shape, BF16),
            pltpu.VMEM(up.shape, BF16),
            pltpu.VMEM(down.shape, F32),
            pltpu.VMEM(up.shape, F32),
            pltpu.VMEM((tensor_count, w.shape[0], out_block), BF16),
            pltpu.VMEM((dp_count * length, wide), BF16),
            pltpu.VMEM((dp_count * length, wide), BF16),
            pltpu.VMEM((dp_count, length, wide), BF16),
            pltpu.VMEM((dp_count, length, wide), BF16),
            pltpu.VMEM((tensor_count, rows, out_block), BF16),
            pltpu.VMEM((tensor_count, rows, out_block), BF16),
            pltpu.VMEM((tensor_count, rows, out_block), BF16),
            pltpu.VMEM((tensor_count, dp_count * length, 2 * rank), BF16),
            pltpu.VMEM((resident, dp_count * length, rank), BF16),
            pltpu.VMEM((resident, dp_count * length, rank), BF16),
            pltpu.VMEM((rows, block), F32),
            dma((tensor_count,)),
            dma((4,)),
            dma((dp_count,)),
            dma((dp_count,)),
            dma((dp_count,)),
            dma((dp_count,)),
            dma((tensor_count,)),
            dma((tensor_count,)),
            dma((tensor_count,)),
            dma((tensor_count,)),
            dma((groups, tensor_count)),
            dma((groups, tensor_count)),
        ],
        compiler_params=pltpu.CompilerParams(
            collective_id=1, has_side_effects=True, vmem_limit_bytes=60 * 1024 * 1024
        ),
    )(
        table, weights, tok.reshape(seqs, length, block), w, down, up, cot,
        cot.reshape(seqs, length, out_block))


def relayed(dp_count, tensor_count, table, weights, tok, w, down, up, cot, seqs):
    resident, rank, block = down.shape
    out_block = up.shape[2]
    rows = tok.shape[0]
    length = rows // seqs
    half = dp_count // 2
    anywhere = pl.BlockSpec(memory_space=pl.ANY)
    wide = block + out_block
    vmem = pl.BlockSpec(memory_space=pltpu.VMEM)
    smem = pl.BlockSpec(memory_space=pltpu.SMEM)
    dma = pltpu.SemaphoreType.DMA

    def slots(*lead):
        return pltpu.VMEM(lead + (length, wide), BF16)

    return pl.pallas_call(
        functools.partial(relay_kernel, dp_count, tensor_count),
        out_shape=shapes_of(rows, block, out_block, resident, rank),
        in_specs=[smem, smem, vmem, anywhere, anywhere, anywhere, vmem, vmem],
        out_specs=(vmem, vmem, anywhere, anywhere),
        scratch_shapes=[
            pltpu.VMEM(down.shape, BF16),
            pltpu.VMEM(up.shape, BF16),
            pltpu.VMEM(down.shape, F32),
            pltpu.VMEM(up.shape, F32),
            pltpu.VMEM((tensor_count, w.shape[0], out_block), BF16),
            slots(half - 1),
            slots(half - 1),
            pltpu.VMEM((dp_count * length, wide), BF16),
            slots(2, half - 1),
            slots(2, half - 2),
            slots(dp_count),
            slots(dp_count - 1),
            slots(2, half - 1),
            slots(2, half - 1),
            pltpu.VMEM((tensor_count, rows, out_block), BF16),
            pltpu.VMEM((tensor_count, rows, out_block), BF16),
            pltpu.VMEM((tensor_count, rows, out_block), BF16),
            pltpu.VMEM((tensor_count, dp_count * length, 2 * rank), BF16),
            pltpu.VMEM((resident, dp_count * length, rank), BF16),
            pltpu.VMEM((resident, dp_count * length, rank), BF16),
            pltpu.VMEM((rows, block), F32),
            dma((tensor_count,)),
            dma((4,)),
            dma((half,)),
            dma((dp_count,)),
            dma((half - 1,)),
            dma((2, half - 1)),
            dma((2, half - 1)),
            dma((dp_count,)),
            dma((dp_count - 1,)),
            dma((2, half - 1)),
            dma((2, half - 1)),
            dma((tensor_count,)),
            dma((tensor_count,)),
            dma((tensor_count,)),
            dma((tensor_count,)),
            dma((3, tensor_count)),
            dma((3, tensor_count)),
        ],
        compiler_params=pltpu.CompilerParams(
            collective_id=0, has_side_effects=True, vmem_limit_bytes=60 * 1024 * 1024
        ),
    )(
        table, weights, tok.reshape(seqs, length, block), w, down, up, cot,
        cot.reshape(seqs, length, out_block))


def on_device(dp_count, tensor_count, tok, w, down, up, cot, seq_index, storage):
    resident = down.shape[0]
    seqs = seq_index.shape[0] // dp_count
    anywhere = pl.BlockSpec(memory_space=pl.ANY)
    smem = pl.BlockSpec(memory_space=pltpu.SMEM)
    dma = pltpu.SemaphoreType.DMA
    args = (tok, w, down, up, cot)
    if relay_fits(dp_count, seqs):
        table, weights = pl.pallas_call(
            functools.partial(relay_routes, dp_count, seqs, resident),
            out_shape=(
                jax.ShapeDtypeStruct((32,), jnp.int32),
                jax.ShapeDtypeStruct((resident * dp_count + resident,), F32),
            ),
            in_specs=[smem, smem],
            out_specs=(smem, smem),
        )(seq_index, storage)
        results = lax.cond(
            table[7] > 0,
            lambda: relayed(dp_count, tensor_count, table, weights, *args, seqs),
            lambda: direct(dp_count, tensor_count, *args, seq_index, storage),
        )
    else:
        results = direct(dp_count, tensor_count, *args, seq_index, storage)
    pieces = (1, 2, resident, 1)
    return pl.pallas_call(
        functools.partial(finish, pieces),
        out_shape=tuple(jax.ShapeDtypeStruct(r.shape, r.dtype) for r in results),
        in_specs=[anywhere] * 4,
        out_specs=(anywhere,) * 4,
        scratch_shapes=[pltpu.VMEM(r.shape, r.dtype) for r in results] + [
            dma((sum(pieces),)), dma((sum(pieces),))],
    )(*results)


def solution(mesh):
    in_specs = (
        P("dp", "tensor"),
        P("tensor", None),
        P("dp", None, "tensor"),
        P("dp", None, "tensor"),
        P("dp", "tensor"),
        P(),
        P(),
    )
    out_specs = (
        P("dp", "tensor"),
        P("dp", "tensor"),
        P("dp", None, "tensor"),
        P("dp", None, "tensor"),
    )
    return jax.shard_map(
        functools.partial(on_device, mesh.shape["dp"], mesh.shape["tensor"]),
        mesh=mesh, in_specs=in_specs, out_specs=out_specs, check_vma=False,
    )
```

```python
import functools

import jax
import jax.numpy as jnp
from jax import lax
from jax.experimental import pallas as pl
from jax.experimental.pallas import tpu as pltpu
from jax.sharding import PartitionSpec as P

adapter_scale = 0.25
MESH = pl.DeviceIdType.MESH
F32 = jnp.float32
BF16 = jnp.bfloat16


def nt_dot(a, b):
    return lax.dot_general(a, b, (((1,), (1,)), ((), ())), preferred_element_type=F32)


def tn_dot(a, b):
    return lax.dot_general(a, b, (((0,), (0,)), ((), ())), preferred_element_type=F32)


def partner(d, k, dp_count):
    out, bit = d, 1
    while bit < dp_count:
        if k & bit:
            out = out + bit - 2 * bit * lax.rem(lax.div(d, jnp.int32(bit)), jnp.int32(2))
        bit *= 2
    return out


def routes(dp_count, seqs, resident, seq_ref, store_ref, table_ref, weight_ref):
    d = lax.axis_index("dp")
    rows = [store_ref[seq_ref[d * seqs + j]] for j in range(seqs)]
    owners = [lax.div(r, jnp.int32(resident)) for r in rows]
    dist = []
    for j in range(seqs):
        slot = jnp.int32(0)
        for k in range(1, dp_count):
            slot = jnp.where(owners[j] == partner(d, k, dp_count), jnp.int32(k), slot)
        dist.append(slot)
    for j in range(seqs):
        table_ref[2 * dp_count + j] = dist[j]
    for k in range(dp_count):
        pick = jnp.int32(0)
        for j in range(seqs):
            pick = jnp.where(dist[j] == k, jnp.int32(j), pick)
        table_ref[k] = pick
    counts = [jnp.float32(0.0)] * resident
    for k in range(dp_count):
        reader = partner(d, k, dp_count)
        found = jnp.int32(-1)
        for j in range(seqs):
            local = store_ref[seq_ref[reader * seqs + j]] - d * resident
            found = jnp.where((local >= 0) & (local < resident), local, found)
        table_ref[dp_count + k] = jnp.maximum(found, 0)
        for a in range(resident):
            hit = jnp.where(found == a, jnp.float32(1.0), jnp.float32(0.0))
            weight_ref[a * dp_count + k] = hit
            counts[a] = counts[a] + hit
    for a in range(resident):
        weight_ref[resident * dp_count + a] = counts[a]


def slot_groups(dp_count):
    order = list(range(dp_count - 1, -1, -1))
    quarter = dp_count // 4
    return [order[:quarter], order[quarter:2 * quarter], order[2 * quarter:]]


def kernel(
    dp_count,
    tensor_count,
    table_ref,
    weight_ref,
    tok_ref,
    w_ref,
    down_hbm,
    up_hbm,
    cot_ref,
    cot_seq_ref,
    kvo_ref,
    tg_ref,
    gd_hbm,
    gu_hbm,
    down_ref,
    up_ref,
    gd_ref,
    gu_ref,
    w_v,
    slot_out,
    slot_in,
    ret_out,
    ret_in,
    cots,
    parts,
    part_in,
    ranks,
    back_m,
    inner_m,
    acc,
    w_sem,
    local_sem,
    slot_ssem,
    slot_rsem,
    ret_ssem,
    ret_rsem,
    cot_ssem,
    cot_rsem,
    part_ssem,
    part_rsem,
    rank_ssem,
    rank_rsem,
):
    d = lax.axis_index("dp")
    t = lax.axis_index("tensor")
    resident, rank, block = down_ref.shape
    out_block = up_ref.shape[2]
    seqs, length = tok_ref.shape[:2]
    rows = seqs * length
    groups = slot_groups(dp_count)
    starts = [sum(len(g) for g in groups[:i]) for i in range(len(groups))]

    def dp_to(k):
        return partner(d, k, dp_count)

    def t_to(q):
        return lax.rem(t + q, tensor_count)

    def t_from(q):
        return lax.rem(t + tensor_count - q, tensor_count)

    def w_copy(i):
        c = t_to(i)
        return pltpu.make_async_copy(
            w_ref.at[:, pl.ds(pl.multiple_of(c * out_block, out_block), out_block)],
            w_v.at[i],
            w_sem.at[i],
        )

    down_copy = pltpu.make_async_copy(down_hbm, down_ref, local_sem.at[0])
    up_copy = pltpu.make_async_copy(up_hbm, up_ref, local_sem.at[1])
    gd_copy = pltpu.make_async_copy(gd_ref, gd_hbm, local_sem.at[2])
    gu_copy = pltpu.make_async_copy(gu_ref, gu_hbm, local_sem.at[3])
    for i in range(tensor_count):
        w_copy(i).start()
    down_copy.start()
    up_copy.start()

    barrier = pltpu.get_barrier_semaphore()
    for k in range(1, dp_count):
        pl.semaphore_signal(barrier, inc=1, device_id={"dp": dp_to(k)}, device_id_type=MESH)
    for q in range(1, tensor_count):
        pl.semaphore_signal(barrier, inc=1, device_id={"tensor": t_to(q)}, device_id_type=MESH)

    for k in range(dp_count):
        pick = table_ref[k]
        target = slot_in if k == 0 else slot_out
        target[k * length:(k + 1) * length, :block] = tok_ref[pick]
        target[k * length:(k + 1) * length, block:] = cot_seq_ref[pick]

    pl.semaphore_wait(barrier, dp_count + tensor_count - 2)

    def cot_copy(q):
        return pltpu.make_async_remote_copy(
            cot_ref, cots.at[q], cot_ssem.at[q], cot_rsem.at[q],
            device_id={"tensor": t_to(q)}, device_id_type=MESH)

    def slot_copy(k):
        at = pl.ds(k * length, length)
        return pltpu.make_async_remote_copy(
            slot_out.at[at], slot_in.at[at], slot_ssem.at[k], slot_rsem.at[k],
            device_id={"dp": dp_to(k)}, device_id_type=MESH)

    def ret_copy(k):
        return pltpu.make_async_remote_copy(
            ret_out.at[k], ret_in.at[k], ret_ssem.at[k], ret_rsem.at[k],
            device_id={"dp": dp_to(k)}, device_id_type=MESH)

    def part_copy(q):
        return pltpu.make_async_remote_copy(
            parts.at[q], part_in.at[q], part_ssem.at[q], part_rsem.at[q],
            device_id={"tensor": t_to(q)}, device_id_type=MESH)

    def rank_rows(g):
        return pl.ds(starts[g] * length, len(groups[g]) * length)

    def rank_copy(g, q):
        return pltpu.make_async_remote_copy(
            ranks.at[t, rank_rows(g)], ranks.at[t, rank_rows(g)], rank_ssem.at[g, q], rank_rsem.at[g, q],
            device_id={"tensor": t_to(q)}, device_id_type=MESH)

    for k in range(dp_count - 1, 0, -1):
        slot_copy(k).start()
    for q in range(1, tensor_count):
        cot_copy(q).start()

    adapter_of = [table_ref[dp_count + k] for k in range(dp_count)]
    weights = [[weight_ref[a * dp_count + k] for k in range(dp_count)] for a in range(resident)]
    counts = [weight_ref[resident * dp_count + a] for a in range(resident)]

    def frozen_block(i, carry):
        w_copy(i).wait()
        parts[i] = jnp.dot(tok_ref[...].reshape(rows, block), w_v[i], preferred_element_type=F32).astype(BF16)
        return carry

    lax.fori_loop(0, tensor_count, frozen_block, 0)

    def rank_stage(g):
        for m, k in enumerate(groups[g]):
            if k:
                slot_copy(k).wait_recv()
            x = slot_in[k * length:(k + 1) * length, :block]
            c = slot_in[k * length:(k + 1) * length, block:]
            inner = nt_dot(x, down_ref[adapter_of[k]])
            back = nt_dot(c, up_ref[adapter_of[k]])
            ranks[t, (starts[g] + m) * length:(starts[g] + m + 1) * length, :] = jnp.concatenate(
                [inner, back], axis=1).astype(BF16)
        for q in range(1, tensor_count):
            rank_copy(g, q).start()

    def base_block(i, carry):
        q = lax.rem(tensor_count - i, tensor_count)
        acc[...] += nt_dot(cots[q], w_v[i])
        return carry

    def use_stage(g):
        for q in range(1, tensor_count):
            s = t_from(q)
            pltpu.make_async_remote_copy(
                ranks.at[s, rank_rows(g)], ranks.at[s, rank_rows(g)], rank_ssem.at[g, q], rank_rsem.at[g, q],
                device_id={"tensor": t_to(q)}, device_id_type=MESH).wait_recv()
        for q in range(1, tensor_count):
            rank_copy(g, q).wait_send()
        total = ranks[0, rank_rows(g)].astype(F32)
        for s in range(1, tensor_count):
            total = total + ranks[s, rank_rows(g)].astype(F32)
        for m, k in enumerate(groups[g]):
            lines = total[m * length:(m + 1) * length]
            inner = lines[:, :rank].astype(BF16)
            back = lines[:, rank:].astype(BF16)
            target = ret_out if k else ret_in
            target[k, :, :block] = (adapter_scale * jnp.dot(
                back, down_ref[adapter_of[k]], preferred_element_type=F32)).astype(BF16)
            target[k, :, block:] = (adapter_scale * jnp.dot(
                inner, up_ref[adapter_of[k]], preferred_element_type=F32)).astype(BF16)
            for a in range(resident):
                at = slice(k * length, (k + 1) * length)
                back_m[a, at, :] = (back.astype(F32) * weights[a][k]).astype(BF16)
                inner_m[a, at, :] = (inner.astype(F32) * weights[a][k]).astype(BF16)
            if k:
                ret_copy(k).start()

    for q in range(1, tensor_count):
        part_copy(q).start()
    half = max(1, tensor_count // 2)
    acc[...] = nt_dot(cot_ref[...], w_v[0])
    for q in range(1, tensor_count):
        cot_copy(q).wait_recv()
    lax.fori_loop(1, half, base_block, 0)
    down_copy.wait()
    up_copy.wait()
    rank_stage(0)
    lax.fori_loop(half, tensor_count, base_block, 0)
    use_stage(0)
    rank_stage(1)
    use_stage(1)
    rank_stage(2)
    use_stage(2)

    x_all = slot_in[:, :block]
    c_all = slot_in[:, block:]
    for a in range(resident):
        gd_ref[a] = tn_dot(back_m[a], x_all) * (
            adapter_scale / jnp.maximum(jnp.full((1, block), counts[a], F32), 1.0))
        gu_ref[a] = tn_dot(inner_m[a], c_all) * (
            adapter_scale / jnp.maximum(jnp.full((1, out_block), counts[a], F32), 1.0))

    gd_copy.start()
    gu_copy.start()
    for q in range(1, tensor_count):
        part_copy(q).wait_recv()
    backbone = parts[0].astype(F32)
    for q in range(1, tensor_count):
        backbone = backbone + part_in[q].astype(F32)
    for k in range(1, dp_count):
        ret_copy(k).wait_recv()
    for j in range(seqs):
        at = slice(j * length, (j + 1) * length)
        came = ret_in[table_ref[2 * dp_count + j]]
        kvo_ref[at, :] = (backbone[at] + came[:, block:].astype(F32)).astype(BF16)
        tg_ref[at, :] = (acc[at, :] + came[:, :block].astype(F32)).astype(BF16)

    for k in range(1, dp_count):
        slot_copy(k).wait_send()
        ret_copy(k).wait_send()
    for q in range(1, tensor_count):
        cot_copy(q).wait_send()
        part_copy(q).wait_send()
    gd_copy.wait()
    gu_copy.wait()


def mix(first, second, flag):
    return jnp.where(flag > 0, first, second)


def relay_fits(dp_count, seqs):
    return dp_count == 2 * seqs and seqs == 4


def relay_routes(dp_count, seqs, resident, seq_ref, store_ref, table_ref, weight_ref):
    d = lax.axis_index("dp")
    half = dp_count // 2
    xor = lax.bitwise_xor
    level = lax.div(d, jnp.int32(2))
    inner = lax.rem(lax.div(level + 1, jnp.int32(2)), jnp.int32(2))
    home = (2 - lax.div(d, jnp.int32(half))) * 2 + lax.rem(d, jnp.int32(2))
    zero, one = jnp.int32(0), jnp.int32(1)
    hub = xor(d, 2 - 2 * inner)
    worst = zero
    counts = [jnp.float32(0.0)] * resident
    for k in range(dp_count):
        p = xor(d, jnp.int32(k))
        crossing, found = zero, jnp.int32(-1)
        near = [zero] * half
        has, which = [zero] * half, [zero] * half
        apart = []
        for j in range(seqs):
            row = store_ref[seq_ref[p * seqs + j]]
            owner = lax.div(row, jnp.int32(resident))
            away = xor(owner, p)
            crossing = crossing + jnp.where(away >= half, one, zero)
            found = jnp.where(owner == d, row - d * resident, found)
            if k == 0:
                step = xor(owner, home)
                apart.append((away, step))
                for m in range(half):
                    near[m] = jnp.where(away == m, jnp.int32(j), near[m])
            if k in (0, half, half + 2):
                step = xor(owner, home if k == 0 else hub)
                for m in range(half):
                    hit = step == half - 1 - m
                    has[m] = jnp.where(hit, one, has[m])
                    which[m] = jnp.where(hit, jnp.int32(j), which[m])
        worst = jnp.maximum(worst, crossing)
        if k == 0:
            for m in range(half):
                table_ref[m] = near[m]
            table_ref[half] = jnp.where(has[0] > 0, which[0], which[1])
            table_ref[half + 1] = jnp.where((has[0] > 0) & (has[1] > 0), which[1], which[2])
            table_ref[half + 2] = jnp.where(has[3] > 0, which[3], which[2])
            place = [zero, jnp.where(has[0] > 0, one, zero), jnp.where(has[3] > 0, one, jnp.int32(2)), jnp.int32(2)]
            for j in range(seqs):
                away, step = apart[j]
                came = away
                for m in range(half):
                    came = jnp.where(step == half - 1 - m, half + place[m], came)
                table_ref[8 + j] = came
        if k in (half, half + 2):
            q = inner if k == half else 1 - inner
            table_ref[20 + 3 * q] = has[0]
            table_ref[21 + 3 * q] = has[0] * has[1]
            table_ref[22 + 3 * q] = has[3]
        s = jnp.int32(k) if k < half else xor(jnp.int32(k), 2 * inner)
        table_ref[12 + s] = jnp.maximum(found, 0)
        for a in range(resident):
            hit = jnp.where(found == a, jnp.float32(1.0), jnp.float32(0.0))
            weight_ref[a * dp_count + s] = hit
            counts[a] = counts[a] + hit
    for a in range(resident):
        weight_ref[resident * dp_count + a] = counts[a]
    table_ref[7] = jnp.where(worst < half, one, zero)


def relay_kernel(
    dp_count,
    tensor_count,
    table_ref,
    weight_ref,
    tok_ref,
    w_ref,
    down_hbm,
    up_hbm,
    cot_ref,
    cot_seq_ref,
    kvo_ref,
    tg_ref,
    gd_hbm,
    gu_hbm,
    down_ref,
    up_ref,
    gd_ref,
    gu_ref,
    w_v,
    near_out,
    cross_out,
    slot_in,
    relay_in,
    relay_out,
    ret_out,
    ret_in,
    relay_ret,
    back_out,
    cots,
    parts,
    part_in,
    ranks,
    back_m,
    inner_m,
    acc,
    w_sem,
    local_sem,
    near_ssem,
    near_rsem,
    slot_rsem,
    cross_ssem,
    relay_rsem,
    fwd_ssem,
    ret_ssem,
    ret_rsem,
    owner_rsem,
    back_ssem,
    cot_ssem,
    cot_rsem,
    part_ssem,
    part_rsem,
    rank_ssem,
    rank_rsem,
):
    d = lax.axis_index("dp")
    t = lax.axis_index("tensor")
    resident, rank, block = down_ref.shape
    out_block = up_ref.shape[2]
    seqs, length = tok_ref.shape[:2]
    rows = seqs * length
    bit = length // 2
    half = dp_count // 2
    level = lax.div(d, jnp.int32(2))
    inner = lax.rem(lax.div(level + 1, jnp.int32(2)), jnp.int32(2))
    outer = 1 - inner
    home = (2 - lax.div(d, jnp.int32(half))) * 2 + lax.rem(d, jnp.int32(2))
    peer = [partner(d, k, dp_count) for k in range(dp_count)]
    groups = [[0, 1, 2, 3], [4, 5], [6, 7]]
    starts = [0, 4, 6]
    close, far = 0, 1

    def t_to(q):
        return lax.rem(t + q, tensor_count)

    def t_from(q):
        return lax.rem(t + tensor_count - q, tensor_count)

    def lines(s):
        return slice(s * length, (s + 1) * length)

    def w_copy(i):
        c = t_to(i)
        return pltpu.make_async_copy(
            w_ref.at[:, pl.ds(pl.multiple_of(c * out_block, out_block), out_block)],
            w_v.at[i],
            w_sem.at[i],
        )

    def over(source, target, ssem, rsem, **where):
        return pltpu.make_async_remote_copy(
            source, target, ssem, rsem, device_id=where, device_id_type=MESH)

    def piece(h):
        return pl.ds(h * bit, bit)

    def slot_at(s, h):
        return slot_in.at[pl.ds(s * length + h * bit, bit)]

    def near_copy(k):
        return over(near_out.at[k - 1], slot_in.at[pl.ds(k * length, length)],
                    near_ssem.at[k], near_rsem.at[k], dp=peer[k])

    def cross_copy(i, h):
        return over(cross_out.at[i, piece(h)], relay_in.at[outer, i, piece(h)],
                    cross_ssem.at[i, h], relay_rsem.at[outer, i, h], dp=home)

    def cross_came(q, i, h):
        return over(cross_out.at[i, piece(h)], relay_in.at[q, i, piece(h)],
                    cross_ssem.at[i, h], relay_rsem.at[q, i, h], dp=home)

    def fwd_copy(q, m, h):
        source = relay_in.at[q, 0, piece(h)] if m == 0 else relay_out.at[q, m - 1, piece(h)]
        s = half + 2 * q + (0 if m == 1 else 1)
        return over(source, slot_at(s, h), fwd_ssem.at[q, m, h], slot_rsem.at[s - half, h], dp=peer[3 - m])

    def slot_came(s, h):
        return over(near_out.at[0, piece(h)], slot_at(s, h), near_ssem.at[0], slot_rsem.at[s - half, h], dp=peer[1])

    def ret_near(k):
        return over(ret_out.at[k], ret_in.at[k], ret_ssem.at[k, 0], ret_rsem.at[k, 0], dp=peer[k])

    def ret_same(q, h):
        s = half + 2 * q
        return over(ret_out.at[s, piece(h)], relay_ret.at[q, 1, piece(h)],
                    ret_ssem.at[s, h], owner_rsem.at[q, 1, h], dp=peer[2])

    def ret_other(q, h):
        s = half + 2 * q + 1
        return over(ret_out.at[s, piece(h)], relay_ret.at[q, 2, piece(h)],
                    ret_ssem.at[s, h], owner_rsem.at[q, 2, h], dp=peer[1])

    def ret_merged(q, h):
        return over(back_out.at[q, 0, piece(h)], relay_ret.at[q, 0, piece(h)],
                    back_ssem.at[q, 0, h], owner_rsem.at[q, 0, h], dp=peer[2])

    def owner_came(q, m, h):
        return over(ret_out.at[1, piece(h)], relay_ret.at[q, m, piece(h)],
                    ret_ssem.at[1, h], owner_rsem.at[q, m, h], dp=peer[1])

    def back_copy(q, i, h):
        source = relay_ret.at[q, 0, piece(h)] if i == 0 else back_out.at[q, i, piece(h)]
        return over(source, ret_in.at[half + i, piece(h)],
                    back_ssem.at[q, i, h], ret_rsem.at[half + i, h],
                    dp=peer[half + 2 - 2 * q])

    def back_came(i, h):
        return over(ret_out.at[1, piece(h)], ret_in.at[half + i, piece(h)],
                    ret_ssem.at[1, h], ret_rsem.at[half + i, h], dp=peer[1])

    def cot_copy(q):
        return over(cot_ref, cots.at[q], cot_ssem.at[q], cot_rsem.at[q], tensor=t_to(q))

    def part_copy(q):
        return over(parts.at[q], part_in.at[q], part_ssem.at[q], part_rsem.at[q], tensor=t_to(q))

    def rank_rows(g):
        return pl.ds(starts[g] * length, len(groups[g]) * length)

    def rank_copy(g, q):
        at = ranks.at[t, rank_rows(g)]
        return over(at, at, rank_ssem.at[g, q], rank_rsem.at[g, q], tensor=t_to(q))

    def rank_came(g, q):
        at = ranks.at[t_from(q), rank_rows(g)]
        return over(at, at, rank_ssem.at[g, q], rank_rsem.at[g, q], tensor=t_to(q))

    down_copy = pltpu.make_async_copy(down_hbm, down_ref, local_sem.at[0])
    up_copy = pltpu.make_async_copy(up_hbm, up_ref, local_sem.at[1])
    gd_copy = pltpu.make_async_copy(gd_ref, gd_hbm, local_sem.at[2])
    gu_copy = pltpu.make_async_copy(gu_ref, gu_hbm, local_sem.at[3])

    barrier = pltpu.get_barrier_semaphore()
    for k in range(1, half + 1):
        pl.semaphore_signal(barrier, inc=1, device_id={"dp": peer[k]}, device_id_type=MESH)

    @pl.when(inner == 1)
    def _():
        pl.semaphore_signal(barrier, inc=1, device_id={"dp": peer[half + 2]}, device_id_type=MESH)

    for q in range(1, tensor_count):
        pl.semaphore_signal(barrier, inc=1, device_id={"tensor": t_to(q)}, device_id_type=MESH)
    for i in range(tensor_count):
        w_copy(i).start()
    down_copy.start()
    up_copy.start()

    for i in range(half - 1):
        pick = table_ref[half + i]
        cross_out[i, :, :block] = tok_ref[pick]
        cross_out[i, :, block:] = cot_seq_ref[pick]
    for k in range(half):
        pick = table_ref[k]
        if k == 0:
            slot_in[:length, :block] = tok_ref[pick]
            slot_in[:length, block:] = cot_seq_ref[pick]
        else:
            near_out[k - 1, :, :block] = tok_ref[pick]
            near_out[k - 1, :, block:] = cot_seq_ref[pick]

    pl.semaphore_wait(barrier, half + inner + tensor_count - 1)

    for i in range(half - 1):
        for h in range(2):
            cross_copy(i, h).start()
    for k in (3, 2, 1):
        near_copy(k).start()
    for q in range(1, tensor_count):
        cot_copy(q).start()

    adapter_of = [table_ref[12 + s] for s in range(dp_count)]
    flags = [[table_ref[20 + 3 * q + i] for i in range(3)] for q in range(2)]
    weights = [[weight_ref[a * dp_count + s] for s in range(dp_count)] for a in range(resident)]
    counts = [weight_ref[resident * dp_count + a] for a in range(resident)]

    def relay(q, i):
        @pl.when(inner == 1)
        def _():
            for h in range(2):
                at = slice(h * bit, (h + 1) * bit)
                cross_came(q, i, h).wait_recv()
                if i == 1:
                    relay_out[q, 0, at] = mix(relay_in[q, 1, at], relay_in[q, 0, at], flags[q][0])
                if i == 2:
                    relay_out[q, 1, at] = mix(relay_in[q, 1, at], relay_in[q, 2, at], flags[q][2])
                fwd_copy(q, i, h).start()
            if i == 2:
                slot_in[lines(half + 2 * q), :] = relay_in[q, 2]

    def hand_back(q, i):
        @pl.when(inner == 1)
        def _():
            for h in range(2):
                at = slice(h * bit, (h + 1) * bit)
                if i == 0:
                    owner_came(q, 0, h).wait_recv()
                if i == 1:
                    owner_came(q, 1, h).wait_recv()
                    owner_came(q, 2, h).wait_recv()
                    back_out[q, 1, at] = mix(relay_ret[q, 1, at], relay_ret[q, 2, at], flags[q][1])
                if i == 2:
                    back_out[q, 2, at] = mix(ret_out[half + 2 * q, at], relay_ret[q, 2, at], flags[q][2])
                back_copy(q, i, h).start()

    def merge_out(q):
        @pl.when(inner == 0)
        def _():
            for h in range(2):
                at = slice(h * bit, (h + 1) * bit)
                owner_came(q, 2, h).wait_recv()
                back_out[q, 0, at] = mix(relay_ret[q, 2, at], ret_out[half + 2 * q, at], flags[q][0])
                ret_merged(q, h).start()

    def frozen_block(i, carry):
        w_copy(i).wait()
        parts[i] = jnp.dot(tok_ref[...].reshape(rows, block), w_v[i], preferred_element_type=F32).astype(BF16)
        return carry

    def base_block(i, carry):
        q = lax.rem(tensor_count - i, tensor_count)
        acc[...] += nt_dot(cots[q], w_v[i])
        return carry

    def rank_stage(g):
        for s in groups[g]:
            if s and s < half:
                near_copy(s).wait_recv()
            if s >= half and s % 2 == 1:
                for h in range(2):
                    slot_came(s, h).wait_recv()
            if s >= half and s % 2 == 0:
                @pl.when(inner == 0)
                def _():
                    for h in range(2):
                        slot_came(s, h).wait_recv()
        for s in groups[g]:
            x = slot_in[lines(s), :block]
            c = slot_in[lines(s), block:]
            inner_s = nt_dot(x, down_ref[adapter_of[s]])
            back_s = nt_dot(c, up_ref[adapter_of[s]])
            ranks[t, lines(s), :] = jnp.concatenate([inner_s, back_s], axis=1).astype(BF16)
        for q in range(1, tensor_count):
            rank_copy(g, q).start()

    def use_stage(g):
        for q in range(1, tensor_count):
            rank_came(g, q).wait_recv()
        for q in range(1, tensor_count):
            rank_copy(g, q).wait_send()
        total = ranks[0, rank_rows(g)].astype(F32)
        for s in range(1, tensor_count):
            total = total + ranks[s, rank_rows(g)].astype(F32)
        for m, s in enumerate(groups[g]):
            part = total[m * length:(m + 1) * length]
            mid = part[:, :rank].astype(BF16)
            back = part[:, rank:].astype(BF16)
            target = ret_out if s else ret_in
            target[s, :, :block] = (adapter_scale * jnp.dot(
                back, down_ref[adapter_of[s]], preferred_element_type=F32)).astype(BF16)
            target[s, :, block:] = (adapter_scale * jnp.dot(
                mid, up_ref[adapter_of[s]], preferred_element_type=F32)).astype(BF16)
            for a in range(resident):
                back_m[a, lines(s), :] = (back.astype(F32) * weights[a][s]).astype(BF16)
                inner_m[a, lines(s), :] = (mid.astype(F32) * weights[a][s]).astype(BF16)
        if g:
            q = g - 1
            for h in range(2):
                ret_other(q, h).start()

            @pl.when(inner == 0)
            def _():
                for h in range(2):
                    ret_same(q, h).start()

    middle = max(1, tensor_count // 2)
    lax.fori_loop(0, middle, frozen_block, 0)
    lax.fori_loop(middle, tensor_count, frozen_block, 0)
    for q in range(1, tensor_count):
        part_copy(q).start()
    acc[...] = nt_dot(cot_ref[...], w_v[0])
    relay(far, 0)
    for q in range(1, tensor_count):
        cot_copy(q).wait_recv()
    lax.fori_loop(1, middle, base_block, 0)
    down_copy.wait()
    up_copy.wait()
    relay(far, 1)
    lax.fori_loop(middle, tensor_count, base_block, 0)
    relay(far, 2)
    relay(close, 0)
    rank_stage(2)
    relay(close, 1)
    rank_stage(0)
    use_stage(2)
    relay(close, 2)
    use_stage(0)
    merge_out(far)
    hand_back(far, 0)
    hand_back(far, 1)
    hand_back(far, 2)
    rank_stage(1)
    use_stage(1)
    merge_out(close)
    for k in (3, 2, 1):
        ret_near(k).start()

    x_all = slot_in[:, :block]
    c_all = slot_in[:, block:]
    for a in range(resident):
        gd_ref[a] = tn_dot(back_m[a], x_all) * (
            adapter_scale / jnp.maximum(jnp.full((1, block), counts[a], F32), 1.0))
        gu_ref[a] = tn_dot(inner_m[a], c_all) * (
            adapter_scale / jnp.maximum(jnp.full((1, out_block), counts[a], F32), 1.0))
    gd_copy.start()
    gu_copy.start()
    for i in range(half - 1):
        hand_back(close, i)
    for q in range(1, tensor_count):
        part_copy(q).wait_recv()
    backbone = parts[0].astype(F32)
    for q in range(1, tensor_count):
        backbone = backbone + part_in[q].astype(F32)
    for k in range(1, half):
        ret_near(k).wait_recv()
    for i in range(half - 1):
        for h in range(2):
            back_came(i, h).wait_recv()
    for j in range(seqs):
        came = ret_in[table_ref[8 + j]]
        kvo_ref[lines(j), :] = (backbone[lines(j)] + came[:, block:].astype(F32)).astype(BF16)
        tg_ref[lines(j), :] = (acc[lines(j), :] + came[:, :block].astype(F32)).astype(BF16)

    for k in range(1, half):
        near_copy(k).wait_send()
        ret_near(k).wait_send()
    for h in range(2):
        for i in range(half - 1):
            cross_copy(i, h).wait_send()
        for q in range(2):
            ret_other(q, h).wait_send()

    @pl.when(inner == 0)
    def _():
        for q in range(2):
            for h in range(2):
                ret_same(q, h).wait_send()
                ret_merged(q, h).wait_send()

    @pl.when(inner == 1)
    def _():
        for q in range(2):
            for i in range(half - 1):
                for h in range(2):
                    fwd_copy(q, i, h).wait_send()
                    back_copy(q, i, h).wait_send()

    for q in range(1, tensor_count):
        cot_copy(q).wait_send()
        part_copy(q).wait_send()
    gd_copy.wait()
    gu_copy.wait()


def finish(pieces, *refs):
    n = len(pieces)
    given, out, sem = refs[:n], refs[n:2 * n], refs[2 * n]
    steps = [(i, p) for i in range(n) for p in range(pieces[i])]

    def move(at, i, p):
        span = given[i].shape[0] // pieces[i]
        rows = pl.ds(p * span, span)
        return pltpu.make_async_copy(given[i].at[rows], out[i].at[rows], sem.at[at])

    for at, (i, p) in enumerate(steps):
        move(at, i, p).start()
    for at, (i, p) in enumerate(steps):
        move(at, i, p).wait()


def shapes_of(rows, block, out_block, resident, rank):
    return (
        jax.ShapeDtypeStruct((rows, out_block), BF16),
        jax.ShapeDtypeStruct((rows, block), BF16),
        jax.ShapeDtypeStruct((resident, rank, block), F32),
        jax.ShapeDtypeStruct((resident, rank, out_block), F32),
    )


def direct(dp_count, tensor_count, tok, w, down, up, cot, seq_index, storage):
    resident, rank, block = down.shape
    out_block = up.shape[2]
    rows = tok.shape[0]
    seqs = seq_index.shape[0] // dp_count
    length = rows // seqs
    groups = len(slot_groups(dp_count))
    anywhere = pl.BlockSpec(memory_space=pl.ANY)
    wide = block + out_block
    vmem = pl.BlockSpec(memory_space=pltpu.VMEM)
    smem = pl.BlockSpec(memory_space=pltpu.SMEM)
    dma = pltpu.SemaphoreType.DMA
    table, weights = pl.pallas_call(
        functools.partial(routes, dp_count, seqs, resident),
        out_shape=(
            jax.ShapeDtypeStruct((2 * dp_count + seqs,), jnp.int32),
            jax.ShapeDtypeStruct((resident * dp_count + resident,), F32),
        ),
        in_specs=[smem, smem],
        out_specs=(smem, smem),
    )(seq_index, storage)
    return pl.pallas_call(
        functools.partial(kernel, dp_count, tensor_count),
        out_shape=shapes_of(rows, block, out_block, resident, rank),
        in_specs=[smem, smem, vmem, anywhere, anywhere, anywhere, vmem, vmem],
        out_specs=(vmem, vmem, anywhere, anywhere),
        scratch_shapes=[
            pltpu.VMEM(down.shape, BF16),
            pltpu.VMEM(up.shape, BF16),
            pltpu.VMEM(down.shape, F32),
            pltpu.VMEM(up.shape, F32),
            pltpu.VMEM((tensor_count, w.shape[0], out_block), BF16),
            pltpu.VMEM((dp_count * length, wide), BF16),
            pltpu.VMEM((dp_count * length, wide), BF16),
            pltpu.VMEM((dp_count, length, wide), BF16),
            pltpu.VMEM((dp_count, length, wide), BF16),
            pltpu.VMEM((tensor_count, rows, out_block), BF16),
            pltpu.VMEM((tensor_count, rows, out_block), BF16),
            pltpu.VMEM((tensor_count, rows, out_block), BF16),
            pltpu.VMEM((tensor_count, dp_count * length, 2 * rank), BF16),
            pltpu.VMEM((resident, dp_count * length, rank), BF16),
            pltpu.VMEM((resident, dp_count * length, rank), BF16),
            pltpu.VMEM((rows, block), F32),
            dma((tensor_count,)),
            dma((4,)),
            dma((dp_count,)),
            dma((dp_count,)),
            dma((dp_count,)),
            dma((dp_count,)),
            dma((tensor_count,)),
            dma((tensor_count,)),
            dma((tensor_count,)),
            dma((tensor_count,)),
            dma((groups, tensor_count)),
            dma((groups, tensor_count)),
        ],
        compiler_params=pltpu.CompilerParams(
            collective_id=1, has_side_effects=True, vmem_limit_bytes=60 * 1024 * 1024
        ),
    )(
        table, weights, tok.reshape(seqs, length, block), w, down, up, cot,
        cot.reshape(seqs, length, out_block))


def relayed(dp_count, tensor_count, table, weights, tok, w, down, up, cot, seqs):
    resident, rank, block = down.shape
    out_block = up.shape[2]
    rows = tok.shape[0]
    length = rows // seqs
    half = dp_count // 2
    anywhere = pl.BlockSpec(memory_space=pl.ANY)
    wide = block + out_block
    vmem = pl.BlockSpec(memory_space=pltpu.VMEM)
    smem = pl.BlockSpec(memory_space=pltpu.SMEM)
    dma = pltpu.SemaphoreType.DMA

    def slots(*lead):
        return pltpu.VMEM(lead + (length, wide), BF16)

    return pl.pallas_call(
        functools.partial(relay_kernel, dp_count, tensor_count),
        out_shape=shapes_of(rows, block, out_block, resident, rank),
        in_specs=[smem, smem, vmem, anywhere, anywhere, anywhere, vmem, vmem],
        out_specs=(vmem, vmem, anywhere, anywhere),
        scratch_shapes=[
            pltpu.VMEM(down.shape, BF16),
            pltpu.VMEM(up.shape, BF16),
            pltpu.VMEM(down.shape, F32),
            pltpu.VMEM(up.shape, F32),
            pltpu.VMEM((tensor_count, w.shape[0], out_block), BF16),
            slots(half - 1),
            slots(half - 1),
            pltpu.VMEM((dp_count * length, wide), BF16),
            slots(2, half - 1),
            slots(2, half - 2),
            slots(dp_count),
            slots(dp_count - 1),
            slots(2, half - 1),
            slots(2, half - 1),
            pltpu.VMEM((tensor_count, rows, out_block), BF16),
            pltpu.VMEM((tensor_count, rows, out_block), BF16),
            pltpu.VMEM((tensor_count, rows, out_block), BF16),
            pltpu.VMEM((tensor_count, dp_count * length, 2 * rank), BF16),
            pltpu.VMEM((resident, dp_count * length, rank), BF16),
            pltpu.VMEM((resident, dp_count * length, rank), BF16),
            pltpu.VMEM((rows, block), F32),
            dma((tensor_count,)),
            dma((4,)),
            dma((half,)),
            dma((half,)),
            dma((half, 2)),
            dma((half - 1, 2)),
            dma((2, half - 1, 2)),
            dma((2, half - 1, 2)),
            dma((dp_count, 2)),
            dma((dp_count - 1, 2)),
            dma((2, half - 1, 2)),
            dma((2, half - 1, 2)),
            dma((tensor_count,)),
            dma((tensor_count,)),
            dma((tensor_count,)),
            dma((tensor_count,)),
            dma((3, tensor_count)),
            dma((3, tensor_count)),
        ],
        compiler_params=pltpu.CompilerParams(
            collective_id=0, has_side_effects=True, vmem_limit_bytes=60 * 1024 * 1024
        ),
    )(
        table, weights, tok.reshape(seqs, length, block), w, down, up, cot,
        cot.reshape(seqs, length, out_block))


def on_device(dp_count, tensor_count, tok, w, down, up, cot, seq_index, storage):
    resident = down.shape[0]
    seqs = seq_index.shape[0] // dp_count
    anywhere = pl.BlockSpec(memory_space=pl.ANY)
    vmem = pl.BlockSpec(memory_space=pltpu.VMEM)
    smem = pl.BlockSpec(memory_space=pltpu.SMEM)
    dma = pltpu.SemaphoreType.DMA
    args = (tok, w, down, up, cot)
    if relay_fits(dp_count, seqs):
        table, weights = pl.pallas_call(
            functools.partial(relay_routes, dp_count, seqs, resident),
            out_shape=(
                jax.ShapeDtypeStruct((32,), jnp.int32),
                jax.ShapeDtypeStruct((resident * dp_count + resident,), F32),
            ),
            in_specs=[smem, smem],
            out_specs=(smem, smem),
        )(seq_index, storage)
        results = lax.cond(
            table[7] > 0,
            lambda: relayed(dp_count, tensor_count, table, weights, *args, seqs),
            lambda: direct(dp_count, tensor_count, *args, seq_index, storage),
        )
    else:
        results = direct(dp_count, tensor_count, *args, seq_index, storage)
    pieces = (1, 2, resident, 1)
    return pl.pallas_call(
        functools.partial(finish, pieces),
        out_shape=tuple(jax.ShapeDtypeStruct(r.shape, r.dtype) for r in results),
        in_specs=[vmem] * 4,
        out_specs=(anywhere,) * 4,
        scratch_shapes=[dma((sum(pieces),))],
    )(*results)


def solution(mesh):
    in_specs = (
        P("dp", "tensor"),
        P("tensor", None),
        P("dp", None, "tensor"),
        P("dp", None, "tensor"),
        P("dp", "tensor"),
        P(),
        P(),
    )
    out_specs = (
        P("dp", "tensor"),
        P("dp", "tensor"),
        P("dp", None, "tensor"),
        P("dp", None, "tensor"),
    )
    return jax.shard_map(
        functools.partial(on_device, mesh.shape["dp"], mesh.shape["tensor"]),
        mesh=mesh, in_specs=in_specs, out_specs=out_specs, check_vma=False,
    )
```

```python
import functools

import jax
import jax.numpy as jnp
from jax import lax
from jax.experimental import pallas as pl
from jax.experimental.pallas import tpu as pltpu
from jax.sharding import PartitionSpec as P

adapter_scale = 0.25
MESH = pl.DeviceIdType.MESH
F32 = jnp.float32
BF16 = jnp.bfloat16


def nt_dot(a, b):
    return lax.dot_general(a, b, (((1,), (1,)), ((), ())), preferred_element_type=F32)


def tn_dot(a, b):
    return lax.dot_general(a, b, (((0,), (0,)), ((), ())), preferred_element_type=F32)


def partner(d, k, dp_count):
    out, bit = d, 1
    while bit < dp_count:
        if k & bit:
            out = out + bit - 2 * bit * lax.rem(lax.div(d, jnp.int32(bit)), jnp.int32(2))
        bit *= 2
    return out


def routes(dp_count, seqs, resident, seq_ref, store_ref, table_ref, weight_ref):
    d = lax.axis_index("dp")
    rows = [store_ref[seq_ref[d * seqs + j]] for j in range(seqs)]
    owners = [lax.div(r, jnp.int32(resident)) for r in rows]
    dist = []
    for j in range(seqs):
        slot = jnp.int32(0)
        for k in range(1, dp_count):
            slot = jnp.where(owners[j] == partner(d, k, dp_count), jnp.int32(k), slot)
        dist.append(slot)
    for j in range(seqs):
        table_ref[2 * dp_count + j] = dist[j]
    for k in range(dp_count):
        pick = jnp.int32(0)
        for j in range(seqs):
            pick = jnp.where(dist[j] == k, jnp.int32(j), pick)
        table_ref[k] = pick
    counts = [jnp.float32(0.0)] * resident
    for k in range(dp_count):
        reader = partner(d, k, dp_count)
        found = jnp.int32(-1)
        for j in range(seqs):
            local = store_ref[seq_ref[reader * seqs + j]] - d * resident
            found = jnp.where((local >= 0) & (local < resident), local, found)
        table_ref[dp_count + k] = jnp.maximum(found, 0)
        for a in range(resident):
            hit = jnp.where(found == a, jnp.float32(1.0), jnp.float32(0.0))
            weight_ref[a * dp_count + k] = hit
            counts[a] = counts[a] + hit
    for a in range(resident):
        weight_ref[resident * dp_count + a] = counts[a]


def slot_groups(dp_count):
    order = list(range(dp_count - 1, -1, -1))
    quarter = dp_count // 4
    return [order[:quarter], order[quarter:2 * quarter], order[2 * quarter:]]


def kernel(
    dp_count,
    tensor_count,
    table_ref,
    weight_ref,
    tok_ref,
    w_ref,
    down_hbm,
    up_hbm,
    cot_ref,
    cot_seq_ref,
    kvo_ref,
    tg_ref,
    gd_hbm,
    gu_hbm,
    down_ref,
    up_ref,
    gd_ref,
    gu_ref,
    w_v,
    slot_out,
    slot_in,
    ret_out,
    ret_in,
    cots,
    parts,
    part_in,
    ranks,
    back_m,
    inner_m,
    acc,
    w_sem,
    local_sem,
    slot_ssem,
    slot_rsem,
    ret_ssem,
    ret_rsem,
    cot_ssem,
    cot_rsem,
    part_ssem,
    part_rsem,
    rank_ssem,
    rank_rsem,
):
    d = lax.axis_index("dp")
    t = lax.axis_index("tensor")
    resident, rank, block = down_ref.shape
    out_block = up_ref.shape[2]
    seqs, length = tok_ref.shape[:2]
    rows = seqs * length
    groups = slot_groups(dp_count)
    starts = [sum(len(g) for g in groups[:i]) for i in range(len(groups))]

    def dp_to(k):
        return partner(d, k, dp_count)

    def t_to(q):
        return lax.rem(t + q, tensor_count)

    def t_from(q):
        return lax.rem(t + tensor_count - q, tensor_count)

    def w_copy(i):
        c = t_to(i)
        return pltpu.make_async_copy(
            w_ref.at[:, pl.ds(pl.multiple_of(c * out_block, out_block), out_block)],
            w_v.at[i],
            w_sem.at[i],
        )

    down_copy = pltpu.make_async_copy(down_hbm, down_ref, local_sem.at[0])
    up_copy = pltpu.make_async_copy(up_hbm, up_ref, local_sem.at[1])
    gd_copy = pltpu.make_async_copy(gd_ref, gd_hbm, local_sem.at[2])
    gu_copy = pltpu.make_async_copy(gu_ref, gu_hbm, local_sem.at[3])
    for i in range(tensor_count):
        w_copy(i).start()
    down_copy.start()
    up_copy.start()

    barrier = pltpu.get_barrier_semaphore()
    for k in range(1, dp_count):
        pl.semaphore_signal(barrier, inc=1, device_id={"dp": dp_to(k)}, device_id_type=MESH)
    for q in range(1, tensor_count):
        pl.semaphore_signal(barrier, inc=1, device_id={"tensor": t_to(q)}, device_id_type=MESH)

    for k in range(dp_count):
        pick = table_ref[k]
        target = slot_in if k == 0 else slot_out
        target[k * length:(k + 1) * length, :block] = tok_ref[pick]
        target[k * length:(k + 1) * length, block:] = cot_seq_ref[pick]

    pl.semaphore_wait(barrier, dp_count + tensor_count - 2)

    def cot_copy(q):
        return pltpu.make_async_remote_copy(
            cot_ref, cots.at[q], cot_ssem.at[q], cot_rsem.at[q],
            device_id={"tensor": t_to(q)}, device_id_type=MESH)

    def slot_copy(k):
        at = pl.ds(k * length, length)
        return pltpu.make_async_remote_copy(
            slot_out.at[at], slot_in.at[at], slot_ssem.at[k], slot_rsem.at[k],
            device_id={"dp": dp_to(k)}, device_id_type=MESH)

    def ret_copy(k):
        return pltpu.make_async_remote_copy(
            ret_out.at[k], ret_in.at[k], ret_ssem.at[k], ret_rsem.at[k],
            device_id={"dp": dp_to(k)}, device_id_type=MESH)

    def part_copy(q):
        return pltpu.make_async_remote_copy(
            parts.at[q], part_in.at[q], part_ssem.at[q], part_rsem.at[q],
            device_id={"tensor": t_to(q)}, device_id_type=MESH)

    def rank_rows(g):
        return pl.ds(starts[g] * length, len(groups[g]) * length)

    def rank_copy(g, q):
        return pltpu.make_async_remote_copy(
            ranks.at[t, rank_rows(g)], ranks.at[t, rank_rows(g)], rank_ssem.at[g, q], rank_rsem.at[g, q],
            device_id={"tensor": t_to(q)}, device_id_type=MESH)

    for k in range(dp_count - 1, 0, -1):
        slot_copy(k).start()
    for q in range(1, tensor_count):
        cot_copy(q).start()

    adapter_of = [table_ref[dp_count + k] for k in range(dp_count)]
    weights = [[weight_ref[a * dp_count + k] for k in range(dp_count)] for a in range(resident)]
    counts = [weight_ref[resident * dp_count + a] for a in range(resident)]

    def frozen_block(i, carry):
        w_copy(i).wait()
        parts[i] = jnp.dot(tok_ref[...].reshape(rows, block), w_v[i], preferred_element_type=F32).astype(BF16)
        return carry

    lax.fori_loop(0, tensor_count, frozen_block, 0)

    def rank_stage(g):
        for m, k in enumerate(groups[g]):
            if k:
                slot_copy(k).wait_recv()
            x = slot_in[k * length:(k + 1) * length, :block]
            c = slot_in[k * length:(k + 1) * length, block:]
            inner = nt_dot(x, down_ref[adapter_of[k]])
            back = nt_dot(c, up_ref[adapter_of[k]])
            ranks[t, (starts[g] + m) * length:(starts[g] + m + 1) * length, :] = jnp.concatenate(
                [inner, back], axis=1).astype(BF16)
        for q in range(1, tensor_count):
            rank_copy(g, q).start()

    def base_block(i, carry):
        q = lax.rem(tensor_count - i, tensor_count)
        acc[...] += nt_dot(cots[q], w_v[i])
        return carry

    def use_stage(g):
        for q in range(1, tensor_count):
            s = t_from(q)
            pltpu.make_async_remote_copy(
                ranks.at[s, rank_rows(g)], ranks.at[s, rank_rows(g)], rank_ssem.at[g, q], rank_rsem.at[g, q],
                device_id={"tensor": t_to(q)}, device_id_type=MESH).wait_recv()
        for q in range(1, tensor_count):
            rank_copy(g, q).wait_send()
        total = ranks[0, rank_rows(g)].astype(F32)
        for s in range(1, tensor_count):
            total = total + ranks[s, rank_rows(g)].astype(F32)
        for m, k in enumerate(groups[g]):
            lines = total[m * length:(m + 1) * length]
            inner = lines[:, :rank].astype(BF16)
            back = lines[:, rank:].astype(BF16)
            target = ret_out if k else ret_in
            target[k, :, :block] = (adapter_scale * jnp.dot(
                back, down_ref[adapter_of[k]], preferred_element_type=F32)).astype(BF16)
            target[k, :, block:] = (adapter_scale * jnp.dot(
                inner, up_ref[adapter_of[k]], preferred_element_type=F32)).astype(BF16)
            for a in range(resident):
                at = slice(k * length, (k + 1) * length)
                back_m[a, at, :] = (back.astype(F32) * weights[a][k]).astype(BF16)
                inner_m[a, at, :] = (inner.astype(F32) * weights[a][k]).astype(BF16)
            if k:
                ret_copy(k).start()

    for q in range(1, tensor_count):
        part_copy(q).start()
    half = max(1, tensor_count // 2)
    acc[...] = nt_dot(cot_ref[...], w_v[0])
    for q in range(1, tensor_count):
        cot_copy(q).wait_recv()
    lax.fori_loop(1, half, base_block, 0)
    down_copy.wait()
    up_copy.wait()
    rank_stage(0)
    lax.fori_loop(half, tensor_count, base_block, 0)
    use_stage(0)
    rank_stage(1)
    use_stage(1)
    rank_stage(2)
    use_stage(2)

    x_all = slot_in[:, :block]
    c_all = slot_in[:, block:]
    for a in range(resident):
        gd_ref[a] = tn_dot(back_m[a], x_all) * (
            adapter_scale / jnp.maximum(jnp.full((1, block), counts[a], F32), 1.0))
        gu_ref[a] = tn_dot(inner_m[a], c_all) * (
            adapter_scale / jnp.maximum(jnp.full((1, out_block), counts[a], F32), 1.0))

    gd_copy.start()
    gu_copy.start()
    for q in range(1, tensor_count):
        part_copy(q).wait_recv()
    backbone = parts[0].astype(F32)
    for q in range(1, tensor_count):
        backbone = backbone + part_in[q].astype(F32)
    for k in range(1, dp_count):
        ret_copy(k).wait_recv()
    for j in range(seqs):
        at = slice(j * length, (j + 1) * length)
        came = ret_in[table_ref[2 * dp_count + j]]
        kvo_ref[at, :] = (backbone[at] + came[:, block:].astype(F32)).astype(BF16)
        tg_ref[at, :] = (acc[at, :] + came[:, :block].astype(F32)).astype(BF16)

    for k in range(1, dp_count):
        slot_copy(k).wait_send()
        ret_copy(k).wait_send()
    for q in range(1, tensor_count):
        cot_copy(q).wait_send()
        part_copy(q).wait_send()
    gd_copy.wait()
    gu_copy.wait()


def mix(first, second, flag):
    return jnp.where(flag > 0, first, second)


def relay_fits(dp_count, seqs):
    return dp_count == 2 * seqs and seqs == 4


def relay_routes(dp_count, seqs, resident, seq_ref, store_ref, table_ref, weight_ref, fits_ref):
    d = lax.axis_index("dp")
    half = dp_count // 2
    xor = lax.bitwise_xor
    level = lax.div(d, jnp.int32(2))
    inner = lax.rem(lax.div(level + 1, jnp.int32(2)), jnp.int32(2))
    home = (2 - lax.div(d, jnp.int32(half))) * 2 + lax.rem(d, jnp.int32(2))
    zero, one = jnp.int32(0), jnp.int32(1)
    hub = xor(d, 2 - 2 * inner)
    worst = zero
    counts = [jnp.float32(0.0)] * resident
    for k in range(dp_count):
        p = xor(d, jnp.int32(k))
        crossing, found = zero, jnp.int32(-1)
        near = [zero] * half
        has, which = [zero] * half, [zero] * half
        apart = []
        for j in range(seqs):
            row = store_ref[seq_ref[p * seqs + j]]
            owner = lax.div(row, jnp.int32(resident))
            away = xor(owner, p)
            crossing = crossing + jnp.where(away >= half, one, zero)
            found = jnp.where(owner == d, row - d * resident, found)
            if k == 0:
                step = xor(owner, home)
                apart.append((away, step))
                for m in range(half):
                    near[m] = jnp.where(away == m, jnp.int32(j), near[m])
            if k in (0, half, half + 2):
                step = xor(owner, home if k == 0 else hub)
                for m in range(half):
                    hit = step == half - 1 - m
                    has[m] = jnp.where(hit, one, has[m])
                    which[m] = jnp.where(hit, jnp.int32(j), which[m])
        worst = jnp.maximum(worst, crossing)
        if k == 0:
            for m in range(half):
                table_ref[m] = near[m]
            table_ref[half] = jnp.where(has[0] > 0, which[0], which[1])
            table_ref[half + 1] = jnp.where((has[0] > 0) & (has[1] > 0), which[1], which[2])
            table_ref[half + 2] = jnp.where(has[3] > 0, which[3], which[2])
            place = [zero, jnp.where(has[0] > 0, one, zero), jnp.where(has[3] > 0, one, jnp.int32(2)), jnp.int32(2)]
            for j in range(seqs):
                away, step = apart[j]
                came = away
                for m in range(half):
                    came = jnp.where(step == half - 1 - m, half + place[m], came)
                table_ref[8 + j] = came
        if k in (half, half + 2):
            q = inner if k == half else 1 - inner
            table_ref[20 + 3 * q] = has[0]
            table_ref[21 + 3 * q] = has[0] * has[1]
            table_ref[22 + 3 * q] = has[3]
        s = jnp.int32(k) if k < half else xor(jnp.int32(k), 2 * inner)
        table_ref[12 + s] = jnp.maximum(found, 0)
        for a in range(resident):
            hit = jnp.where(found == a, jnp.float32(1.0), jnp.float32(0.0))
            weight_ref[a * dp_count + s] = hit
            counts[a] = counts[a] + hit
    for a in range(resident):
        weight_ref[resident * dp_count + a] = counts[a]
    fits_ref[0] = jnp.where(worst < half, one, zero)


def relay_kernel(
    dp_count,
    tensor_count,
    table_ref,
    weight_ref,
    tok_hbm,
    w_ref,
    down_hbm,
    up_hbm,
    cot_hbm,
    kvo_ref,
    tg_ref,
    gd_hbm,
    gu_hbm,
    down_ref,
    up_ref,
    gd_ref,
    gu_ref,
    tok_ref,
    cot_ref,
    w_v,
    near_out,
    cross_out,
    stage_in,
    slot_in,
    relay_out,
    bulk,
    ret_in,
    cots,
    parts,
    part_in,
    ranks,
    ranks_in,
    back_m,
    inner_m,
    acc,
    w_sem,
    local_sem,
    send_sem,
    near_rsem,
    slot_rsem,
    relay_rsem,
    stage_rsem,
    owner_rsem,
    ret_rsem,
    cot_ssem,
    cot_rsem,
    part_ssem,
    part_rsem,
    rank_ssem,
    rank_rsem,
):
    d = lax.axis_index("dp")
    t = lax.axis_index("tensor")
    resident, rank, block = down_ref.shape
    out_block = up_ref.shape[2]
    seqs, length = tok_ref.shape[:2]
    rows = seqs * length
    bit = length // 2
    half = dp_count // 2
    level = lax.div(d, jnp.int32(2))
    inner = lax.rem(lax.div(level + 1, jnp.int32(2)), jnp.int32(2))
    outer = 1 - inner
    peer = [partner(d, k, dp_count) for k in range(dp_count)]
    groups = [[0, 1, 2, 3], [4, 5], [6, 7]]
    starts = [0, 4, 6]
    close, far = 0, 1

    ret_out = bulk.at[pl.ds(0, dp_count)]
    relay_ret, back_out, relay_in = (
        bulk.at[pl.ds(dp_count + 2 * (half - 1) * n, 2 * (half - 1))] for n in range(3))

    def t_to(q):
        return lax.rem(t + q, tensor_count)

    def t_from(q):
        return lax.rem(t + tensor_count - q, tensor_count)

    def lines(s):
        return slice(s * length, (s + 1) * length)

    def w_copy(i):
        c = t_to(i)
        return pltpu.make_async_copy(
            w_ref.at[:, pl.ds(pl.multiple_of(c * out_block, out_block), out_block)],
            w_v.at[i],
            w_sem.at[i],
        )

    def over(source, target, ssem, rsem, **where):
        return pltpu.make_async_remote_copy(
            source, target, ssem, rsem, device_id=where, device_id_type=MESH)

    def piece(h):
        return pl.ds(h * bit, bit)

    def slot_at(s, h):
        return slot_in.at[pl.ds(s * length + h * bit, bit)]

    def near_copy(k):
        return over(near_out.at[k - 1], slot_in.at[pl.ds(k * length, length)], send_sem, near_rsem, dp=peer[k])

    def near_came():
        at = slot_in.at[pl.ds(length, (half - 1) * length)]
        return over(at, at, send_sem, near_rsem, dp=peer[1])

    def cross_copy(i, h):
        return over(cross_out.at[i, piece(h)], relay_in.at[i, piece(h)],
                    send_sem, relay_rsem.at[close, i, h], dp=peer[half + 2])

    def stage_copy(i, h):
        return over(cross_out.at[i, piece(h)], stage_in.at[i, piece(h)], send_sem, stage_rsem.at[i, h], dp=peer[2])

    def onward_copy(i, h):
        return over(stage_in.at[i, piece(h)], relay_in.at[half - 1 + i, piece(h)],
                    send_sem, relay_rsem.at[far, i, h], dp=peer[half + 2])

    def cross_came(q, i, h):
        at = relay_in.at[(half - 1) * q + i, piece(h)]
        return over(at, at, send_sem, relay_rsem.at[q, i, h], dp=peer[half + 2])

    def fwd_copy(q, m, h):
        s = half + 2 * q + (0 if m == 1 else 1)
        source = relay_out.at[q, m - 1, piece(h)] if m else relay_in.at[(half - 1) * q, piece(h)]
        return over(source, slot_at(s, h), send_sem, slot_rsem.at[s - half], dp=peer[3 - m])

    def slot_came(s):
        at = slot_in.at[pl.ds(s * length, length)]
        return over(at, at, send_sem, slot_rsem.at[s - half], dp=peer[1])

    def ret_near(k):
        return over(ret_out.at[k], ret_in.at[k], send_sem, ret_rsem, dp=peer[k])

    def ret_same(q, h):
        return over(ret_out.at[half + 2 * q, piece(h)], relay_ret.at[(half - 1) * q + 1, piece(h)],
                    send_sem, owner_rsem.at[q, 1, h], dp=peer[2])

    def ret_other(q, h):
        return over(ret_out.at[half + 2 * q + 1, piece(h)], relay_ret.at[(half - 1) * q + 2, piece(h)],
                    send_sem, owner_rsem.at[q, 2, h], dp=peer[1])

    def ret_merged(q, h):
        return over(back_out.at[(half - 1) * q, piece(h)], relay_ret.at[(half - 1) * q, piece(h)],
                    send_sem, owner_rsem.at[q, 0, h], dp=peer[2])

    def owner_came(q, m, h):
        at = relay_ret.at[(half - 1) * q + m, piece(h)]
        return over(at, at, send_sem, owner_rsem.at[q, m, h], dp=peer[1])

    def back_copy(q, i, h):
        source = (back_out if i else relay_ret).at[(half - 1) * q + i, piece(h)]
        return over(source, ret_in.at[half + i, piece(h)], send_sem, ret_rsem, dp=peer[half + 2 - 2 * q])

    def rets_came():
        at = ret_in.at[pl.ds(1, 2 * half - 2)]
        return over(at, at, send_sem, ret_rsem, dp=peer[1])

    def sent(count):
        return over(bulk.at[pl.ds(0, count)], bulk.at[pl.ds(0, count)], send_sem, ret_rsem, dp=peer[1])

    def cot_copy(q):
        return over(cot_ref, cots.at[q], cot_ssem, cot_rsem, tensor=t_to(q))

    def cots_came():
        at = cots.at[pl.ds(1, tensor_count - 1)]
        return over(at, at, cot_ssem, cot_rsem, tensor=t_to(1))

    def part_copy(q):
        return over(parts.at[q], part_in.at[q], part_ssem, part_rsem, tensor=t_to(q))

    def parts_came():
        at = part_in.at[pl.ds(1, tensor_count - 1)]
        return over(at, at, part_ssem, part_rsem, tensor=t_to(1))

    def rank_rows(g):
        return pl.ds(starts[g] * length, len(groups[g]) * length)

    def rank_copy(g, q):
        return over(ranks.at[rank_rows(g)], ranks_in.at[q - 1, rank_rows(g)], rank_ssem, rank_rsem.at[g], tensor=t_to(q))

    def ranks_came(g):
        at = ranks_in.at[:, rank_rows(g)]
        return over(at, at, rank_ssem, rank_rsem.at[g], tensor=t_to(1))

    def ranks_sent():
        return over(ranks_in, ranks_in, rank_ssem, rank_rsem.at[0], tensor=t_to(1))

    down_copy = pltpu.make_async_copy(down_hbm, down_ref, local_sem.at[0])
    up_copy = pltpu.make_async_copy(up_hbm, up_ref, local_sem.at[1])
    gd_copy = pltpu.make_async_copy(gd_ref, gd_hbm, local_sem.at[2])
    gu_copy = pltpu.make_async_copy(gu_ref, gu_hbm, local_sem.at[3])

    tok_copy = pltpu.make_async_copy(tok_hbm, tok_ref, local_sem.at[4])
    seed_copy = pltpu.make_async_copy(cot_hbm, cot_ref, local_sem.at[5])
    tok_copy.start()
    seed_copy.start()

    barrier = pltpu.get_barrier_semaphore()
    for k in range(1, half + 1):
        pl.semaphore_signal(barrier, inc=1, device_id={"dp": peer[k]}, device_id_type=MESH)

    @pl.when(inner == 1)
    def _():
        pl.semaphore_signal(barrier, inc=1, device_id={"dp": peer[half + 2]}, device_id_type=MESH)

    for q in range(1, tensor_count):
        pl.semaphore_signal(barrier, inc=1, device_id={"tensor": t_to(q)}, device_id_type=MESH)
    for i in range(tensor_count):
        w_copy(i).start()
    down_copy.start()
    up_copy.start()
    tok_copy.wait()
    seed_copy.wait()

    for i in range(half - 1):
        pick = table_ref[half + i]
        cross_out[i, :, :block] = tok_ref[pick]
        cross_out[i, :, block:] = cot_ref[pick]
    for k in range(half):
        pick = table_ref[k]
        if k == 0:
            slot_in[:length, :block] = tok_ref[pick]
            slot_in[:length, block:] = cot_ref[pick]
        else:
            near_out[k - 1, :, :block] = tok_ref[pick]
            near_out[k - 1, :, block:] = cot_ref[pick]

    pl.semaphore_wait(barrier, half + inner + tensor_count - 1)

    @pl.when(inner == 1)
    def _():
        for i in range(half - 1):
            for h in range(2):
                cross_copy(i, h).start()

    @pl.when(inner == 0)
    def _():
        near_copy(3).start()
        for i in range(half - 1):
            for h in range(2):
                stage_copy(i, h).start()

    near_copy(1).start()
    near_copy(2).start()

    for q in range(1, tensor_count):
        cot_copy(q).start()

    adapter_of = [table_ref[12 + s] for s in range(dp_count)]
    flags = [[table_ref[20 + 3 * q + i] for i in range(3)] for q in range(2)]
    weights = [[weight_ref[a * dp_count + s] for s in range(dp_count)] for a in range(resident)]
    counts = [weight_ref[resident * dp_count + a] for a in range(resident)]

    def onward(i):
        @pl.when(inner == 1)
        def _():
            for h in range(2):
                stage_copy(i, h).wait_recv()
                onward_copy(i, h).start()

    def relay(q, i):
        base = (half - 1) * q

        @pl.when(inner == 1)
        def _():
            for h in range(2):
                at = slice(h * bit, (h + 1) * bit)
                cross_came(q, i, h).wait_recv()
                if i == 1:
                    relay_out[q, 0, at] = mix(relay_in[base + 1, at], relay_in[base, at], flags[q][0])
                if i == 2:
                    relay_out[q, 1, at] = mix(relay_in[base + 1, at], relay_in[base + 2, at], flags[q][2])
                fwd_copy(q, i, h).start()
            if i == 2:
                slot_in[lines(half + 2 * q), :] = relay_in[base + 2]

    def hand_back(q, i):
        base = (half - 1) * q

        @pl.when(inner == 1)
        def _():
            for h in range(2):
                at = slice(h * bit, (h + 1) * bit)
                owner_came(q, i, h).wait_recv()
                if i == 1:
                    back_out[base + 1, at] = mix(relay_ret[base + 1, at], relay_ret[base + 2, at], flags[q][1])
                if i == 2:
                    back_out[base + 2, at] = mix(ret_out[half + 2 * q, at], relay_ret[base + 2, at], flags[q][2])
                back_copy(q, i, h).start()

    def merge_out(q):
        base = (half - 1) * q

        @pl.when(inner == 0)
        def _():
            for h in range(2):
                at = slice(h * bit, (h + 1) * bit)
                owner_came(q, 2, h).wait_recv()
                back_out[base, at] = mix(relay_ret[base + 2, at], ret_out[half + 2 * q, at], flags[q][0])
                ret_merged(q, h).start()

    def frozen_block(i, carry):
        w_copy(i).wait()
        parts[i] = jnp.dot(tok_ref[...].reshape(rows, block), w_v[i], preferred_element_type=F32).astype(BF16)
        return carry

    def base_block(i, carry):
        q = lax.rem(tensor_count - i, tensor_count)
        acc[...] += nt_dot(cots[q].reshape(rows, out_block), w_v[i])
        return carry

    def rank_stage(g):
        if g == 0:
            near_came().wait_recv()
        else:
            slot_came(groups[g][1]).wait_recv()

            @pl.when(inner == 0)
            def _():
                slot_came(groups[g][0]).wait_recv()

        for s in groups[g]:
            x = slot_in[lines(s), :block]
            c = slot_in[lines(s), block:]
            inner_s = nt_dot(x, down_ref[adapter_of[s]])
            back_s = nt_dot(c, up_ref[adapter_of[s]])
            ranks[lines(s), :] = jnp.concatenate([inner_s, back_s], axis=1).astype(BF16)
        for q in range(1, tensor_count):
            rank_copy(g, q).start()

    def use_stage(g):
        ranks_came(g).wait_recv()
        total = ranks[rank_rows(g)].astype(F32)
        for s in range(tensor_count - 1):
            total = total + ranks_in[s, rank_rows(g)].astype(F32)
        for m, s in enumerate(groups[g]):
            part = total[m * length:(m + 1) * length]
            mid = part[:, :rank].astype(BF16)
            back = part[:, rank:].astype(BF16)
            target = ret_out if s else ret_in
            target[s, :, :block] = (adapter_scale * jnp.dot(
                back, down_ref[adapter_of[s]], preferred_element_type=F32)).astype(BF16)
            target[s, :, block:] = (adapter_scale * jnp.dot(
                mid, up_ref[adapter_of[s]], preferred_element_type=F32)).astype(BF16)
            for a in range(resident):
                back_m[a, lines(s), :] = (back.astype(F32) * weights[a][s]).astype(BF16)
                inner_m[a, lines(s), :] = (mid.astype(F32) * weights[a][s]).astype(BF16)
        if g:
            q = g - 1
            for h in range(2):
                ret_other(q, h).start()

            @pl.when(inner == 0)
            def _():
                for h in range(2):
                    ret_same(q, h).start()

    middle = max(1, tensor_count // 2)
    lax.fori_loop(0, middle, frozen_block, 0)
    lax.fori_loop(middle, tensor_count, frozen_block, 0)
    for q in range(1, tensor_count):
        part_copy(q).start()
    acc[...] = nt_dot(cot_ref[...].reshape(rows, out_block), w_v[0])
    relay(close, 0)
    cots_came().wait_recv()
    lax.fori_loop(1, middle, base_block, 0)
    down_copy.wait()
    up_copy.wait()
    onward(0)

    relay(close, 1)

    @pl.when(inner == 1)
    def _():
        near_copy(3).start()

    lax.fori_loop(middle, tensor_count, base_block, 0)
    onward(1)
    relay(close, 2)
    onward(2)
    relay(far, 0)
    rank_stage(1)
    use_stage(1)
    relay(far, 1)
    rank_stage(0)
    merge_out(close)
    relay(far, 2)
    use_stage(0)

    @pl.when(inner == 1)
    def _():
        ret_near(3).start()

    ret_near(2).start()
    hand_back(close, 2)
    hand_back(close, 1)
    rank_stage(2)
    hand_back(close, 0)
    use_stage(2)
    merge_out(far)
    ret_near(1).start()

    @pl.when(inner == 0)
    def _():
        ret_near(3).start()

    x_all = slot_in[:, :block]
    c_all = slot_in[:, block:]
    for a in range(resident):
        gd_ref[a] = tn_dot(back_m[a], x_all) * (
            adapter_scale / jnp.maximum(jnp.full((1, block), counts[a], F32), 1.0))
        gu_ref[a] = tn_dot(inner_m[a], c_all) * (
            adapter_scale / jnp.maximum(jnp.full((1, out_block), counts[a], F32), 1.0))
    gd_copy.start()
    gu_copy.start()
    for i in (2, 1, 0):
        hand_back(far, i)
    parts_came().wait_recv()
    backbone = parts[0].astype(F32)
    for q in range(1, tensor_count):
        backbone = backbone + part_in[q].astype(F32)
    rets_came().wait_recv()
    for j in range(seqs):
        came = ret_in[table_ref[8 + j]]
        kvo_ref[lines(j), :] = (backbone[lines(j)] + came[:, block:].astype(F32)).astype(BF16)
        tg_ref[lines(j), :] = (acc[lines(j), :] + came[:, :block].astype(F32)).astype(BF16)

    cots_came().wait_send()
    parts_came().wait_send()
    ranks_sent().wait_send()

    @pl.when(inner == 0)
    def _():
        sent(5 * half - 5).wait_send()

    @pl.when(inner == 1)
    def _():
        sent(dp_count + 6 * half - 6).wait_send()

    gd_copy.wait()
    gu_copy.wait()


def finish(pieces, *refs):
    n = len(pieces)
    given, out, sem = refs[:n], refs[n:2 * n], refs[2 * n]
    steps = [(i, p) for i in range(n) for p in range(pieces[i])]

    def move(at, i, p):
        span = given[i].shape[0] // pieces[i]
        rows = pl.ds(p * span, span)
        return pltpu.make_async_copy(given[i].at[rows], out[i].at[rows], sem.at[at])

    for at, (i, p) in enumerate(steps):
        move(at, i, p).start()
    for at, (i, p) in enumerate(steps):
        move(at, i, p).wait()


def shapes_of(rows, block, out_block, resident, rank):
    return (
        jax.ShapeDtypeStruct((rows, out_block), BF16),
        jax.ShapeDtypeStruct((rows, block), BF16),
        jax.ShapeDtypeStruct((resident, rank, block), F32),
        jax.ShapeDtypeStruct((resident, rank, out_block), F32),
    )


def direct(dp_count, tensor_count, tok, w, down, up, cot, seq_index, storage):
    resident, rank, block = down.shape
    out_block = up.shape[2]
    rows = tok.shape[0]
    seqs = seq_index.shape[0] // dp_count
    length = rows // seqs
    groups = len(slot_groups(dp_count))
    anywhere = pl.BlockSpec(memory_space=pl.ANY)
    wide = block + out_block
    vmem = pl.BlockSpec(memory_space=pltpu.VMEM)
    smem = pl.BlockSpec(memory_space=pltpu.SMEM)
    dma = pltpu.SemaphoreType.DMA
    table, weights = pl.pallas_call(
        functools.partial(routes, dp_count, seqs, resident),
        out_shape=(
            jax.ShapeDtypeStruct((2 * dp_count + seqs,), jnp.int32),
            jax.ShapeDtypeStruct((resident * dp_count + resident,), F32),
        ),
        in_specs=[smem, smem],
        out_specs=(smem, smem),
    )(seq_index, storage)
    return pl.pallas_call(
        functools.partial(kernel, dp_count, tensor_count),
        out_shape=shapes_of(rows, block, out_block, resident, rank),
        in_specs=[smem, smem, vmem, anywhere, anywhere, anywhere, vmem, vmem],
        out_specs=(vmem, vmem, anywhere, anywhere),
        scratch_shapes=[
            pltpu.VMEM(down.shape, BF16),
            pltpu.VMEM(up.shape, BF16),
            pltpu.VMEM(down.shape, F32),
            pltpu.VMEM(up.shape, F32),
            pltpu.VMEM((tensor_count, w.shape[0], out_block), BF16),
            pltpu.VMEM((dp_count * length, wide), BF16),
            pltpu.VMEM((dp_count * length, wide), BF16),
            pltpu.VMEM((dp_count, length, wide), BF16),
            pltpu.VMEM((dp_count, length, wide), BF16),
            pltpu.VMEM((tensor_count, rows, out_block), BF16),
            pltpu.VMEM((tensor_count, rows, out_block), BF16),
            pltpu.VMEM((tensor_count, rows, out_block), BF16),
            pltpu.VMEM((tensor_count, dp_count * length, 2 * rank), BF16),
            pltpu.VMEM((resident, dp_count * length, rank), BF16),
            pltpu.VMEM((resident, dp_count * length, rank), BF16),
            pltpu.VMEM((rows, block), F32),
            dma((tensor_count,)),
            dma((4,)),
            dma((dp_count,)),
            dma((dp_count,)),
            dma((dp_count,)),
            dma((dp_count,)),
            dma((tensor_count,)),
            dma((tensor_count,)),
            dma((tensor_count,)),
            dma((tensor_count,)),
            dma((groups, tensor_count)),
            dma((groups, tensor_count)),
        ],
        compiler_params=pltpu.CompilerParams(
            collective_id=1, has_side_effects=True, vmem_limit_bytes=60 * 1024 * 1024
        ),
    )(
        table, weights, tok.reshape(seqs, length, block), w, down, up, cot,
        cot.reshape(seqs, length, out_block))


def relayed(dp_count, tensor_count, table, weights, tok, w, down, up, cot, seqs):
    resident, rank, block = down.shape
    out_block = up.shape[2]
    rows = tok.shape[0]
    length = rows // seqs
    half = dp_count // 2
    anywhere = pl.BlockSpec(memory_space=pl.ANY)
    wide = block + out_block
    vmem = pl.BlockSpec(memory_space=pltpu.VMEM)
    smem = pl.BlockSpec(memory_space=pltpu.SMEM)
    dma = pltpu.SemaphoreType.DMA

    def slots(*lead):
        return pltpu.VMEM(lead + (length, wide), BF16)

    return pl.pallas_call(
        functools.partial(relay_kernel, dp_count, tensor_count),
        out_shape=shapes_of(rows, block, out_block, resident, rank),
        in_specs=[smem, smem] + [anywhere] * 5,
        out_specs=(vmem, vmem, anywhere, anywhere),
        scratch_shapes=[
            pltpu.VMEM(down.shape, BF16),
            pltpu.VMEM(up.shape, BF16),
            pltpu.VMEM(down.shape, F32),
            pltpu.VMEM(up.shape, F32),
            pltpu.VMEM((seqs, length, block), BF16),
            pltpu.VMEM((seqs, length, out_block), BF16),
            pltpu.VMEM((tensor_count, w.shape[0], out_block), BF16),
            slots(half - 1),
            slots(half - 1),
            slots(half - 1),
            pltpu.VMEM((dp_count * length, wide), BF16),
            slots(2, half - 2),
            slots(dp_count + 6 * half - 6),
            slots(dp_count - 1),
            pltpu.VMEM((tensor_count, seqs, length, out_block), BF16),
            pltpu.VMEM((tensor_count, rows, out_block), BF16),
            pltpu.VMEM((tensor_count, rows, out_block), BF16),
            pltpu.VMEM((dp_count * length, 2 * rank), BF16),
            pltpu.VMEM((tensor_count - 1, dp_count * length, 2 * rank), BF16),
            pltpu.VMEM((resident, dp_count * length, rank), BF16),
            pltpu.VMEM((resident, dp_count * length, rank), BF16),
            pltpu.VMEM((rows, block), F32),
            dma((tensor_count,)),
            dma((6,)),
            dma,
            dma,
            dma((half,)),
            dma((2, half - 1, 2)),
            dma((half - 1, 2)),
            dma((2, half - 1, 2)),
            dma,
            dma,
            dma,
            dma,
            dma,
            dma,
            dma((3,)),
        ],
        compiler_params=pltpu.CompilerParams(
            collective_id=0, has_side_effects=True, vmem_limit_bytes=60 * 1024 * 1024
        ),
    )(
        table, weights, tok.reshape(seqs, length, block), w, down, up, cot.reshape(seqs, length, out_block))


def on_device(dp_count, tensor_count, tok, w, down, up, cot, seq_index, storage):
    resident = down.shape[0]
    seqs = seq_index.shape[0] // dp_count
    anywhere = pl.BlockSpec(memory_space=pl.ANY)
    vmem = pl.BlockSpec(memory_space=pltpu.VMEM)
    smem = pl.BlockSpec(memory_space=pltpu.SMEM)
    dma = pltpu.SemaphoreType.DMA
    args = (tok, w, down, up, cot)
    if relay_fits(dp_count, seqs):
        table, weights, fits = pl.pallas_call(
            functools.partial(relay_routes, dp_count, seqs, resident),
            out_shape=(
                jax.ShapeDtypeStruct((32,), jnp.int32),
                jax.ShapeDtypeStruct((resident * dp_count + resident,), F32),
                jax.ShapeDtypeStruct((1,), jnp.int32),
            ),
            in_specs=[smem, smem],
            out_specs=(smem,) * 3,
        )(seq_index, storage)
        results = lax.cond(
            fits.reshape(()) > 0,
            lambda: relayed(dp_count, tensor_count, table, weights, *args, seqs),
            lambda: direct(dp_count, tensor_count, *args, seq_index, storage),
        )
    else:
        results = direct(dp_count, tensor_count, *args, seq_index, storage)
    pieces = (1, 2, resident, 1)
    return pl.pallas_call(
        functools.partial(finish, pieces),
        out_shape=tuple(jax.ShapeDtypeStruct(r.shape, r.dtype) for r in results),
        in_specs=[vmem] * 4,
        out_specs=(anywhere,) * 4,
        scratch_shapes=[dma((sum(pieces),))],
    )(*results)


def solution(mesh):
    in_specs = (
        P("dp", "tensor"),
        P("tensor", None),
        P("dp", None, "tensor"),
        P("dp", None, "tensor"),
        P("dp", "tensor"),
        P(),
        P(),
    )
    out_specs = (
        P("dp", "tensor"),
        P("dp", "tensor"),
        P("dp", None, "tensor"),
        P("dp", None, "tensor"),
    )
    return jax.shard_map(
        functools.partial(on_device, mesh.shape["dp"], mesh.shape["tensor"]),
        mesh=mesh, in_specs=in_specs, out_specs=out_specs, check_vma=False,
    )
```

```python
import functools

import jax
import jax.numpy as jnp
from jax import lax
from jax.experimental import pallas as pl
from jax.experimental.pallas import tpu as pltpu
from jax.sharding import PartitionSpec as P

adapter_scale = 0.25
MESH = pl.DeviceIdType.MESH
F32 = jnp.float32
BF16 = jnp.bfloat16


def nt_dot(a, b):
    return lax.dot_general(a, b, (((1,), (1,)), ((), ())), preferred_element_type=F32)


def tn_dot(a, b):
    return lax.dot_general(a, b, (((0,), (0,)), ((), ())), preferred_element_type=F32)


def partner(d, k, dp_count):
    out, bit = d, 1
    while bit < dp_count:
        if k & bit:
            out = out + bit - 2 * bit * lax.rem(lax.div(d, jnp.int32(bit)), jnp.int32(2))
        bit *= 2
    return out


def routes(dp_count, seqs, resident, seq_ref, store_ref, table_ref, weight_ref):
    d = lax.axis_index("dp")
    rows = [store_ref[seq_ref[d * seqs + j]] for j in range(seqs)]
    owners = [lax.div(r, jnp.int32(resident)) for r in rows]
    dist = []
    for j in range(seqs):
        slot = jnp.int32(0)
        for k in range(1, dp_count):
            slot = jnp.where(owners[j] == partner(d, k, dp_count), jnp.int32(k), slot)
        dist.append(slot)
    for j in range(seqs):
        table_ref[2 * dp_count + j] = dist[j]
    for k in range(dp_count):
        pick = jnp.int32(0)
        for j in range(seqs):
            pick = jnp.where(dist[j] == k, jnp.int32(j), pick)
        table_ref[k] = pick
    counts = [jnp.float32(0.0)] * resident
    for k in range(dp_count):
        reader = partner(d, k, dp_count)
        found = jnp.int32(-1)
        for j in range(seqs):
            local = store_ref[seq_ref[reader * seqs + j]] - d * resident
            found = jnp.where((local >= 0) & (local < resident), local, found)
        table_ref[dp_count + k] = jnp.maximum(found, 0)
        for a in range(resident):
            hit = jnp.where(found == a, jnp.float32(1.0), jnp.float32(0.0))
            weight_ref[a * dp_count + k] = hit
            counts[a] = counts[a] + hit
    for a in range(resident):
        weight_ref[resident * dp_count + a] = counts[a]


def slot_groups(dp_count):
    order = list(range(dp_count - 1, -1, -1))
    quarter = dp_count // 4
    return [order[:quarter], order[quarter:2 * quarter], order[2 * quarter:]]


def kernel(
    dp_count,
    tensor_count,
    table_ref,
    weight_ref,
    tok_ref,
    w_ref,
    down_hbm,
    up_hbm,
    cot_ref,
    cot_seq_ref,
    kvo_ref,
    tg_ref,
    gd_hbm,
    gu_hbm,
    down_ref,
    up_ref,
    gd_ref,
    gu_ref,
    w_v,
    slot_out,
    slot_in,
    ret_out,
    ret_in,
    cots,
    parts,
    part_in,
    ranks,
    back_m,
    inner_m,
    acc,
    w_sem,
    local_sem,
    slot_ssem,
    slot_rsem,
    ret_ssem,
    ret_rsem,
    cot_ssem,
    cot_rsem,
    part_ssem,
    part_rsem,
    rank_ssem,
    rank_rsem,
):
    d = lax.axis_index("dp")
    t = lax.axis_index("tensor")
    resident, rank, block = down_ref.shape
    out_block = up_ref.shape[2]
    seqs, length = tok_ref.shape[:2]
    rows = seqs * length
    groups = slot_groups(dp_count)
    starts = [sum(len(g) for g in groups[:i]) for i in range(len(groups))]

    def dp_to(k):
        return partner(d, k, dp_count)

    def t_to(q):
        return lax.rem(t + q, tensor_count)

    def t_from(q):
        return lax.rem(t + tensor_count - q, tensor_count)

    def w_copy(i):
        c = t_to(i)
        return pltpu.make_async_copy(
            w_ref.at[:, pl.ds(pl.multiple_of(c * out_block, out_block), out_block)],
            w_v.at[i],
            w_sem.at[i],
        )

    down_copy = pltpu.make_async_copy(down_hbm, down_ref, local_sem.at[0])
    up_copy = pltpu.make_async_copy(up_hbm, up_ref, local_sem.at[1])
    gd_copy = pltpu.make_async_copy(gd_ref, gd_hbm, local_sem.at[2])
    gu_copy = pltpu.make_async_copy(gu_ref, gu_hbm, local_sem.at[3])
    for i in range(tensor_count):
        w_copy(i).start()
    down_copy.start()
    up_copy.start()

    barrier = pltpu.get_barrier_semaphore()
    for k in range(1, dp_count):
        pl.semaphore_signal(barrier, inc=1, device_id={"dp": dp_to(k)}, device_id_type=MESH)
    for q in range(1, tensor_count):
        pl.semaphore_signal(barrier, inc=1, device_id={"tensor": t_to(q)}, device_id_type=MESH)

    for k in range(dp_count):
        pick = table_ref[k]
        target = slot_in if k == 0 else slot_out
        target[k * length:(k + 1) * length, :block] = tok_ref[pick]
        target[k * length:(k + 1) * length, block:] = cot_seq_ref[pick]

    pl.semaphore_wait(barrier, dp_count + tensor_count - 2)

    def cot_copy(q):
        return pltpu.make_async_remote_copy(
            cot_ref, cots.at[q], cot_ssem.at[q], cot_rsem.at[q],
            device_id={"tensor": t_to(q)}, device_id_type=MESH)

    def slot_copy(k):
        at = pl.ds(k * length, length)
        return pltpu.make_async_remote_copy(
            slot_out.at[at], slot_in.at[at], slot_ssem.at[k], slot_rsem.at[k],
            device_id={"dp": dp_to(k)}, device_id_type=MESH)

    def ret_copy(k):
        return pltpu.make_async_remote_copy(
            ret_out.at[k], ret_in.at[k], ret_ssem.at[k], ret_rsem.at[k],
            device_id={"dp": dp_to(k)}, device_id_type=MESH)

    def part_copy(q):
        return pltpu.make_async_remote_copy(
            parts.at[q], part_in.at[q], part_ssem.at[q], part_rsem.at[q],
            device_id={"tensor": t_to(q)}, device_id_type=MESH)

    def rank_rows(g):
        return pl.ds(starts[g] * length, len(groups[g]) * length)

    def rank_copy(g, q):
        return pltpu.make_async_remote_copy(
            ranks.at[t, rank_rows(g)], ranks.at[t, rank_rows(g)], rank_ssem.at[g, q], rank_rsem.at[g, q],
            device_id={"tensor": t_to(q)}, device_id_type=MESH)

    for k in range(dp_count - 1, 0, -1):
        slot_copy(k).start()
    for q in range(1, tensor_count):
        cot_copy(q).start()

    adapter_of = [table_ref[dp_count + k] for k in range(dp_count)]
    weights = [[weight_ref[a * dp_count + k] for k in range(dp_count)] for a in range(resident)]
    counts = [weight_ref[resident * dp_count + a] for a in range(resident)]

    def frozen_block(i, carry):
        w_copy(i).wait()
        parts[i] = jnp.dot(tok_ref[...].reshape(rows, block), w_v[i], preferred_element_type=F32).astype(BF16)
        return carry

    lax.fori_loop(0, tensor_count, frozen_block, 0)

    def rank_stage(g):
        for m, k in enumerate(groups[g]):
            if k:
                slot_copy(k).wait_recv()
            x = slot_in[k * length:(k + 1) * length, :block]
            c = slot_in[k * length:(k + 1) * length, block:]
            inner = nt_dot(x, down_ref[adapter_of[k]])
            back = nt_dot(c, up_ref[adapter_of[k]])
            ranks[t, (starts[g] + m) * length:(starts[g] + m + 1) * length, :] = jnp.concatenate(
                [inner, back], axis=1).astype(BF16)
        for q in range(1, tensor_count):
            rank_copy(g, q).start()

    def base_block(i, carry):
        q = lax.rem(tensor_count - i, tensor_count)
        acc[...] += nt_dot(cots[q], w_v[i])
        return carry

    def use_stage(g):
        for q in range(1, tensor_count):
            s = t_from(q)
            pltpu.make_async_remote_copy(
                ranks.at[s, rank_rows(g)], ranks.at[s, rank_rows(g)], rank_ssem.at[g, q], rank_rsem.at[g, q],
                device_id={"tensor": t_to(q)}, device_id_type=MESH).wait_recv()
        for q in range(1, tensor_count):
            rank_copy(g, q).wait_send()
        total = ranks[0, rank_rows(g)].astype(F32)
        for s in range(1, tensor_count):
            total = total + ranks[s, rank_rows(g)].astype(F32)
        for m, k in enumerate(groups[g]):
            lines = total[m * length:(m + 1) * length]
            inner = lines[:, :rank].astype(BF16)
            back = lines[:, rank:].astype(BF16)
            target = ret_out if k else ret_in
            target[k, :, :block] = (adapter_scale * jnp.dot(
                back, down_ref[adapter_of[k]], preferred_element_type=F32)).astype(BF16)
            target[k, :, block:] = (adapter_scale * jnp.dot(
                inner, up_ref[adapter_of[k]], preferred_element_type=F32)).astype(BF16)
            for a in range(resident):
                at = slice(k * length, (k + 1) * length)
                back_m[a, at, :] = (back.astype(F32) * weights[a][k]).astype(BF16)
                inner_m[a, at, :] = (inner.astype(F32) * weights[a][k]).astype(BF16)
            if k:
                ret_copy(k).start()

    for q in range(1, tensor_count):
        part_copy(q).start()
    half = max(1, tensor_count // 2)
    acc[...] = nt_dot(cot_ref[...], w_v[0])
    for q in range(1, tensor_count):
        cot_copy(q).wait_recv()
    lax.fori_loop(1, half, base_block, 0)
    down_copy.wait()
    up_copy.wait()
    rank_stage(0)
    lax.fori_loop(half, tensor_count, base_block, 0)
    use_stage(0)
    rank_stage(1)
    use_stage(1)
    rank_stage(2)
    use_stage(2)

    x_all = slot_in[:, :block]
    c_all = slot_in[:, block:]
    for a in range(resident):
        gd_ref[a] = tn_dot(back_m[a], x_all) * (
            adapter_scale / jnp.maximum(jnp.full((1, block), counts[a], F32), 1.0))
        gu_ref[a] = tn_dot(inner_m[a], c_all) * (
            adapter_scale / jnp.maximum(jnp.full((1, out_block), counts[a], F32), 1.0))

    gd_copy.start()
    gu_copy.start()
    for q in range(1, tensor_count):
        part_copy(q).wait_recv()
    backbone = parts[0].astype(F32)
    for q in range(1, tensor_count):
        backbone = backbone + part_in[q].astype(F32)
    for k in range(1, dp_count):
        ret_copy(k).wait_recv()
    for j in range(seqs):
        at = slice(j * length, (j + 1) * length)
        came = ret_in[table_ref[2 * dp_count + j]]
        kvo_ref[at, :] = (backbone[at] + came[:, block:].astype(F32)).astype(BF16)
        tg_ref[at, :] = (acc[at, :] + came[:, :block].astype(F32)).astype(BF16)

    for k in range(1, dp_count):
        slot_copy(k).wait_send()
        ret_copy(k).wait_send()
    for q in range(1, tensor_count):
        cot_copy(q).wait_send()
        part_copy(q).wait_send()
    gd_copy.wait()
    gu_copy.wait()


def mix(first, second, flag):
    return jnp.where(flag > 0, first, second)


def relay_fits(dp_count, seqs):
    return dp_count == 2 * seqs and seqs == 4


def relay_routes(dp_count, seqs, resident, seq_ref, store_ref, table_ref, weight_ref, fits_ref):
    d = lax.axis_index("dp")
    half = dp_count // 2
    xor = lax.bitwise_xor
    level = lax.div(d, jnp.int32(2))
    inner = lax.rem(lax.div(level + 1, jnp.int32(2)), jnp.int32(2))
    home = (2 - lax.div(d, jnp.int32(half))) * 2 + lax.rem(d, jnp.int32(2))
    zero, one = jnp.int32(0), jnp.int32(1)
    hub = xor(d, 2 - 2 * inner)
    worst = zero
    counts = [jnp.float32(0.0)] * resident
    for k in range(dp_count):
        p = xor(d, jnp.int32(k))
        crossing, found = zero, jnp.int32(-1)
        near = [zero] * half
        has, which = [zero] * half, [zero] * half
        apart = []
        for j in range(seqs):
            row = store_ref[seq_ref[p * seqs + j]]
            owner = lax.div(row, jnp.int32(resident))
            away = xor(owner, p)
            crossing = crossing + jnp.where(away >= half, one, zero)
            found = jnp.where(owner == d, row - d * resident, found)
            if k == 0:
                step = xor(owner, home)
                apart.append((away, step))
                for m in range(half):
                    near[m] = jnp.where(away == m, jnp.int32(j), near[m])
            if k in (0, half, half + 2):
                step = xor(owner, home if k == 0 else hub)
                for m in range(half):
                    hit = step == half - 1 - m
                    has[m] = jnp.where(hit, one, has[m])
                    which[m] = jnp.where(hit, jnp.int32(j), which[m])
        worst = jnp.maximum(worst, crossing)
        if k == 0:
            for m in range(half):
                table_ref[m] = near[m]
            table_ref[half] = jnp.where(has[0] > 0, which[0], which[1])
            table_ref[half + 1] = jnp.where((has[0] > 0) & (has[1] > 0), which[1], which[2])
            table_ref[half + 2] = jnp.where(has[3] > 0, which[3], which[2])
            place = [zero, jnp.where(has[0] > 0, one, zero), jnp.where(has[3] > 0, one, jnp.int32(2)), jnp.int32(2)]
            for j in range(seqs):
                away, step = apart[j]
                came = away
                for m in range(half):
                    came = jnp.where(step == half - 1 - m, half + place[m], came)
                table_ref[8 + j] = came
        if k in (half, half + 2):
            q = inner if k == half else 1 - inner
            table_ref[20 + 3 * q] = has[0]
            table_ref[21 + 3 * q] = has[0] * has[1]
            table_ref[22 + 3 * q] = has[3]
        s = jnp.int32(k) if k < half else xor(jnp.int32(k), 2 * inner)
        table_ref[12 + s] = jnp.maximum(found, 0)
        for a in range(resident):
            hit = jnp.where(found == a, jnp.float32(1.0), jnp.float32(0.0))
            weight_ref[a * dp_count + s] = hit
            counts[a] = counts[a] + hit
    for a in range(resident):
        weight_ref[resident * dp_count + a] = counts[a]
    fits_ref[0] = jnp.where(worst < half, one, zero)


def relay_kernel(
    dp_count,
    tensor_count,
    table_ref,
    weight_ref,
    tok_hbm,
    w_ref,
    down_hbm,
    up_hbm,
    cot_hbm,
    kvo_ref,
    tg_ref,
    gd_hbm,
    gu_hbm,
    down_ref,
    up_ref,
    gd_ref,
    gu_ref,
    tok_ref,
    cot_ref,
    w_v,
    near_out,
    cross_out,
    stage_in,
    slot_in,
    relay_out,
    bulk,
    ret_in,
    cots,
    parts,
    part_in,
    ranks,
    ranks_in,
    back_m,
    inner_m,
    acc,
    w_sem,
    local_sem,
    send_sem,
    near_rsem,
    slot_rsem,
    relay_rsem,
    stage_rsem,
    owner_rsem,
    ret_rsem,
    cot_ssem,
    cot_rsem,
    part_ssem,
    part_rsem,
    rank_ssem,
    rank_rsem,
):
    d = lax.axis_index("dp")
    t = lax.axis_index("tensor")
    resident, rank, block = down_ref.shape
    out_block = up_ref.shape[2]
    seqs, length = tok_ref.shape[:2]
    rows = seqs * length
    bit = length // 2
    half = dp_count // 2
    level = lax.div(d, jnp.int32(2))
    inner = lax.rem(lax.div(level + 1, jnp.int32(2)), jnp.int32(2))
    outer = 1 - inner
    peer = [partner(d, k, dp_count) for k in range(dp_count)]
    groups = [[0, 1, 2, 3], [4, 5], [6, 7]]
    starts = [0, 4, 6]
    close, far = 0, 1

    ret_out = bulk.at[pl.ds(0, dp_count)]
    relay_ret, back_out, relay_in = (
        bulk.at[pl.ds(dp_count + 2 * (half - 1) * n, 2 * (half - 1))] for n in range(3))

    def t_to(q):
        return lax.rem(t + q, tensor_count)

    def t_from(q):
        return lax.rem(t + tensor_count - q, tensor_count)

    def lines(s):
        return slice(s * length, (s + 1) * length)

    def w_copy(i):
        c = t_to(i)
        return pltpu.make_async_copy(
            w_ref.at[:, pl.ds(pl.multiple_of(c * out_block, out_block), out_block)],
            w_v.at[i],
            w_sem.at[i],
        )

    def over(source, target, ssem, rsem, **where):
        return pltpu.make_async_remote_copy(
            source, target, ssem, rsem, device_id=where, device_id_type=MESH)

    def piece(h):
        return pl.ds(h * bit, bit)

    def slot_at(s, h):
        return slot_in.at[pl.ds(s * length + h * bit, bit)]

    def near_copy(k):
        return over(near_out.at[k - 1], slot_in.at[pl.ds(k * length, length)], send_sem, near_rsem, dp=peer[k])

    def near_came():
        at = slot_in.at[pl.ds(length, (half - 1) * length)]
        return over(at, at, send_sem, near_rsem, dp=peer[1])

    def cross_copy(i, h):
        return over(cross_out.at[i, piece(h)], relay_in.at[i, piece(h)],
                    send_sem, relay_rsem.at[close, i, h], dp=peer[half + 2])

    def stage_copy(i, h):
        return over(cross_out.at[i, piece(h)], stage_in.at[i, piece(h)], send_sem, stage_rsem.at[i, h], dp=peer[2])

    def onward_copy(i, h):
        return over(stage_in.at[i, piece(h)], relay_in.at[half - 1 + i, piece(h)],
                    send_sem, relay_rsem.at[far, i, h], dp=peer[half + 2])

    def cross_came(q, i, h):
        at = relay_in.at[(half - 1) * q + i, piece(h)]
        return over(at, at, send_sem, relay_rsem.at[q, i, h], dp=peer[half + 2])

    def fwd_copy(q, m, h):
        s = half + 2 * q + (0 if m == 1 else 1)
        source = relay_out.at[q, m - 1, piece(h)] if m else relay_in.at[(half - 1) * q, piece(h)]
        return over(source, slot_at(s, h), send_sem, slot_rsem.at[s - half, h], dp=peer[3 - m])

    def slot_came(s, h):
        return over(slot_at(s, h), slot_at(s, h), send_sem, slot_rsem.at[s - half, h], dp=peer[1])

    def ret_near(k):
        return over(ret_out.at[k], ret_in.at[k], send_sem, ret_rsem, dp=peer[k])

    def ret_same(q, h):
        return over(ret_out.at[half + 2 * q, piece(h)], relay_ret.at[(half - 1) * q + 1, piece(h)],
                    send_sem, owner_rsem.at[q, 1, h], dp=peer[2])

    def ret_other(q, h):
        return over(ret_out.at[half + 2 * q + 1, piece(h)], relay_ret.at[(half - 1) * q + 2, piece(h)],
                    send_sem, owner_rsem.at[q, 2, h], dp=peer[1])

    def ret_merged(q, h):
        return over(back_out.at[(half - 1) * q, piece(h)], relay_ret.at[(half - 1) * q, piece(h)],
                    send_sem, owner_rsem.at[q, 0, h], dp=peer[2])

    def owner_came(q, m, h):
        at = relay_ret.at[(half - 1) * q + m, piece(h)]
        return over(at, at, send_sem, owner_rsem.at[q, m, h], dp=peer[1])

    def back_copy(q, i, h):
        source = (back_out if i else relay_ret).at[(half - 1) * q + i, piece(h)]
        return over(source, ret_in.at[half + i, piece(h)], send_sem, ret_rsem, dp=peer[half + 2 - 2 * q])

    def rets_came():
        at = ret_in.at[pl.ds(1, 2 * half - 2)]
        return over(at, at, send_sem, ret_rsem, dp=peer[1])

    def sent(count):
        return over(bulk.at[pl.ds(0, count)], bulk.at[pl.ds(0, count)], send_sem, ret_rsem, dp=peer[1])

    def cot_copy(q):
        return over(cot_ref, cots.at[q], cot_ssem, cot_rsem, tensor=t_to(q))

    def cots_came():
        at = cots.at[pl.ds(1, tensor_count - 1)]
        return over(at, at, cot_ssem, cot_rsem, tensor=t_to(1))

    def part_copy(q):
        return over(parts.at[q], part_in.at[q], part_ssem, part_rsem, tensor=t_to(q))

    def parts_came():
        at = part_in.at[pl.ds(1, tensor_count - 1)]
        return over(at, at, part_ssem, part_rsem, tensor=t_to(1))

    def spans(g, h):
        size = length if g == 0 else bit
        return [(s, slice(s * length + h * size, s * length + (h + 1) * size)) for s in groups[g]]

    def rank_at(g, h):
        return 2 * starts[g] * bit + h * len(groups[g]) * bit

    def rank_rows(g, h):
        return pl.ds(rank_at(g, h), len(groups[g]) * (length if g == 0 else bit))

    def rank_sem(g, h):
        return rank_rsem.at[2 * g - 1 + h if g else 0]

    def rank_copy(g, h, q):
        return over(ranks.at[rank_rows(g, h)], ranks_in.at[q - 1, rank_rows(g, h)],
                    rank_ssem, rank_sem(g, h), tensor=t_to(q))

    def ranks_came(g, h):
        at = ranks_in.at[:, rank_rows(g, h)]
        return over(at, at, rank_ssem, rank_sem(g, h), tensor=t_to(1))

    def ranks_sent():
        return over(ranks_in, ranks_in, rank_ssem, rank_rsem.at[0], tensor=t_to(1))

    down_copy = pltpu.make_async_copy(down_hbm, down_ref, local_sem.at[0])
    up_copy = pltpu.make_async_copy(up_hbm, up_ref, local_sem.at[1])
    gd_copy = pltpu.make_async_copy(gd_ref, gd_hbm, local_sem.at[2])
    gu_copy = pltpu.make_async_copy(gu_ref, gu_hbm, local_sem.at[3])

    tok_copy = pltpu.make_async_copy(tok_hbm, tok_ref, local_sem.at[4])
    seed_copy = pltpu.make_async_copy(cot_hbm, cot_ref, local_sem.at[5])
    tok_copy.start()
    seed_copy.start()

    barrier = pltpu.get_barrier_semaphore()
    for k in range(1, half + 1):
        pl.semaphore_signal(barrier, inc=1, device_id={"dp": peer[k]}, device_id_type=MESH)

    @pl.when(inner == 1)
    def _():
        pl.semaphore_signal(barrier, inc=1, device_id={"dp": peer[half + 2]}, device_id_type=MESH)

    for q in range(1, tensor_count):
        pl.semaphore_signal(barrier, inc=1, device_id={"tensor": t_to(q)}, device_id_type=MESH)
    for i in range(tensor_count):
        w_copy(i).start()
    down_copy.start()
    up_copy.start()
    tok_copy.wait()
    seed_copy.wait()

    for i in range(half - 1):
        pick = table_ref[half + i]
        cross_out[i, :, :block] = tok_ref[pick]
        cross_out[i, :, block:] = cot_ref[pick]
    for k in range(half):
        pick = table_ref[k]
        if k == 0:
            slot_in[:length, :block] = tok_ref[pick]
            slot_in[:length, block:] = cot_ref[pick]
        else:
            near_out[k - 1, :, :block] = tok_ref[pick]
            near_out[k - 1, :, block:] = cot_ref[pick]

    pl.semaphore_wait(barrier, half + inner + tensor_count - 1)

    @pl.when(inner == 1)
    def _():
        for i in range(half - 1):
            for h in range(2):
                cross_copy(i, h).start()

    @pl.when(inner == 0)
    def _():
        near_copy(3).start()
        for i in range(half - 1):
            for h in range(2):
                stage_copy(i, h).start()

    near_copy(1).start()
    near_copy(2).start()

    for q in range(1, tensor_count):
        cot_copy(q).start()

    adapter_of = [table_ref[12 + s] for s in range(dp_count)]
    flags = [[table_ref[20 + 3 * q + i] for i in range(3)] for q in range(2)]
    weights = [[weight_ref[a * dp_count + s] for s in range(dp_count)] for a in range(resident)]
    counts = [weight_ref[resident * dp_count + a] for a in range(resident)]

    def onward(i):
        @pl.when(inner == 1)
        def _():
            for h in range(2):
                stage_copy(i, h).wait_recv()
                onward_copy(i, h).start()

    def relay(q, i):
        base = (half - 1) * q

        @pl.when(inner == 1)
        def _():
            for h in range(2):
                at = slice(h * bit, (h + 1) * bit)
                cross_came(q, i, h).wait_recv()
                if i == 1:
                    relay_out[q, 0, at] = mix(relay_in[base + 1, at], relay_in[base, at], flags[q][0])
                if i == 2:
                    relay_out[q, 1, at] = mix(relay_in[base + 1, at], relay_in[base + 2, at], flags[q][2])
                fwd_copy(q, i, h).start()
            if i == 2:
                slot_in[lines(half + 2 * q), :] = relay_in[base + 2]

    def hand_back(q, i):
        base = (half - 1) * q

        @pl.when(inner == 1)
        def _():
            for h in range(2):
                at = slice(h * bit, (h + 1) * bit)
                owner_came(q, i, h).wait_recv()
                if i == 1:
                    back_out[base + 1, at] = mix(relay_ret[base + 1, at], relay_ret[base + 2, at], flags[q][1])
                if i == 2:
                    back_out[base + 2, at] = mix(ret_out[half + 2 * q, at], relay_ret[base + 2, at], flags[q][2])
                back_copy(q, i, h).start()

    def merge_out(q):
        base = (half - 1) * q

        @pl.when(inner == 0)
        def _():
            for h in range(2):
                at = slice(h * bit, (h + 1) * bit)
                owner_came(q, 2, h).wait_recv()
                back_out[base, at] = mix(relay_ret[base + 2, at], ret_out[half + 2 * q, at], flags[q][0])
                ret_merged(q, h).start()

    def frozen_block(i, carry):
        w_copy(i).wait()
        parts[i] = jnp.dot(tok_ref[...].reshape(rows, block), w_v[i], preferred_element_type=F32).astype(BF16)
        return carry

    def base_block(i, carry):
        q = lax.rem(tensor_count - i, tensor_count)
        acc[...] += nt_dot(cots[q].reshape(rows, out_block), w_v[i])
        return carry

    def rank_stage(g, h):
        if g == 0:
            near_came().wait_recv()
        else:
            slot_came(groups[g][1], h).wait_recv()

            @pl.when(inner == 0)
            def _():
                slot_came(groups[g][0], h).wait_recv()

        base = rank_at(g, h)
        for s, at in spans(g, h):
            x = slot_in[at, :block]
            c = slot_in[at, block:]
            inner_s = nt_dot(x, down_ref[adapter_of[s]])
            back_s = nt_dot(c, up_ref[adapter_of[s]])
            size = at.stop - at.start
            ranks[base:base + size, :] = jnp.concatenate([inner_s, back_s], axis=1).astype(BF16)
            base += size
        for q in range(1, tensor_count):
            rank_copy(g, h, q).start()

    def use_stage(g, h):
        ranks_came(g, h).wait_recv()
        total = ranks[rank_rows(g, h)].astype(F32)
        for s in range(tensor_count - 1):
            total = total + ranks_in[s, rank_rows(g, h)].astype(F32)
        base = 0
        for s, at in spans(g, h):
            size = at.stop - at.start
            part = total[base:base + size]
            base += size
            mid = part[:, :rank].astype(BF16)
            back = part[:, rank:].astype(BF16)
            target = ret_out if s else ret_in
            to = slice(at.start - s * length, at.stop - s * length)
            target[s, to, :block] = (adapter_scale * jnp.dot(
                back, down_ref[adapter_of[s]], preferred_element_type=F32)).astype(BF16)
            target[s, to, block:] = (adapter_scale * jnp.dot(
                mid, up_ref[adapter_of[s]], preferred_element_type=F32)).astype(BF16)
            for a in range(resident):
                back_m[a, at, :] = (back.astype(F32) * weights[a][s]).astype(BF16)
                inner_m[a, at, :] = (mid.astype(F32) * weights[a][s]).astype(BF16)
        if g:
            ret_other(g - 1, h).start()

            @pl.when(inner == 0)
            def _():
                ret_same(g - 1, h).start()

    middle = max(1, tensor_count // 2)
    lax.fori_loop(0, middle, frozen_block, 0)
    lax.fori_loop(middle, tensor_count, frozen_block, 0)
    for q in range(1, tensor_count):
        part_copy(q).start()
    acc[...] = nt_dot(cot_ref[...].reshape(rows, out_block), w_v[0])
    relay(close, 0)
    cots_came().wait_recv()
    lax.fori_loop(1, middle, base_block, 0)
    down_copy.wait()
    up_copy.wait()
    onward(0)

    relay(close, 1)

    @pl.when(inner == 1)
    def _():
        near_copy(3).start()

    lax.fori_loop(middle, tensor_count, base_block, 0)
    onward(1)
    relay(close, 2)
    rank_stage(1, 0)
    onward(2)
    relay(far, 0)
    rank_stage(1, 1)
    use_stage(1, 0)
    use_stage(1, 1)
    relay(far, 1)
    rank_stage(0, 0)
    merge_out(close)
    relay(far, 2)
    use_stage(0, 0)

    @pl.when(inner == 1)
    def _():
        ret_near(3).start()

    ret_near(2).start()
    hand_back(close, 2)
    hand_back(close, 1)
    rank_stage(2, 0)
    rank_stage(2, 1)
    hand_back(close, 0)
    use_stage(2, 0)
    use_stage(2, 1)
    merge_out(far)

    @pl.when(inner == 0)
    def _():
        ret_near(1).start()
        ret_near(3).start()

    x_all = slot_in[:, :block]
    c_all = slot_in[:, block:]
    for a in range(resident):
        gd_ref[a] = tn_dot(back_m[a], x_all) * (
            adapter_scale / jnp.maximum(jnp.full((1, block), counts[a], F32), 1.0))
        gu_ref[a] = tn_dot(inner_m[a], c_all) * (
            adapter_scale / jnp.maximum(jnp.full((1, out_block), counts[a], F32), 1.0))
    gd_copy.start()
    gu_copy.start()
    hand_back(far, 2)

    @pl.when(inner == 1)
    def _():
        ret_near(1).start()

    hand_back(far, 1)
    hand_back(far, 0)
    parts_came().wait_recv()
    backbone = parts[0].astype(F32)
    for q in range(1, tensor_count):
        backbone = backbone + part_in[q].astype(F32)
    rets_came().wait_recv()
    for j in range(seqs):
        came = ret_in[table_ref[8 + j]]
        kvo_ref[lines(j), :] = (backbone[lines(j)] + came[:, block:].astype(F32)).astype(BF16)
        tg_ref[lines(j), :] = (acc[lines(j), :] + came[:, :block].astype(F32)).astype(BF16)

    cots_came().wait_send()
    parts_came().wait_send()
    ranks_sent().wait_send()

    @pl.when(inner == 0)
    def _():
        sent(5 * half - 5).wait_send()

    @pl.when(inner == 1)
    def _():
        sent(dp_count + 6 * half - 6).wait_send()

    gd_copy.wait()
    gu_copy.wait()


def finish(pieces, *refs):
    n = len(pieces)
    given, out, sem = refs[:n], refs[n:2 * n], refs[2 * n]
    steps = [(i, p) for i in range(n) for p in range(pieces[i])]

    def move(at, i, p):
        span = given[i].shape[0] // pieces[i]
        rows = pl.ds(p * span, span)
        return pltpu.make_async_copy(given[i].at[rows], out[i].at[rows], sem.at[at])

    for at, (i, p) in enumerate(steps):
        move(at, i, p).start()
    for at, (i, p) in enumerate(steps):
        move(at, i, p).wait()


def shapes_of(rows, block, out_block, resident, rank):
    return (
        jax.ShapeDtypeStruct((rows, out_block), BF16),
        jax.ShapeDtypeStruct((rows, block), BF16),
        jax.ShapeDtypeStruct((resident, rank, block), F32),
        jax.ShapeDtypeStruct((resident, rank, out_block), F32),
    )


def direct(dp_count, tensor_count, tok, w, down, up, cot, seq_index, storage):
    resident, rank, block = down.shape
    out_block = up.shape[2]
    rows = tok.shape[0]
    seqs = seq_index.shape[0] // dp_count
    length = rows // seqs
    groups = len(slot_groups(dp_count))
    anywhere = pl.BlockSpec(memory_space=pl.ANY)
    wide = block + out_block
    vmem = pl.BlockSpec(memory_space=pltpu.VMEM)
    smem = pl.BlockSpec(memory_space=pltpu.SMEM)
    dma = pltpu.SemaphoreType.DMA
    table, weights = pl.pallas_call(
        functools.partial(routes, dp_count, seqs, resident),
        out_shape=(
            jax.ShapeDtypeStruct((2 * dp_count + seqs,), jnp.int32),
            jax.ShapeDtypeStruct((resident * dp_count + resident,), F32),
        ),
        in_specs=[smem, smem],
        out_specs=(smem, smem),
    )(seq_index, storage)
    return pl.pallas_call(
        functools.partial(kernel, dp_count, tensor_count),
        out_shape=shapes_of(rows, block, out_block, resident, rank),
        in_specs=[smem, smem, vmem, anywhere, anywhere, anywhere, vmem, vmem],
        out_specs=(vmem, vmem, anywhere, anywhere),
        scratch_shapes=[
            pltpu.VMEM(down.shape, BF16),
            pltpu.VMEM(up.shape, BF16),
            pltpu.VMEM(down.shape, F32),
            pltpu.VMEM(up.shape, F32),
            pltpu.VMEM((tensor_count, w.shape[0], out_block), BF16),
            pltpu.VMEM((dp_count * length, wide), BF16),
            pltpu.VMEM((dp_count * length, wide), BF16),
            pltpu.VMEM((dp_count, length, wide), BF16),
            pltpu.VMEM((dp_count, length, wide), BF16),
            pltpu.VMEM((tensor_count, rows, out_block), BF16),
            pltpu.VMEM((tensor_count, rows, out_block), BF16),
            pltpu.VMEM((tensor_count, rows, out_block), BF16),
            pltpu.VMEM((tensor_count, dp_count * length, 2 * rank), BF16),
            pltpu.VMEM((resident, dp_count * length, rank), BF16),
            pltpu.VMEM((resident, dp_count * length, rank), BF16),
            pltpu.VMEM((rows, block), F32),
            dma((tensor_count,)),
            dma((4,)),
            dma((dp_count,)),
            dma((dp_count,)),
            dma((dp_count,)),
            dma((dp_count,)),
            dma((tensor_count,)),
            dma((tensor_count,)),
            dma((tensor_count,)),
            dma((tensor_count,)),
            dma((groups, tensor_count)),
            dma((groups, tensor_count)),
        ],
        compiler_params=pltpu.CompilerParams(
            collective_id=1, has_side_effects=True, vmem_limit_bytes=60 * 1024 * 1024
        ),
    )(
        table, weights, tok.reshape(seqs, length, block), w, down, up, cot,
        cot.reshape(seqs, length, out_block))


def relayed(dp_count, tensor_count, table, weights, tok, w, down, up, cot, seqs):
    resident, rank, block = down.shape
    out_block = up.shape[2]
    rows = tok.shape[0]
    length = rows // seqs
    half = dp_count // 2
    anywhere = pl.BlockSpec(memory_space=pl.ANY)
    wide = block + out_block
    vmem = pl.BlockSpec(memory_space=pltpu.VMEM)
    smem = pl.BlockSpec(memory_space=pltpu.SMEM)
    dma = pltpu.SemaphoreType.DMA

    def slots(*lead):
        return pltpu.VMEM(lead + (length, wide), BF16)

    return pl.pallas_call(
        functools.partial(relay_kernel, dp_count, tensor_count),
        out_shape=shapes_of(rows, block, out_block, resident, rank),
        in_specs=[smem, smem] + [anywhere] * 5,
        out_specs=(vmem, vmem, anywhere, anywhere),
        scratch_shapes=[
            pltpu.VMEM(down.shape, BF16),
            pltpu.VMEM(up.shape, BF16),
            pltpu.VMEM(down.shape, F32),
            pltpu.VMEM(up.shape, F32),
            pltpu.VMEM((seqs, length, block), BF16),
            pltpu.VMEM((seqs, length, out_block), BF16),
            pltpu.VMEM((tensor_count, w.shape[0], out_block), BF16),
            slots(half - 1),
            slots(half - 1),
            slots(half - 1),
            pltpu.VMEM((dp_count * length, wide), BF16),
            slots(2, half - 2),
            slots(dp_count + 6 * half - 6),
            slots(dp_count - 1),
            pltpu.VMEM((tensor_count, seqs, length, out_block), BF16),
            pltpu.VMEM((tensor_count, rows, out_block), BF16),
            pltpu.VMEM((tensor_count, rows, out_block), BF16),
            pltpu.VMEM((dp_count * length, 2 * rank), BF16),
            pltpu.VMEM((tensor_count - 1, dp_count * length, 2 * rank), BF16),
            pltpu.VMEM((resident, dp_count * length, rank), BF16),
            pltpu.VMEM((resident, dp_count * length, rank), BF16),
            pltpu.VMEM((rows, block), F32),
            dma((tensor_count,)),
            dma((6,)),
            dma,
            dma,
            dma((half, 2)),
            dma((2, half - 1, 2)),
            dma((half - 1, 2)),
            dma((2, half - 1, 2)),
            dma,
            dma,
            dma,
            dma,
            dma,
            dma,
            dma((5,)),
        ],
        compiler_params=pltpu.CompilerParams(
            collective_id=0, has_side_effects=True, vmem_limit_bytes=60 * 1024 * 1024
        ),
    )(
        table, weights, tok.reshape(seqs, length, block), w, down, up, cot.reshape(seqs, length, out_block))


def on_device(dp_count, tensor_count, tok, w, down, up, cot, seq_index, storage):
    resident = down.shape[0]
    seqs = seq_index.shape[0] // dp_count
    anywhere = pl.BlockSpec(memory_space=pl.ANY)
    vmem = pl.BlockSpec(memory_space=pltpu.VMEM)
    smem = pl.BlockSpec(memory_space=pltpu.SMEM)
    dma = pltpu.SemaphoreType.DMA
    args = (tok, w, down, up, cot)
    if relay_fits(dp_count, seqs):
        table, weights, fits = pl.pallas_call(
            functools.partial(relay_routes, dp_count, seqs, resident),
            out_shape=(
                jax.ShapeDtypeStruct((32,), jnp.int32),
                jax.ShapeDtypeStruct((resident * dp_count + resident,), F32),
                jax.ShapeDtypeStruct((1,), jnp.int32),
            ),
            in_specs=[smem, smem],
            out_specs=(smem,) * 3,
        )(seq_index, storage)
        results = lax.cond(
            fits.reshape(()) > 0,
            lambda: relayed(dp_count, tensor_count, table, weights, *args, seqs),
            lambda: direct(dp_count, tensor_count, *args, seq_index, storage),
        )
    else:
        results = direct(dp_count, tensor_count, *args, seq_index, storage)
    pieces = (1, 2, resident, 1)
    return pl.pallas_call(
        functools.partial(finish, pieces),
        out_shape=tuple(jax.ShapeDtypeStruct(r.shape, r.dtype) for r in results),
        in_specs=[vmem] * 4,
        out_specs=(anywhere,) * 4,
        scratch_shapes=[dma((sum(pieces),))],
    )(*results)


def solution(mesh):
    in_specs = (
        P("dp", "tensor"),
        P("tensor", None),
        P("dp", None, "tensor"),
        P("dp", None, "tensor"),
        P("dp", "tensor"),
        P(),
        P(),
    )
    out_specs = (
        P("dp", "tensor"),
        P("dp", "tensor"),
        P("dp", None, "tensor"),
        P("dp", None, "tensor"),
    )
    return jax.shard_map(
        functools.partial(on_device, mesh.shape["dp"], mesh.shape["tensor"]),
        mesh=mesh, in_specs=in_specs, out_specs=out_specs, check_vma=False,
    )
```

```python
import functools

import jax
import jax.numpy as jnp
from jax import lax
from jax.experimental import pallas as pl
from jax.experimental.pallas import tpu as pltpu
from jax.sharding import PartitionSpec as P

adapter_scale = 0.25
MESH = pl.DeviceIdType.MESH
F32 = jnp.float32
BF16 = jnp.bfloat16


def nt_dot(a, b):
    return lax.dot_general(a, b, (((1,), (1,)), ((), ())), preferred_element_type=F32)


def tn_dot(a, b):
    return lax.dot_general(a, b, (((0,), (0,)), ((), ())), preferred_element_type=F32)


def partner(d, k, dp_count):
    out, bit = d, 1
    while bit < dp_count:
        if k & bit:
            out = out + bit - 2 * bit * lax.rem(lax.div(d, jnp.int32(bit)), jnp.int32(2))
        bit *= 2
    return out


def routes(dp_count, seqs, resident, seq_ref, store_ref, table_ref, weight_ref):
    d = lax.axis_index("dp")
    rows = [store_ref[seq_ref[d * seqs + j]] for j in range(seqs)]
    owners = [lax.div(r, jnp.int32(resident)) for r in rows]
    dist = []
    for j in range(seqs):
        slot = jnp.int32(0)
        for k in range(1, dp_count):
            slot = jnp.where(owners[j] == partner(d, k, dp_count), jnp.int32(k), slot)
        dist.append(slot)
    for j in range(seqs):
        table_ref[2 * dp_count + j] = dist[j]
    for k in range(dp_count):
        pick = jnp.int32(0)
        for j in range(seqs):
            pick = jnp.where(dist[j] == k, jnp.int32(j), pick)
        table_ref[k] = pick
    counts = [jnp.float32(0.0)] * resident
    for k in range(dp_count):
        reader = partner(d, k, dp_count)
        found = jnp.int32(-1)
        for j in range(seqs):
            local = store_ref[seq_ref[reader * seqs + j]] - d * resident
            found = jnp.where((local >= 0) & (local < resident), local, found)
        table_ref[dp_count + k] = jnp.maximum(found, 0)
        for a in range(resident):
            hit = jnp.where(found == a, jnp.float32(1.0), jnp.float32(0.0))
            weight_ref[a * dp_count + k] = hit
            counts[a] = counts[a] + hit
    for a in range(resident):
        weight_ref[resident * dp_count + a] = counts[a]


def slot_groups(dp_count):
    order = list(range(dp_count - 1, -1, -1))
    quarter = dp_count // 4
    return [order[:quarter], order[quarter:2 * quarter], order[2 * quarter:]]


def kernel(
    dp_count,
    tensor_count,
    table_ref,
    weight_ref,
    tok_ref,
    w_ref,
    down_hbm,
    up_hbm,
    cot_ref,
    cot_seq_ref,
    kvo_ref,
    tg_ref,
    gd_hbm,
    gu_hbm,
    down_ref,
    up_ref,
    gd_ref,
    gu_ref,
    w_v,
    slot_out,
    slot_in,
    ret_out,
    ret_in,
    cots,
    parts,
    part_in,
    ranks,
    back_m,
    inner_m,
    acc,
    w_sem,
    local_sem,
    slot_ssem,
    slot_rsem,
    ret_ssem,
    ret_rsem,
    cot_ssem,
    cot_rsem,
    part_ssem,
    part_rsem,
    rank_ssem,
    rank_rsem,
):
    d = lax.axis_index("dp")
    t = lax.axis_index("tensor")
    resident, rank, block = down_ref.shape
    out_block = up_ref.shape[2]
    seqs, length = tok_ref.shape[:2]
    rows = seqs * length
    groups = slot_groups(dp_count)
    starts = [sum(len(g) for g in groups[:i]) for i in range(len(groups))]

    def dp_to(k):
        return partner(d, k, dp_count)

    def t_to(q):
        return lax.rem(t + q, tensor_count)

    def t_from(q):
        return lax.rem(t + tensor_count - q, tensor_count)

    def w_copy(i):
        c = t_to(i)
        return pltpu.make_async_copy(
            w_ref.at[:, pl.ds(pl.multiple_of(c * out_block, out_block), out_block)],
            w_v.at[i],
            w_sem.at[i],
        )

    down_copy = pltpu.make_async_copy(down_hbm, down_ref, local_sem.at[0])
    up_copy = pltpu.make_async_copy(up_hbm, up_ref, local_sem.at[1])
    gd_copy = pltpu.make_async_copy(gd_ref, gd_hbm, local_sem.at[2])
    gu_copy = pltpu.make_async_copy(gu_ref, gu_hbm, local_sem.at[3])
    for i in range(tensor_count):
        w_copy(i).start()
    down_copy.start()
    up_copy.start()

    barrier = pltpu.get_barrier_semaphore()
    for k in range(1, dp_count):
        pl.semaphore_signal(barrier, inc=1, device_id={"dp": dp_to(k)}, device_id_type=MESH)
    for q in range(1, tensor_count):
        pl.semaphore_signal(barrier, inc=1, device_id={"tensor": t_to(q)}, device_id_type=MESH)

    for k in range(dp_count):
        pick = table_ref[k]
        target = slot_in if k == 0 else slot_out
        target[k * length:(k + 1) * length, :block] = tok_ref[pick]
        target[k * length:(k + 1) * length, block:] = cot_seq_ref[pick]

    pl.semaphore_wait(barrier, dp_count + tensor_count - 2)

    def cot_copy(q):
        return pltpu.make_async_remote_copy(
            cot_ref, cots.at[q], cot_ssem.at[q], cot_rsem.at[q],
            device_id={"tensor": t_to(q)}, device_id_type=MESH)

    def slot_copy(k):
        at = pl.ds(k * length, length)
        return pltpu.make_async_remote_copy(
            slot_out.at[at], slot_in.at[at], slot_ssem.at[k], slot_rsem.at[k],
            device_id={"dp": dp_to(k)}, device_id_type=MESH)

    def ret_copy(k):
        return pltpu.make_async_remote_copy(
            ret_out.at[k], ret_in.at[k], ret_ssem.at[k], ret_rsem.at[k],
            device_id={"dp": dp_to(k)}, device_id_type=MESH)

    def part_copy(q):
        return pltpu.make_async_remote_copy(
            parts.at[q], part_in.at[q], part_ssem.at[q], part_rsem.at[q],
            device_id={"tensor": t_to(q)}, device_id_type=MESH)

    def rank_rows(g):
        return pl.ds(starts[g] * length, len(groups[g]) * length)

    def rank_copy(g, q):
        return pltpu.make_async_remote_copy(
            ranks.at[t, rank_rows(g)], ranks.at[t, rank_rows(g)], rank_ssem.at[g, q], rank_rsem.at[g, q],
            device_id={"tensor": t_to(q)}, device_id_type=MESH)

    for k in range(dp_count - 1, 0, -1):
        slot_copy(k).start()
    for q in range(1, tensor_count):
        cot_copy(q).start()

    adapter_of = [table_ref[dp_count + k] for k in range(dp_count)]
    weights = [[weight_ref[a * dp_count + k] for k in range(dp_count)] for a in range(resident)]
    counts = [weight_ref[resident * dp_count + a] for a in range(resident)]

    def frozen_block(i, carry):
        w_copy(i).wait()
        parts[i] = jnp.dot(tok_ref[...].reshape(rows, block), w_v[i], preferred_element_type=F32).astype(BF16)
        return carry

    lax.fori_loop(0, tensor_count, frozen_block, 0)

    def rank_stage(g):
        for m, k in enumerate(groups[g]):
            if k:
                slot_copy(k).wait_recv()
            x = slot_in[k * length:(k + 1) * length, :block]
            c = slot_in[k * length:(k + 1) * length, block:]
            inner = nt_dot(x, down_ref[adapter_of[k]])
            back = nt_dot(c, up_ref[adapter_of[k]])
            ranks[t, (starts[g] + m) * length:(starts[g] + m + 1) * length, :] = jnp.concatenate(
                [inner, back], axis=1).astype(BF16)
        for q in range(1, tensor_count):
            rank_copy(g, q).start()

    def base_block(i, carry):
        q = lax.rem(tensor_count - i, tensor_count)
        acc[...] += nt_dot(cots[q], w_v[i])
        return carry

    def use_stage(g):
        for q in range(1, tensor_count):
            s = t_from(q)
            pltpu.make_async_remote_copy(
                ranks.at[s, rank_rows(g)], ranks.at[s, rank_rows(g)], rank_ssem.at[g, q], rank_rsem.at[g, q],
                device_id={"tensor": t_to(q)}, device_id_type=MESH).wait_recv()
        for q in range(1, tensor_count):
            rank_copy(g, q).wait_send()
        total = ranks[0, rank_rows(g)].astype(F32)
        for s in range(1, tensor_count):
            total = total + ranks[s, rank_rows(g)].astype(F32)
        for m, k in enumerate(groups[g]):
            lines = total[m * length:(m + 1) * length]
            inner = lines[:, :rank].astype(BF16)
            back = lines[:, rank:].astype(BF16)
            target = ret_out if k else ret_in
            target[k, :, :block] = (adapter_scale * jnp.dot(
                back, down_ref[adapter_of[k]], preferred_element_type=F32)).astype(BF16)
            target[k, :, block:] = (adapter_scale * jnp.dot(
                inner, up_ref[adapter_of[k]], preferred_element_type=F32)).astype(BF16)
            for a in range(resident):
                at = slice(k * length, (k + 1) * length)
                back_m[a, at, :] = (back.astype(F32) * weights[a][k]).astype(BF16)
                inner_m[a, at, :] = (inner.astype(F32) * weights[a][k]).astype(BF16)
            if k:
                ret_copy(k).start()

    for q in range(1, tensor_count):
        part_copy(q).start()
    half = max(1, tensor_count // 2)
    acc[...] = nt_dot(cot_ref[...], w_v[0])
    for q in range(1, tensor_count):
        cot_copy(q).wait_recv()
    lax.fori_loop(1, half, base_block, 0)
    down_copy.wait()
    up_copy.wait()
    rank_stage(0)
    lax.fori_loop(half, tensor_count, base_block, 0)
    use_stage(0)
    rank_stage(1)
    use_stage(1)
    rank_stage(2)
    use_stage(2)

    x_all = slot_in[:, :block]
    c_all = slot_in[:, block:]
    for a in range(resident):
        gd_ref[a] = tn_dot(back_m[a], x_all) * (
            adapter_scale / jnp.maximum(jnp.full((1, block), counts[a], F32), 1.0))
        gu_ref[a] = tn_dot(inner_m[a], c_all) * (
            adapter_scale / jnp.maximum(jnp.full((1, out_block), counts[a], F32), 1.0))

    gd_copy.start()
    gu_copy.start()
    for q in range(1, tensor_count):
        part_copy(q).wait_recv()
    backbone = parts[0].astype(F32)
    for q in range(1, tensor_count):
        backbone = backbone + part_in[q].astype(F32)
    for k in range(1, dp_count):
        ret_copy(k).wait_recv()
    for j in range(seqs):
        at = slice(j * length, (j + 1) * length)
        came = ret_in[table_ref[2 * dp_count + j]]
        kvo_ref[at, :] = (backbone[at] + came[:, block:].astype(F32)).astype(BF16)
        tg_ref[at, :] = (acc[at, :] + came[:, :block].astype(F32)).astype(BF16)

    for k in range(1, dp_count):
        slot_copy(k).wait_send()
        ret_copy(k).wait_send()
    for q in range(1, tensor_count):
        cot_copy(q).wait_send()
        part_copy(q).wait_send()
    gd_copy.wait()
    gu_copy.wait()


def mix(first, second, flag):
    return jnp.where(flag > 0, first, second)


def relay_fits(dp_count, seqs):
    return dp_count == 2 * seqs and seqs == 4


def relay_routes(dp_count, seqs, resident, seq_ref, store_ref, table_ref, weight_ref, fits_ref):
    d = lax.axis_index("dp")
    half = dp_count // 2
    xor = lax.bitwise_xor
    level = lax.div(d, jnp.int32(2))
    inner = lax.rem(lax.div(level + 1, jnp.int32(2)), jnp.int32(2))
    home = (2 - lax.div(d, jnp.int32(half))) * 2 + lax.rem(d, jnp.int32(2))
    zero, one = jnp.int32(0), jnp.int32(1)
    hub = xor(d, 2 - 2 * inner)
    worst = zero
    counts = [jnp.float32(0.0)] * resident
    for k in range(dp_count):
        p = xor(d, jnp.int32(k))
        crossing, found = zero, jnp.int32(-1)
        near = [zero] * half
        has, which = [zero] * half, [zero] * half
        apart = []
        for j in range(seqs):
            row = store_ref[seq_ref[p * seqs + j]]
            owner = lax.div(row, jnp.int32(resident))
            away = xor(owner, p)
            crossing = crossing + jnp.where(away >= half, one, zero)
            found = jnp.where(owner == d, row - d * resident, found)
            if k == 0:
                step = xor(owner, home)
                apart.append((away, step))
                for m in range(half):
                    near[m] = jnp.where(away == m, jnp.int32(j), near[m])
            if k in (0, half, half + 2):
                step = xor(owner, home if k == 0 else hub)
                for m in range(half):
                    hit = step == half - 1 - m
                    has[m] = jnp.where(hit, one, has[m])
                    which[m] = jnp.where(hit, jnp.int32(j), which[m])
        worst = jnp.maximum(worst, crossing)
        if k == 0:
            for m in range(half):
                table_ref[m] = near[m]
            table_ref[half] = jnp.where(has[0] > 0, which[0], which[1])
            table_ref[half + 1] = jnp.where((has[0] > 0) & (has[1] > 0), which[1], which[2])
            table_ref[half + 2] = jnp.where(has[3] > 0, which[3], which[2])
            place = [zero, jnp.where(has[0] > 0, one, zero), jnp.where(has[3] > 0, one, jnp.int32(2)), jnp.int32(2)]
            for j in range(seqs):
                away, step = apart[j]
                came = away
                for m in range(half):
                    came = jnp.where(step == half - 1 - m, half + place[m], came)
                table_ref[8 + j] = came
        if k in (half, half + 2):
            q = inner if k == half else 1 - inner
            table_ref[20 + 3 * q] = has[0]
            table_ref[21 + 3 * q] = has[0] * has[1]
            table_ref[22 + 3 * q] = has[3]
        s = jnp.int32(k) if k < half else xor(jnp.int32(k), 2 * inner)
        table_ref[12 + s] = jnp.maximum(found, 0)
        for a in range(resident):
            hit = jnp.where(found == a, jnp.float32(1.0), jnp.float32(0.0))
            weight_ref[a * dp_count + s] = hit
            counts[a] = counts[a] + hit
    for a in range(resident):
        weight_ref[resident * dp_count + a] = counts[a]
    fits_ref[0] = jnp.where(worst < half, one, zero)


def relay_kernel(
    dp_count,
    tensor_count,
    table_ref,
    weight_ref,
    tok_hbm,
    w_ref,
    down_hbm,
    up_hbm,
    cot_hbm,
    kvo_ref,
    tg_ref,
    gd_hbm,
    gu_hbm,
    down_ref,
    up_ref,
    gd_ref,
    gu_ref,
    tok_ref,
    cot_ref,
    w_v,
    near_out,
    cross_out,
    stage_in,
    slot_in,
    relay_out,
    bulk,
    ret_in,
    cots,
    parts,
    part_in,
    ranks,
    ranks_in,
    back_m,
    inner_m,
    acc,
    w_sem,
    local_sem,
    send_sem,
    near_rsem,
    slot_rsem,
    relay_rsem,
    stage_rsem,
    owner_rsem,
    ret_rsem,
    cot_ssem,
    cot_rsem,
    part_ssem,
    part_rsem,
    rank_ssem,
    rank_rsem,
):
    d = lax.axis_index("dp")
    t = lax.axis_index("tensor")
    resident, rank, block = down_ref.shape
    out_block = up_ref.shape[2]
    seqs, length = tok_ref.shape[:2]
    rows = seqs * length
    bit = length // 2
    half = dp_count // 2
    level = lax.div(d, jnp.int32(2))
    inner = lax.rem(lax.div(level + 1, jnp.int32(2)), jnp.int32(2))
    outer = 1 - inner
    peer = [partner(d, k, dp_count) for k in range(dp_count)]
    groups = [[0, 1, 2, 3], [4, 5], [6, 7]]
    starts = [0, 4, 6]
    close, far = 0, 1

    ret_out = bulk.at[pl.ds(0, dp_count)]
    relay_ret, back_out, relay_in = (
        bulk.at[pl.ds(dp_count + 2 * (half - 1) * n, 2 * (half - 1))] for n in range(3))

    def t_to(q):
        return lax.rem(t + q, tensor_count)

    def t_from(q):
        return lax.rem(t + tensor_count - q, tensor_count)

    def lines(s):
        return slice(s * length, (s + 1) * length)

    def w_copy(i):
        c = t_to(i)
        return pltpu.make_async_copy(
            w_ref.at[:, pl.ds(pl.multiple_of(c * out_block, out_block), out_block)],
            w_v.at[i],
            w_sem.at[i],
        )

    def over(source, target, ssem, rsem, **where):
        return pltpu.make_async_remote_copy(
            source, target, ssem, rsem, device_id=where, device_id_type=MESH)

    def piece(h):
        return pl.ds(h * bit, bit)

    def slot_at(s, h):
        return slot_in.at[pl.ds(s * length + h * bit, bit)]

    def near_copy(k):
        return over(near_out.at[k - 1], slot_in.at[pl.ds(k * length, length)], send_sem, near_rsem, dp=peer[k])

    def near_came():
        at = slot_in.at[pl.ds(length, (half - 1) * length)]
        return over(at, at, send_sem, near_rsem, dp=peer[1])

    def cross_copy(i, h):
        return over(cross_out.at[i, piece(h)], relay_in.at[i, piece(h)],
                    send_sem, relay_rsem.at[close, i, h], dp=peer[half + 2])

    def stage_copy(i, h):
        return over(cross_out.at[i, piece(h)], stage_in.at[i, piece(h)], send_sem, stage_rsem.at[i, h], dp=peer[2])

    def onward_copy(i, h):
        return over(stage_in.at[i, piece(h)], relay_in.at[half - 1 + i, piece(h)],
                    send_sem, relay_rsem.at[far, i, h], dp=peer[half + 2])

    def cross_came(q, i, h):
        at = relay_in.at[(half - 1) * q + i, piece(h)]
        return over(at, at, send_sem, relay_rsem.at[q, i, h], dp=peer[half + 2])

    def fwd_copy(q, m, h):
        s = half + 2 * q + (0 if m == 1 else 1)
        source = relay_out.at[q, m - 1, piece(h)] if m else relay_in.at[(half - 1) * q, piece(h)]
        return over(source, slot_at(s, h), send_sem, slot_rsem.at[s - half, h], dp=peer[3 - m])

    def slot_came(s, h):
        return over(slot_at(s, h), slot_at(s, h), send_sem, slot_rsem.at[s - half, h], dp=peer[1])

    def ret_near(k):
        return over(ret_out.at[k], ret_in.at[k], send_sem, ret_rsem, dp=peer[k])

    def ret_same(q, h):
        return over(ret_out.at[half + 2 * q, piece(h)], relay_ret.at[(half - 1) * q + 1, piece(h)],
                    send_sem, owner_rsem.at[q, 1, h], dp=peer[2])

    def ret_other(q, h):
        return over(ret_out.at[half + 2 * q + 1, piece(h)], relay_ret.at[(half - 1) * q + 2, piece(h)],
                    send_sem, owner_rsem.at[q, 2, h], dp=peer[1])

    def ret_merged(q, h):
        return over(back_out.at[(half - 1) * q, piece(h)], relay_ret.at[(half - 1) * q, piece(h)],
                    send_sem, owner_rsem.at[q, 0, h], dp=peer[2])

    def owner_came(q, m, h):
        at = relay_ret.at[(half - 1) * q + m, piece(h)]
        return over(at, at, send_sem, owner_rsem.at[q, m, h], dp=peer[1])

    def back_copy(q, i, h):
        source = (back_out if i else relay_ret).at[(half - 1) * q + i, piece(h)]
        return over(source, ret_in.at[half + i, piece(h)], send_sem, ret_rsem, dp=peer[half + 2 - 2 * q])

    def rets_came():
        at = ret_in.at[pl.ds(1, 2 * half - 2)]
        return over(at, at, send_sem, ret_rsem, dp=peer[1])

    def sent(count):
        return over(bulk.at[pl.ds(0, count)], bulk.at[pl.ds(0, count)], send_sem, ret_rsem, dp=peer[1])

    def cot_copy(q):
        return over(cot_ref, cots.at[q], cot_ssem, cot_rsem, tensor=t_to(q))

    def cots_came():
        at = cots.at[pl.ds(1, tensor_count - 1)]
        return over(at, at, cot_ssem, cot_rsem, tensor=t_to(1))

    def part_copy(q):
        return over(parts.at[q], part_in.at[q], part_ssem, part_rsem, tensor=t_to(q))

    def parts_came():
        at = part_in.at[pl.ds(1, tensor_count - 1)]
        return over(at, at, part_ssem, part_rsem, tensor=t_to(1))

    def spans(g, h):
        size = length if g == 0 else bit
        return [(s, slice(s * length + h * size, s * length + (h + 1) * size)) for s in groups[g]]

    def rank_at(g, h):
        return 2 * starts[g] * bit + h * len(groups[g]) * bit

    def rank_rows(g, h):
        return pl.ds(rank_at(g, h), len(groups[g]) * (length if g == 0 else bit))

    def rank_sem(g, h):
        return rank_rsem.at[2 * g - 1 + h if g else 0]

    def rank_copy(g, h, q):
        return over(ranks.at[rank_rows(g, h)], ranks_in.at[q - 1, rank_rows(g, h)],
                    rank_ssem, rank_sem(g, h), tensor=t_to(q))

    def ranks_came(g, h):
        at = ranks_in.at[:, rank_rows(g, h)]
        return over(at, at, rank_ssem, rank_sem(g, h), tensor=t_to(1))

    def ranks_sent():
        return over(ranks_in, ranks_in, rank_ssem, rank_rsem.at[0], tensor=t_to(1))

    down_copy = pltpu.make_async_copy(down_hbm, down_ref, local_sem.at[0])
    up_copy = pltpu.make_async_copy(up_hbm, up_ref, local_sem.at[1])
    gd_copy = pltpu.make_async_copy(gd_ref, gd_hbm, local_sem.at[2])
    gu_copy = pltpu.make_async_copy(gu_ref, gu_hbm, local_sem.at[3])

    tok_copy = pltpu.make_async_copy(tok_hbm, tok_ref, local_sem.at[4])
    seed_copy = pltpu.make_async_copy(cot_hbm, cot_ref, local_sem.at[5])
    tok_copy.start()
    seed_copy.start()

    barrier = pltpu.get_barrier_semaphore()
    for k in range(1, half + 1):
        pl.semaphore_signal(barrier, inc=1, device_id={"dp": peer[k]}, device_id_type=MESH)

    @pl.when(inner == 1)
    def _():
        pl.semaphore_signal(barrier, inc=1, device_id={"dp": peer[half + 2]}, device_id_type=MESH)

    for q in range(1, tensor_count):
        pl.semaphore_signal(barrier, inc=1, device_id={"tensor": t_to(q)}, device_id_type=MESH)
    for i in range(tensor_count):
        w_copy(i).start()
    down_copy.start()
    up_copy.start()
    tok_copy.wait()
    seed_copy.wait()

    for i in range(half - 1):
        pick = table_ref[half + i]
        cross_out[i, :, :block] = tok_ref[pick]
        cross_out[i, :, block:] = cot_ref[pick]
    for k in range(half):
        pick = table_ref[k]
        if k == 0:
            slot_in[:length, :block] = tok_ref[pick]
            slot_in[:length, block:] = cot_ref[pick]
        else:
            near_out[k - 1, :, :block] = tok_ref[pick]
            near_out[k - 1, :, block:] = cot_ref[pick]

    pl.semaphore_wait(barrier, half + inner + tensor_count - 1)

    @pl.when(inner == 1)
    def _():
        for i in range(half - 1):
            for h in range(2):
                cross_copy(i, h).start()

    @pl.when(inner == 0)
    def _():
        near_copy(3).start()
        for i in range(half - 1):
            for h in range(2):
                stage_copy(i, h).start()

    near_copy(1).start()
    near_copy(2).start()

    for q in range(1, tensor_count):
        cot_copy(q).start()

    adapter_of = [table_ref[12 + s] for s in range(dp_count)]
    flags = [[table_ref[20 + 3 * q + i] for i in range(3)] for q in range(2)]
    weights = [[weight_ref[a * dp_count + s] for s in range(dp_count)] for a in range(resident)]
    counts = [weight_ref[resident * dp_count + a] for a in range(resident)]

    def onward(i):
        @pl.when(inner == 1)
        def _():
            for h in range(2):
                stage_copy(i, h).wait_recv()
                onward_copy(i, h).start()

    def relay(q, i):
        base = (half - 1) * q

        @pl.when(inner == 1)
        def _():
            for h in range(2):
                at = slice(h * bit, (h + 1) * bit)
                cross_came(q, i, h).wait_recv()
                if i == 1:
                    relay_out[q, 0, at] = mix(relay_in[base + 1, at], relay_in[base, at], flags[q][0])
                if i == 2:
                    relay_out[q, 1, at] = mix(relay_in[base + 1, at], relay_in[base + 2, at], flags[q][2])
                fwd_copy(q, i, h).start()
            if i == 2:
                slot_in[lines(half + 2 * q), :] = relay_in[base + 2]

    def hand_back(q, i):
        base = (half - 1) * q

        @pl.when(inner == 1)
        def _():
            for h in range(2):
                at = slice(h * bit, (h + 1) * bit)
                owner_came(q, i, h).wait_recv()
                if i == 1:
                    back_out[base + 1, at] = mix(relay_ret[base + 1, at], relay_ret[base + 2, at], flags[q][1])
                if i == 2:
                    back_out[base + 2, at] = mix(ret_out[half + 2 * q, at], relay_ret[base + 2, at], flags[q][2])
                back_copy(q, i, h).start()

    def merge_out(q):
        base = (half - 1) * q

        @pl.when(inner == 0)
        def _():
            for h in range(2):
                at = slice(h * bit, (h + 1) * bit)
                owner_came(q, 2, h).wait_recv()
                back_out[base, at] = mix(relay_ret[base + 2, at], ret_out[half + 2 * q, at], flags[q][0])
                ret_merged(q, h).start()

    def frozen_block(i, carry):
        w_copy(i).wait()
        parts[i] = jnp.dot(tok_ref[...].reshape(rows, block), w_v[i], preferred_element_type=F32).astype(BF16)
        return carry

    def base_block(i, carry):
        q = lax.rem(tensor_count - i, tensor_count)
        acc[...] += nt_dot(cots[q].reshape(rows, out_block), w_v[i])
        return carry

    def rank_stage(g, h):
        if g == 0:
            near_came().wait_recv()
        else:
            slot_came(groups[g][1], h).wait_recv()

            @pl.when(inner == 0)
            def _():
                slot_came(groups[g][0], h).wait_recv()

        base = rank_at(g, h)
        for s, at in spans(g, h):
            x = slot_in[at, :block]
            c = slot_in[at, block:]
            inner_s = nt_dot(x, down_ref[adapter_of[s]])
            back_s = nt_dot(c, up_ref[adapter_of[s]])
            size = at.stop - at.start
            ranks[base:base + size, :] = jnp.concatenate([inner_s, back_s], axis=1).astype(BF16)
            base += size
        for q in range(1, tensor_count):
            rank_copy(g, h, q).start()

    def use_stage(g, h):
        ranks_came(g, h).wait_recv()
        total = ranks[rank_rows(g, h)].astype(F32)
        for s in range(tensor_count - 1):
            total = total + ranks_in[s, rank_rows(g, h)].astype(F32)
        base = 0
        for s, at in spans(g, h):
            size = at.stop - at.start
            part = total[base:base + size]
            base += size
            mid = part[:, :rank].astype(BF16)
            back = part[:, rank:].astype(BF16)
            target = ret_out if s else ret_in
            to = slice(at.start - s * length, at.stop - s * length)
            target[s, to, :block] = (adapter_scale * jnp.dot(
                back, down_ref[adapter_of[s]], preferred_element_type=F32)).astype(BF16)
            target[s, to, block:] = (adapter_scale * jnp.dot(
                mid, up_ref[adapter_of[s]], preferred_element_type=F32)).astype(BF16)
            for a in range(resident):
                back_m[a, at, :] = (back.astype(F32) * weights[a][s]).astype(BF16)
                inner_m[a, at, :] = (mid.astype(F32) * weights[a][s]).astype(BF16)
        if g:
            ret_other(g - 1, h).start()

            @pl.when(inner == 0)
            def _():
                ret_same(g - 1, h).start()

    middle = max(1, tensor_count // 2)
    lax.fori_loop(0, middle, frozen_block, 0)
    lax.fori_loop(middle, tensor_count, frozen_block, 0)
    for q in range(1, tensor_count):
        part_copy(q).start()
    acc[...] = nt_dot(cot_ref[...].reshape(rows, out_block), w_v[0])
    relay(close, 0)
    cots_came().wait_recv()
    lax.fori_loop(1, middle, base_block, 0)
    down_copy.wait()
    up_copy.wait()
    onward(0)

    relay(close, 1)

    @pl.when(inner == 1)
    def _():
        near_copy(3).start()

    lax.fori_loop(middle, tensor_count, base_block, 0)
    relay(close, 2)
    onward(1)
    rank_stage(1, 0)
    onward(2)
    relay(far, 0)
    rank_stage(1, 1)
    use_stage(1, 0)
    use_stage(1, 1)
    relay(far, 1)
    rank_stage(0, 0)
    merge_out(close)
    relay(far, 2)
    use_stage(0, 0)

    @pl.when(inner == 1)
    def _():
        ret_near(3).start()

    ret_near(2).start()
    hand_back(close, 2)
    hand_back(close, 1)
    rank_stage(2, 0)
    rank_stage(2, 1)
    hand_back(close, 0)
    use_stage(2, 0)
    use_stage(2, 1)
    merge_out(far)

    @pl.when(inner == 0)
    def _():
        ret_near(1).start()
        ret_near(3).start()

    x_all = slot_in[:, :block]
    c_all = slot_in[:, block:]
    for a in range(resident):
        gd_ref[a] = tn_dot(back_m[a], x_all) * (
            adapter_scale / jnp.maximum(jnp.full((1, block), counts[a], F32), 1.0))
        gu_ref[a] = tn_dot(inner_m[a], c_all) * (
            adapter_scale / jnp.maximum(jnp.full((1, out_block), counts[a], F32), 1.0))
    gd_copy.start()
    gu_copy.start()
    hand_back(far, 2)

    @pl.when(inner == 1)
    def _():
        ret_near(1).start()

    hand_back(far, 1)
    hand_back(far, 0)
    parts_came().wait_recv()
    backbone = parts[0].astype(F32)
    for q in range(1, tensor_count):
        backbone = backbone + part_in[q].astype(F32)
    rets_came().wait_recv()
    for j in range(seqs):
        came = ret_in[table_ref[8 + j]]
        kvo_ref[lines(j), :] = (backbone[lines(j)] + came[:, block:].astype(F32)).astype(BF16)
        tg_ref[lines(j), :] = (acc[lines(j), :] + came[:, :block].astype(F32)).astype(BF16)

    cots_came().wait_send()
    parts_came().wait_send()
    ranks_sent().wait_send()

    @pl.when(inner == 0)
    def _():
        sent(5 * half - 5).wait_send()

    @pl.when(inner == 1)
    def _():
        sent(dp_count + 6 * half - 6).wait_send()

    gd_copy.wait()
    gu_copy.wait()


def finish(pieces, *refs):
    n = len(pieces)
    given, out, sem = refs[:n], refs[n:2 * n], refs[2 * n]
    steps = [(i, p) for i in range(n) for p in range(pieces[i])]

    def move(at, i, p):
        span = given[i].shape[0] // pieces[i]
        rows = pl.ds(p * span, span)
        return pltpu.make_async_copy(given[i].at[rows], out[i].at[rows], sem.at[at])

    for at, (i, p) in enumerate(steps):
        move(at, i, p).start()
    for at, (i, p) in enumerate(steps):
        move(at, i, p).wait()


def shapes_of(rows, block, out_block, resident, rank):
    return (
        jax.ShapeDtypeStruct((rows, out_block), BF16),
        jax.ShapeDtypeStruct((rows, block), BF16),
        jax.ShapeDtypeStruct((resident, rank, block), F32),
        jax.ShapeDtypeStruct((resident, rank, out_block), F32),
    )


def direct(dp_count, tensor_count, tok, w, down, up, cot, seq_index, storage):
    resident, rank, block = down.shape
    out_block = up.shape[2]
    rows = tok.shape[0]
    seqs = seq_index.shape[0] // dp_count
    length = rows // seqs
    groups = len(slot_groups(dp_count))
    anywhere = pl.BlockSpec(memory_space=pl.ANY)
    wide = block + out_block
    vmem = pl.BlockSpec(memory_space=pltpu.VMEM)
    smem = pl.BlockSpec(memory_space=pltpu.SMEM)
    dma = pltpu.SemaphoreType.DMA
    table, weights = pl.pallas_call(
        functools.partial(routes, dp_count, seqs, resident),
        out_shape=(
            jax.ShapeDtypeStruct((2 * dp_count + seqs,), jnp.int32),
            jax.ShapeDtypeStruct((resident * dp_count + resident,), F32),
        ),
        in_specs=[smem, smem],
        out_specs=(smem, smem),
    )(seq_index, storage)
    return pl.pallas_call(
        functools.partial(kernel, dp_count, tensor_count),
        out_shape=shapes_of(rows, block, out_block, resident, rank),
        in_specs=[smem, smem, vmem, anywhere, anywhere, anywhere, vmem, vmem],
        out_specs=(vmem, vmem, anywhere, anywhere),
        scratch_shapes=[
            pltpu.VMEM(down.shape, BF16),
            pltpu.VMEM(up.shape, BF16),
            pltpu.VMEM(down.shape, F32),
            pltpu.VMEM(up.shape, F32),
            pltpu.VMEM((tensor_count, w.shape[0], out_block), BF16),
            pltpu.VMEM((dp_count * length, wide), BF16),
            pltpu.VMEM((dp_count * length, wide), BF16),
            pltpu.VMEM((dp_count, length, wide), BF16),
            pltpu.VMEM((dp_count, length, wide), BF16),
            pltpu.VMEM((tensor_count, rows, out_block), BF16),
            pltpu.VMEM((tensor_count, rows, out_block), BF16),
            pltpu.VMEM((tensor_count, rows, out_block), BF16),
            pltpu.VMEM((tensor_count, dp_count * length, 2 * rank), BF16),
            pltpu.VMEM((resident, dp_count * length, rank), BF16),
            pltpu.VMEM((resident, dp_count * length, rank), BF16),
            pltpu.VMEM((rows, block), F32),
            dma((tensor_count,)),
            dma((4,)),
            dma((dp_count,)),
            dma((dp_count,)),
            dma((dp_count,)),
            dma((dp_count,)),
            dma((tensor_count,)),
            dma((tensor_count,)),
            dma((tensor_count,)),
            dma((tensor_count,)),
            dma((groups, tensor_count)),
            dma((groups, tensor_count)),
        ],
        compiler_params=pltpu.CompilerParams(
            collective_id=1, has_side_effects=True, vmem_limit_bytes=60 * 1024 * 1024
        ),
    )(
        table, weights, tok.reshape(seqs, length, block), w, down, up, cot,
        cot.reshape(seqs, length, out_block))


def relayed(dp_count, tensor_count, table, weights, tok, w, down, up, cot, seqs):
    resident, rank, block = down.shape
    out_block = up.shape[2]
    rows = tok.shape[0]
    length = rows // seqs
    half = dp_count // 2
    anywhere = pl.BlockSpec(memory_space=pl.ANY)
    wide = block + out_block
    vmem = pl.BlockSpec(memory_space=pltpu.VMEM)
    smem = pl.BlockSpec(memory_space=pltpu.SMEM)
    dma = pltpu.SemaphoreType.DMA

    def slots(*lead):
        return pltpu.VMEM(lead + (length, wide), BF16)

    return pl.pallas_call(
        functools.partial(relay_kernel, dp_count, tensor_count),
        out_shape=shapes_of(rows, block, out_block, resident, rank),
        in_specs=[smem, smem] + [anywhere] * 5,
        out_specs=(vmem, vmem, anywhere, anywhere),
        scratch_shapes=[
            pltpu.VMEM(down.shape, BF16),
            pltpu.VMEM(up.shape, BF16),
            pltpu.VMEM(down.shape, F32),
            pltpu.VMEM(up.shape, F32),
            pltpu.VMEM((seqs, length, block), BF16),
            pltpu.VMEM((seqs, length, out_block), BF16),
            pltpu.VMEM((tensor_count, w.shape[0], out_block), BF16),
            slots(half - 1),
            slots(half - 1),
            slots(half - 1),
            pltpu.VMEM((dp_count * length, wide), BF16),
            slots(2, half - 2),
            slots(dp_count + 6 * half - 6),
            slots(dp_count - 1),
            pltpu.VMEM((tensor_count, seqs, length, out_block), BF16),
            pltpu.VMEM((tensor_count, rows, out_block), BF16),
            pltpu.VMEM((tensor_count, rows, out_block), BF16),
            pltpu.VMEM((dp_count * length, 2 * rank), BF16),
            pltpu.VMEM((tensor_count - 1, dp_count * length, 2 * rank), BF16),
            pltpu.VMEM((resident, dp_count * length, rank), BF16),
            pltpu.VMEM((resident, dp_count * length, rank), BF16),
            pltpu.VMEM((rows, block), F32),
            dma((tensor_count,)),
            dma((6,)),
            dma,
            dma,
            dma((half, 2)),
            dma((2, half - 1, 2)),
            dma((half - 1, 2)),
            dma((2, half - 1, 2)),
            dma,
            dma,
            dma,
            dma,
            dma,
            dma,
            dma((5,)),
        ],
        compiler_params=pltpu.CompilerParams(
            collective_id=0, has_side_effects=True, vmem_limit_bytes=60 * 1024 * 1024
        ),
    )(
        table, weights, tok.reshape(seqs, length, block), w, down, up, cot.reshape(seqs, length, out_block))


def on_device(dp_count, tensor_count, tok, w, down, up, cot, seq_index, storage):
    resident = down.shape[0]
    seqs = seq_index.shape[0] // dp_count
    anywhere = pl.BlockSpec(memory_space=pl.ANY)
    vmem = pl.BlockSpec(memory_space=pltpu.VMEM)
    smem = pl.BlockSpec(memory_space=pltpu.SMEM)
    dma = pltpu.SemaphoreType.DMA
    args = (tok, w, down, up, cot)
    if relay_fits(dp_count, seqs):
        table, weights, fits = pl.pallas_call(
            functools.partial(relay_routes, dp_count, seqs, resident),
            out_shape=(
                jax.ShapeDtypeStruct((32,), jnp.int32),
                jax.ShapeDtypeStruct((resident * dp_count + resident,), F32),
                jax.ShapeDtypeStruct((1,), jnp.int32),
            ),
            in_specs=[smem, smem],
            out_specs=(smem,) * 3,
        )(seq_index, storage)
        results = lax.cond(
            fits.reshape(()) > 0,
            lambda: relayed(dp_count, tensor_count, table, weights, *args, seqs),
            lambda: direct(dp_count, tensor_count, *args, seq_index, storage),
        )
    else:
        results = direct(dp_count, tensor_count, *args, seq_index, storage)
    pieces = (1, 2, resident, 1)
    return pl.pallas_call(
        functools.partial(finish, pieces),
        out_shape=tuple(jax.ShapeDtypeStruct(r.shape, r.dtype) for r in results),
        in_specs=[vmem] * 4,
        out_specs=(anywhere,) * 4,
        scratch_shapes=[dma((sum(pieces),))],
    )(*results)


def solution(mesh):
    in_specs = (
        P("dp", "tensor"),
        P("tensor", None),
        P("dp", None, "tensor"),
        P("dp", None, "tensor"),
        P("dp", "tensor"),
        P(),
        P(),
    )
    out_specs = (
        P("dp", "tensor"),
        P("dp", "tensor"),
        P("dp", None, "tensor"),
        P("dp", None, "tensor"),
    )
    return jax.shard_map(
        functools.partial(on_device, mesh.shape["dp"], mesh.shape["tensor"]),
        mesh=mesh, in_specs=in_specs, out_specs=out_specs, check_vma=False,
    )
```

```python
import functools

import jax
import jax.numpy as jnp
from jax import lax
from jax.experimental import pallas as pl
from jax.experimental.pallas import tpu as pltpu
from jax.sharding import PartitionSpec as P

adapter_scale = 0.25
MESH = pl.DeviceIdType.MESH
F32 = jnp.float32
BF16 = jnp.bfloat16


def nt_dot(a, b):
    return lax.dot_general(a, b, (((1,), (1,)), ((), ())), preferred_element_type=F32)


def tn_dot(a, b):
    return lax.dot_general(a, b, (((0,), (0,)), ((), ())), preferred_element_type=F32)


def partner(d, k, dp_count):
    out, bit = d, 1
    while bit < dp_count:
        if k & bit:
            out = out + bit - 2 * bit * lax.rem(lax.div(d, jnp.int32(bit)), jnp.int32(2))
        bit *= 2
    return out


def routes(dp_count, seqs, resident, seq_ref, store_ref, table_ref, weight_ref):
    d = lax.axis_index("dp")
    rows = [store_ref[seq_ref[d * seqs + j]] for j in range(seqs)]
    owners = [lax.div(r, jnp.int32(resident)) for r in rows]
    dist = []
    for j in range(seqs):
        slot = jnp.int32(0)
        for k in range(1, dp_count):
            slot = jnp.where(owners[j] == partner(d, k, dp_count), jnp.int32(k), slot)
        dist.append(slot)
    for j in range(seqs):
        table_ref[2 * dp_count + j] = dist[j]
    for k in range(dp_count):
        pick = jnp.int32(0)
        for j in range(seqs):
            pick = jnp.where(dist[j] == k, jnp.int32(j), pick)
        table_ref[k] = pick
    counts = [jnp.float32(0.0)] * resident
    for k in range(dp_count):
        reader = partner(d, k, dp_count)
        found = jnp.int32(-1)
        for j in range(seqs):
            local = store_ref[seq_ref[reader * seqs + j]] - d * resident
            found = jnp.where((local >= 0) & (local < resident), local, found)
        table_ref[dp_count + k] = jnp.maximum(found, 0)
        for a in range(resident):
            hit = jnp.where(found == a, jnp.float32(1.0), jnp.float32(0.0))
            weight_ref[a * dp_count + k] = hit
            counts[a] = counts[a] + hit
    for a in range(resident):
        weight_ref[resident * dp_count + a] = counts[a]


def slot_groups(dp_count):
    order = list(range(dp_count - 1, -1, -1))
    quarter = dp_count // 4
    return [order[:quarter], order[quarter:2 * quarter], order[2 * quarter:]]


def kernel(
    dp_count,
    tensor_count,
    table_ref,
    weight_ref,
    tok_ref,
    w_ref,
    down_hbm,
    up_hbm,
    cot_ref,
    cot_seq_ref,
    kvo_ref,
    tg_ref,
    gd_hbm,
    gu_hbm,
    down_ref,
    up_ref,
    gd_ref,
    gu_ref,
    w_v,
    slot_out,
    slot_in,
    ret_out,
    ret_in,
    cots,
    parts,
    part_in,
    ranks,
    back_m,
    inner_m,
    acc,
    w_sem,
    local_sem,
    slot_ssem,
    slot_rsem,
    ret_ssem,
    ret_rsem,
    cot_ssem,
    cot_rsem,
    part_ssem,
    part_rsem,
    rank_ssem,
    rank_rsem,
):
    d = lax.axis_index("dp")
    t = lax.axis_index("tensor")
    resident, rank, block = down_ref.shape
    out_block = up_ref.shape[2]
    seqs, length = tok_ref.shape[:2]
    rows = seqs * length
    groups = slot_groups(dp_count)
    starts = [sum(len(g) for g in groups[:i]) for i in range(len(groups))]

    def dp_to(k):
        return partner(d, k, dp_count)

    def t_to(q):
        return lax.rem(t + q, tensor_count)

    def t_from(q):
        return lax.rem(t + tensor_count - q, tensor_count)

    def w_copy(i):
        c = t_to(i)
        return pltpu.make_async_copy(
            w_ref.at[:, pl.ds(pl.multiple_of(c * out_block, out_block), out_block)],
            w_v.at[i],
            w_sem.at[i],
        )

    down_copy = pltpu.make_async_copy(down_hbm, down_ref, local_sem.at[0])
    up_copy = pltpu.make_async_copy(up_hbm, up_ref, local_sem.at[1])
    gd_copy = pltpu.make_async_copy(gd_ref, gd_hbm, local_sem.at[2])
    gu_copy = pltpu.make_async_copy(gu_ref, gu_hbm, local_sem.at[3])
    for i in range(tensor_count):
        w_copy(i).start()
    down_copy.start()
    up_copy.start()

    barrier = pltpu.get_barrier_semaphore()
    for k in range(1, dp_count):
        pl.semaphore_signal(barrier, inc=1, device_id={"dp": dp_to(k)}, device_id_type=MESH)
    for q in range(1, tensor_count):
        pl.semaphore_signal(barrier, inc=1, device_id={"tensor": t_to(q)}, device_id_type=MESH)

    for k in range(dp_count):
        pick = table_ref[k]
        target = slot_in if k == 0 else slot_out
        target[k * length:(k + 1) * length, :block] = tok_ref[pick]
        target[k * length:(k + 1) * length, block:] = cot_seq_ref[pick]

    pl.semaphore_wait(barrier, dp_count + tensor_count - 2)

    def cot_copy(q):
        return pltpu.make_async_remote_copy(
            cot_ref, cots.at[q], cot_ssem.at[q], cot_rsem.at[q],
            device_id={"tensor": t_to(q)}, device_id_type=MESH)

    def slot_copy(k):
        at = pl.ds(k * length, length)
        return pltpu.make_async_remote_copy(
            slot_out.at[at], slot_in.at[at], slot_ssem.at[k], slot_rsem.at[k],
            device_id={"dp": dp_to(k)}, device_id_type=MESH)

    def ret_copy(k):
        return pltpu.make_async_remote_copy(
            ret_out.at[k], ret_in.at[k], ret_ssem.at[k], ret_rsem.at[k],
            device_id={"dp": dp_to(k)}, device_id_type=MESH)

    def part_copy(q):
        return pltpu.make_async_remote_copy(
            parts.at[q], part_in.at[q], part_ssem.at[q], part_rsem.at[q],
            device_id={"tensor": t_to(q)}, device_id_type=MESH)

    def rank_rows(g):
        return pl.ds(starts[g] * length, len(groups[g]) * length)

    def rank_copy(g, q):
        return pltpu.make_async_remote_copy(
            ranks.at[t, rank_rows(g)], ranks.at[t, rank_rows(g)], rank_ssem.at[g, q], rank_rsem.at[g, q],
            device_id={"tensor": t_to(q)}, device_id_type=MESH)

    for k in range(dp_count - 1, 0, -1):
        slot_copy(k).start()
    for q in range(1, tensor_count):
        cot_copy(q).start()

    adapter_of = [table_ref[dp_count + k] for k in range(dp_count)]
    weights = [[weight_ref[a * dp_count + k] for k in range(dp_count)] for a in range(resident)]
    counts = [weight_ref[resident * dp_count + a] for a in range(resident)]

    def frozen_block(i, carry):
        w_copy(i).wait()
        parts[i] = jnp.dot(tok_ref[...].reshape(rows, block), w_v[i], preferred_element_type=F32).astype(BF16)
        return carry

    lax.fori_loop(0, tensor_count, frozen_block, 0)

    def rank_stage(g):
        for m, k in enumerate(groups[g]):
            if k:
                slot_copy(k).wait_recv()
            x = slot_in[k * length:(k + 1) * length, :block]
            c = slot_in[k * length:(k + 1) * length, block:]
            inner = nt_dot(x, down_ref[adapter_of[k]])
            back = nt_dot(c, up_ref[adapter_of[k]])
            ranks[t, (starts[g] + m) * length:(starts[g] + m + 1) * length, :] = jnp.concatenate(
                [inner, back], axis=1).astype(BF16)
        for q in range(1, tensor_count):
            rank_copy(g, q).start()

    def base_block(i, carry):
        q = lax.rem(tensor_count - i, tensor_count)
        acc[...] += nt_dot(cots[q], w_v[i])
        return carry

    def use_stage(g):
        for q in range(1, tensor_count):
            s = t_from(q)
            pltpu.make_async_remote_copy(
                ranks.at[s, rank_rows(g)], ranks.at[s, rank_rows(g)], rank_ssem.at[g, q], rank_rsem.at[g, q],
                device_id={"tensor": t_to(q)}, device_id_type=MESH).wait_recv()
        for q in range(1, tensor_count):
            rank_copy(g, q).wait_send()
        total = ranks[0, rank_rows(g)].astype(F32)
        for s in range(1, tensor_count):
            total = total + ranks[s, rank_rows(g)].astype(F32)
        for m, k in enumerate(groups[g]):
            lines = total[m * length:(m + 1) * length]
            inner = lines[:, :rank].astype(BF16)
            back = lines[:, rank:].astype(BF16)
            target = ret_out if k else ret_in
            target[k, :, :block] = (adapter_scale * jnp.dot(
                back, down_ref[adapter_of[k]], preferred_element_type=F32)).astype(BF16)
            target[k, :, block:] = (adapter_scale * jnp.dot(
                inner, up_ref[adapter_of[k]], preferred_element_type=F32)).astype(BF16)
            for a in range(resident):
                at = slice(k * length, (k + 1) * length)
                back_m[a, at, :] = (back.astype(F32) * weights[a][k]).astype(BF16)
                inner_m[a, at, :] = (inner.astype(F32) * weights[a][k]).astype(BF16)
            if k:
                ret_copy(k).start()

    for q in range(1, tensor_count):
        part_copy(q).start()
    half = max(1, tensor_count // 2)
    acc[...] = nt_dot(cot_ref[...], w_v[0])
    for q in range(1, tensor_count):
        cot_copy(q).wait_recv()
    lax.fori_loop(1, half, base_block, 0)
    down_copy.wait()
    up_copy.wait()
    rank_stage(0)
    lax.fori_loop(half, tensor_count, base_block, 0)
    use_stage(0)
    rank_stage(1)
    use_stage(1)
    rank_stage(2)
    use_stage(2)

    x_all = slot_in[:, :block]
    c_all = slot_in[:, block:]
    for a in range(resident):
        gd_ref[a] = tn_dot(back_m[a], x_all) * (
            adapter_scale / jnp.maximum(jnp.full((1, block), counts[a], F32), 1.0))
        gu_ref[a] = tn_dot(inner_m[a], c_all) * (
            adapter_scale / jnp.maximum(jnp.full((1, out_block), counts[a], F32), 1.0))

    gd_copy.start()
    gu_copy.start()
    for q in range(1, tensor_count):
        part_copy(q).wait_recv()
    backbone = parts[0].astype(F32)
    for q in range(1, tensor_count):
        backbone = backbone + part_in[q].astype(F32)
    for k in range(1, dp_count):
        ret_copy(k).wait_recv()
    for j in range(seqs):
        at = slice(j * length, (j + 1) * length)
        came = ret_in[table_ref[2 * dp_count + j]]
        kvo_ref[at, :] = (backbone[at] + came[:, block:].astype(F32)).astype(BF16)
        tg_ref[at, :] = (acc[at, :] + came[:, :block].astype(F32)).astype(BF16)

    for k in range(1, dp_count):
        slot_copy(k).wait_send()
        ret_copy(k).wait_send()
    for q in range(1, tensor_count):
        cot_copy(q).wait_send()
        part_copy(q).wait_send()
    gd_copy.wait()
    gu_copy.wait()


def mix(first, second, flag):
    return jnp.where(flag > 0, first, second)


def relay_fits(dp_count, seqs):
    return dp_count == 2 * seqs and seqs == 4


def relay_routes(dp_count, seqs, resident, seq_ref, store_ref, table_ref, weight_ref, fits_ref):
    d = lax.axis_index("dp")
    half = dp_count // 2
    xor = lax.bitwise_xor
    level = lax.div(d, jnp.int32(2))
    inner = lax.rem(lax.div(level + 1, jnp.int32(2)), jnp.int32(2))
    home = (2 - lax.div(d, jnp.int32(half))) * 2 + lax.rem(d, jnp.int32(2))
    zero, one = jnp.int32(0), jnp.int32(1)
    hub = xor(d, 2 - 2 * inner)
    worst = zero
    counts = [jnp.float32(0.0)] * resident
    for k in range(dp_count):
        p = xor(d, jnp.int32(k))
        crossing, found = zero, jnp.int32(-1)
        near = [zero] * half
        has, which = [zero] * half, [zero] * half
        apart = []
        for j in range(seqs):
            row = store_ref[seq_ref[p * seqs + j]]
            owner = lax.div(row, jnp.int32(resident))
            away = xor(owner, p)
            crossing = crossing + jnp.where(away >= half, one, zero)
            found = jnp.where(owner == d, row - d * resident, found)
            if k == 0:
                step = xor(owner, home)
                apart.append((away, step))
                for m in range(half):
                    near[m] = jnp.where(away == m, jnp.int32(j), near[m])
            if k in (0, half, half + 2):
                step = xor(owner, home if k == 0 else hub)
                for m in range(half):
                    hit = step == half - 1 - m
                    has[m] = jnp.where(hit, one, has[m])
                    which[m] = jnp.where(hit, jnp.int32(j), which[m])
        worst = jnp.maximum(worst, crossing)
        if k == 0:
            for m in range(half):
                table_ref[m] = near[m]
            table_ref[half] = jnp.where(has[0] > 0, which[0], which[1])
            table_ref[half + 1] = jnp.where((has[0] > 0) & (has[1] > 0), which[1], which[2])
            table_ref[half + 2] = jnp.where(has[3] > 0, which[3], which[2])
            place = [zero, jnp.where(has[0] > 0, one, zero), jnp.where(has[3] > 0, one, jnp.int32(2)), jnp.int32(2)]
            for j in range(seqs):
                away, step = apart[j]
                came = away
                for m in range(half):
                    came = jnp.where(step == half - 1 - m, half + place[m], came)
                table_ref[8 + j] = came
        if k in (half, half + 2):
            q = inner if k == half else 1 - inner
            table_ref[20 + 3 * q] = has[0]
            table_ref[21 + 3 * q] = has[0] * has[1]
            table_ref[22 + 3 * q] = has[3]
        s = jnp.int32(k) if k < half else xor(jnp.int32(k), 2 * inner)
        table_ref[12 + s] = jnp.maximum(found, 0)
        for a in range(resident):
            hit = jnp.where(found == a, jnp.float32(1.0), jnp.float32(0.0))
            weight_ref[a * dp_count + s] = hit
            counts[a] = counts[a] + hit
    for a in range(resident):
        weight_ref[resident * dp_count + a] = counts[a]
    fits_ref[0] = jnp.where(worst < half, one, zero)


def relay_kernel(
    dp_count,
    tensor_count,
    table_ref,
    weight_ref,
    tok_hbm,
    w_ref,
    down_hbm,
    up_hbm,
    cot_hbm,
    kvo_ref,
    tg_ref,
    gd_hbm,
    gu_hbm,
    down_ref,
    up_ref,
    gd_ref,
    gu_ref,
    tok_ref,
    cot_ref,
    w_v,
    near_out,
    cross_out,
    stage_in,
    slot_in,
    relay_out,
    bulk,
    ret_in,
    cots,
    parts,
    part_in,
    ranks,
    ranks_in,
    back_m,
    inner_m,
    acc,
    w_sem,
    local_sem,
    send_sem,
    near_rsem,
    slot_rsem,
    relay_rsem,
    stage_rsem,
    owner_rsem,
    ret_rsem,
    cot_ssem,
    cot_rsem,
    part_ssem,
    part_rsem,
    rank_ssem,
    rank_rsem,
):
    d = lax.axis_index("dp")
    t = lax.axis_index("tensor")
    resident, rank, block = down_ref.shape
    out_block = up_ref.shape[2]
    seqs, length = tok_ref.shape[:2]
    rows = seqs * length
    bit = length // 2
    half = dp_count // 2
    level = lax.div(d, jnp.int32(2))
    inner = lax.rem(lax.div(level + 1, jnp.int32(2)), jnp.int32(2))
    outer = 1 - inner
    peer = [partner(d, k, dp_count) for k in range(dp_count)]
    groups = [[0, 1, 2, 3], [4, 5], [6, 7]]
    starts = [0, 4, 6]
    close, far = 0, 1

    ret_out = bulk.at[pl.ds(0, dp_count)]
    relay_ret, back_out, relay_in = (
        bulk.at[pl.ds(dp_count + 2 * (half - 1) * n, 2 * (half - 1))] for n in range(3))

    def t_to(q):
        return lax.rem(t + q, tensor_count)

    def t_from(q):
        return lax.rem(t + tensor_count - q, tensor_count)

    def lines(s):
        return slice(s * length, (s + 1) * length)

    def w_copy(i):
        c = t_to(i)
        return pltpu.make_async_copy(
            w_ref.at[:, pl.ds(pl.multiple_of(c * out_block, out_block), out_block)],
            w_v.at[i],
            w_sem.at[i],
        )

    def over(source, target, ssem, rsem, **where):
        return pltpu.make_async_remote_copy(
            source, target, ssem, rsem, device_id=where, device_id_type=MESH)

    def piece(h):
        return pl.ds(h * bit, bit)

    def slot_at(s, h):
        return slot_in.at[pl.ds(s * length + h * bit, bit)]

    def near_copy(k):
        return over(near_out.at[k - 1], slot_in.at[pl.ds(k * length, length)], send_sem, near_rsem, dp=peer[k])

    def near_came():
        at = slot_in.at[pl.ds(length, (half - 1) * length)]
        return over(at, at, send_sem, near_rsem, dp=peer[1])

    def cross_copy(i, h):
        return over(cross_out.at[i, piece(h)], relay_in.at[i, piece(h)],
                    send_sem, relay_rsem.at[close, i, h], dp=peer[half + 2])

    def stage_copy(i, h):
        return over(cross_out.at[i, piece(h)], stage_in.at[i, piece(h)], send_sem, stage_rsem.at[i, h], dp=peer[2])

    def onward_copy(i, h):
        return over(stage_in.at[i, piece(h)], relay_in.at[half - 1 + i, piece(h)],
                    send_sem, relay_rsem.at[far, i, h], dp=peer[half + 2])

    def cross_came(q, i, h):
        at = relay_in.at[(half - 1) * q + i, piece(h)]
        return over(at, at, send_sem, relay_rsem.at[q, i, h], dp=peer[half + 2])

    def fwd_copy(q, m, h):
        s = half + 2 * q + (0 if m == 1 else 1)
        source = relay_out.at[q, m - 1, piece(h)] if m else relay_in.at[(half - 1) * q, piece(h)]
        return over(source, slot_at(s, h), send_sem, slot_rsem.at[s - half, h], dp=peer[3 - m])

    def slot_came(s, h):
        return over(slot_at(s, h), slot_at(s, h), send_sem, slot_rsem.at[s - half, h], dp=peer[1])

    def ret_near(k):
        return over(ret_out.at[k], ret_in.at[k], send_sem, ret_rsem, dp=peer[k])

    def ret_same(q, h):
        return over(ret_out.at[half + 2 * q, piece(h)], relay_ret.at[(half - 1) * q + 1, piece(h)],
                    send_sem, owner_rsem.at[q, 1, h], dp=peer[2])

    def ret_other(q, h):
        return over(ret_out.at[half + 2 * q + 1, piece(h)], relay_ret.at[(half - 1) * q + 2, piece(h)],
                    send_sem, owner_rsem.at[q, 2, h], dp=peer[1])

    def ret_merged(q, h):
        return over(back_out.at[(half - 1) * q, piece(h)], relay_ret.at[(half - 1) * q, piece(h)],
                    send_sem, owner_rsem.at[q, 0, h], dp=peer[2])

    def owner_came(q, m, h):
        at = relay_ret.at[(half - 1) * q + m, piece(h)]
        return over(at, at, send_sem, owner_rsem.at[q, m, h], dp=peer[1])

    def back_copy(q, i, h):
        source = (back_out if i else relay_ret).at[(half - 1) * q + i, piece(h)]
        return over(source, ret_in.at[half + i, piece(h)], send_sem, ret_rsem, dp=peer[half + 2 - 2 * q])

    def rets_came():
        at = ret_in.at[pl.ds(1, 2 * half - 2)]
        return over(at, at, send_sem, ret_rsem, dp=peer[1])

    def sent(count):
        return over(bulk.at[pl.ds(0, count)], bulk.at[pl.ds(0, count)], send_sem, ret_rsem, dp=peer[1])

    def cot_copy(q):
        return over(cot_ref, cots.at[q], cot_ssem, cot_rsem, tensor=t_to(q))

    def cots_came():
        at = cots.at[pl.ds(1, tensor_count - 1)]
        return over(at, at, cot_ssem, cot_rsem, tensor=t_to(1))

    def part_copy(q):
        return over(parts.at[q], part_in.at[q], part_ssem, part_rsem, tensor=t_to(q))

    def parts_came():
        at = part_in.at[pl.ds(1, tensor_count - 1)]
        return over(at, at, part_ssem, part_rsem, tensor=t_to(1))

    def spans(g, h):
        size = length if g == 0 else bit
        return [(s, slice(s * length + h * size, s * length + (h + 1) * size)) for s in groups[g]]

    def rank_at(g, h):
        return 2 * starts[g] * bit + h * len(groups[g]) * bit

    def rank_rows(g, h):
        return pl.ds(rank_at(g, h), len(groups[g]) * (length if g == 0 else bit))

    def rank_sem(g, h):
        return rank_rsem.at[2 * g - 1 + h if g else 0]

    def rank_copy(g, h, q):
        return over(ranks.at[rank_rows(g, h)], ranks_in.at[q - 1, rank_rows(g, h)],
                    rank_ssem, rank_sem(g, h), tensor=t_to(q))

    def ranks_came(g, h):
        at = ranks_in.at[:, rank_rows(g, h)]
        return over(at, at, rank_ssem, rank_sem(g, h), tensor=t_to(1))

    def ranks_sent():
        return over(ranks_in, ranks_in, rank_ssem, rank_rsem.at[0], tensor=t_to(1))

    down_copy = pltpu.make_async_copy(down_hbm, down_ref, local_sem.at[0])
    up_copy = pltpu.make_async_copy(up_hbm, up_ref, local_sem.at[1])
    gd_copy = pltpu.make_async_copy(gd_ref, gd_hbm, local_sem.at[2])
    gu_copy = pltpu.make_async_copy(gu_ref, gu_hbm, local_sem.at[3])

    tok_copy = pltpu.make_async_copy(tok_hbm, tok_ref, local_sem.at[4])
    seed_copy = pltpu.make_async_copy(cot_hbm, cot_ref, local_sem.at[5])

    barrier = pltpu.get_barrier_semaphore()
    for k in range(1, half + 1):
        pl.semaphore_signal(barrier, inc=1, device_id={"dp": peer[k]}, device_id_type=MESH)

    @pl.when(inner == 1)
    def _():
        pl.semaphore_signal(barrier, inc=1, device_id={"dp": peer[half + 2]}, device_id_type=MESH)

    for q in range(1, tensor_count):
        pl.semaphore_signal(barrier, inc=1, device_id={"tensor": t_to(q)}, device_id_type=MESH)
    tok_copy.start()
    seed_copy.start()
    for i in range(tensor_count):
        w_copy(i).start()
    down_copy.start()
    up_copy.start()
    tok_copy.wait()
    seed_copy.wait()

    for i in range(half - 1):
        pick = table_ref[half + i]
        cross_out[i, :, :block] = tok_ref[pick]
        cross_out[i, :, block:] = cot_ref[pick]
    for k in range(half):
        pick = table_ref[k]
        if k == 0:
            slot_in[:length, :block] = tok_ref[pick]
            slot_in[:length, block:] = cot_ref[pick]
        else:
            near_out[k - 1, :, :block] = tok_ref[pick]
            near_out[k - 1, :, block:] = cot_ref[pick]

    pl.semaphore_wait(barrier, half + inner + tensor_count - 1)

    @pl.when(inner == 1)
    def _():
        for i in range(half - 1):
            for h in range(2):
                cross_copy(i, h).start()

    @pl.when(inner == 0)
    def _():
        near_copy(3).start()
        for i in range(half - 1):
            for h in range(2):
                stage_copy(i, h).start()

    near_copy(1).start()
    near_copy(2).start()

    for q in range(1, tensor_count):
        cot_copy(q).start()

    adapter_of = [table_ref[12 + s] for s in range(dp_count)]
    flags = [[table_ref[20 + 3 * q + i] for i in range(3)] for q in range(2)]
    weights = [[weight_ref[a * dp_count + s] for s in range(dp_count)] for a in range(resident)]
    counts = [weight_ref[resident * dp_count + a] for a in range(resident)]

    def onward(i):
        @pl.when(inner == 1)
        def _():
            for h in range(2):
                stage_copy(i, h).wait_recv()
                onward_copy(i, h).start()

    def relay(q, i):
        base = (half - 1) * q

        @pl.when(inner == 1)
        def _():
            for h in range(2):
                at = slice(h * bit, (h + 1) * bit)
                cross_came(q, i, h).wait_recv()
                if i == 1:
                    relay_out[q, 0, at] = mix(relay_in[base + 1, at], relay_in[base, at], flags[q][0])
                if i == 2:
                    relay_out[q, 1, at] = mix(relay_in[base + 1, at], relay_in[base + 2, at], flags[q][2])
                fwd_copy(q, i, h).start()
            if i == 2:
                slot_in[lines(half + 2 * q), :] = relay_in[base + 2]

    def hand_back(q, i):
        base = (half - 1) * q

        @pl.when(inner == 1)
        def _():
            for h in range(2):
                at = slice(h * bit, (h + 1) * bit)
                owner_came(q, i, h).wait_recv()
                if i == 1:
                    back_out[base + 1, at] = mix(relay_ret[base + 1, at], relay_ret[base + 2, at], flags[q][1])
                if i == 2:
                    back_out[base + 2, at] = mix(ret_out[half + 2 * q, at], relay_ret[base + 2, at], flags[q][2])
                back_copy(q, i, h).start()

    def merge_out(q):
        base = (half - 1) * q

        @pl.when(inner == 0)
        def _():
            for h in range(2):
                at = slice(h * bit, (h + 1) * bit)
                owner_came(q, 2, h).wait_recv()
                back_out[base, at] = mix(relay_ret[base + 2, at], ret_out[half + 2 * q, at], flags[q][0])
                ret_merged(q, h).start()

    def frozen_block(i, carry):
        w_copy(i).wait()
        parts[i] = jnp.dot(tok_ref[...].reshape(rows, block), w_v[i], preferred_element_type=F32).astype(BF16)
        return carry

    def base_block(i, carry):
        q = lax.rem(tensor_count - i, tensor_count)
        acc[...] += nt_dot(cots[q].reshape(rows, out_block), w_v[i])
        return carry

    def rank_stage(g, h):
        if g == 0:
            near_came().wait_recv()
        else:
            slot_came(groups[g][1], h).wait_recv()

            @pl.when(inner == 0)
            def _():
                slot_came(groups[g][0], h).wait_recv()

        base = rank_at(g, h)
        for s, at in spans(g, h):
            x = slot_in[at, :block]
            c = slot_in[at, block:]
            inner_s = nt_dot(x, down_ref[adapter_of[s]])
            back_s = nt_dot(c, up_ref[adapter_of[s]])
            size = at.stop - at.start
            ranks[base:base + size, :] = jnp.concatenate([inner_s, back_s], axis=1).astype(BF16)
            base += size
        for q in range(1, tensor_count):
            rank_copy(g, h, q).start()

    def use_stage(g, h):
        ranks_came(g, h).wait_recv()
        total = ranks[rank_rows(g, h)].astype(F32)
        for s in range(tensor_count - 1):
            total = total + ranks_in[s, rank_rows(g, h)].astype(F32)
        base = 0
        for s, at in spans(g, h):
            size = at.stop - at.start
            part = total[base:base + size]
            base += size
            mid = part[:, :rank].astype(BF16)
            back = part[:, rank:].astype(BF16)
            target = ret_out if s else ret_in
            to = slice(at.start - s * length, at.stop - s * length)
            target[s, to, :block] = (adapter_scale * jnp.dot(
                back, down_ref[adapter_of[s]], preferred_element_type=F32)).astype(BF16)
            target[s, to, block:] = (adapter_scale * jnp.dot(
                mid, up_ref[adapter_of[s]], preferred_element_type=F32)).astype(BF16)
            for a in range(resident):
                back_m[a, at, :] = (back.astype(F32) * weights[a][s]).astype(BF16)
                inner_m[a, at, :] = (mid.astype(F32) * weights[a][s]).astype(BF16)
        if g:
            ret_other(g - 1, h).start()

            @pl.when(inner == 0)
            def _():
                ret_same(g - 1, h).start()

    middle = max(1, tensor_count // 2)
    lax.fori_loop(0, middle, frozen_block, 0)
    lax.fori_loop(middle, tensor_count, frozen_block, 0)
    for q in range(1, tensor_count):
        part_copy(q).start()
    acc[...] = nt_dot(cot_ref[...].reshape(rows, out_block), w_v[0])
    relay(close, 0)
    cots_came().wait_recv()
    lax.fori_loop(1, middle, base_block, 0)
    down_copy.wait()
    up_copy.wait()
    onward(0)

    relay(close, 1)

    @pl.when(inner == 1)
    def _():
        near_copy(3).start()

    lax.fori_loop(middle, tensor_count, base_block, 0)
    relay(close, 2)
    onward(1)
    rank_stage(1, 0)
    rank_stage(1, 1)
    onward(2)
    relay(far, 0)
    use_stage(1, 0)
    use_stage(1, 1)
    relay(far, 1)
    rank_stage(0, 0)
    merge_out(close)
    relay(far, 2)
    use_stage(0, 0)

    hand_back(close, 2)
    hand_back(close, 1)

    @pl.when(inner == 1)
    def _():
        ret_near(3).start()

    ret_near(2).start()
    rank_stage(2, 0)
    rank_stage(2, 1)
    hand_back(close, 0)
    use_stage(2, 0)
    use_stage(2, 1)
    merge_out(far)

    @pl.when(inner == 0)
    def _():
        ret_near(1).start()
        ret_near(3).start()

    x_all = slot_in[:, :block]
    c_all = slot_in[:, block:]
    for a in range(resident):
        gd_ref[a] = tn_dot(back_m[a], x_all) * (
            adapter_scale / jnp.maximum(jnp.full((1, block), counts[a], F32), 1.0))
        gu_ref[a] = tn_dot(inner_m[a], c_all) * (
            adapter_scale / jnp.maximum(jnp.full((1, out_block), counts[a], F32), 1.0))
    gd_copy.start()
    gu_copy.start()
    hand_back(far, 2)

    @pl.when(inner == 1)
    def _():
        ret_near(1).start()

    hand_back(far, 1)
    hand_back(far, 0)
    parts_came().wait_recv()
    backbone = parts[0].astype(F32)
    for q in range(1, tensor_count):
        backbone = backbone + part_in[q].astype(F32)
    rets_came().wait_recv()
    for j in range(seqs):
        came = ret_in[table_ref[8 + j]]
        kvo_ref[lines(j), :] = (backbone[lines(j)] + came[:, block:].astype(F32)).astype(BF16)
        tg_ref[lines(j), :] = (acc[lines(j), :] + came[:, :block].astype(F32)).astype(BF16)

    cots_came().wait_send()
    parts_came().wait_send()
    ranks_sent().wait_send()

    @pl.when(inner == 0)
    def _():
        sent(5 * half - 5).wait_send()

    @pl.when(inner == 1)
    def _():
        sent(dp_count + 6 * half - 6).wait_send()

    gd_copy.wait()
    gu_copy.wait()


def finish(pieces, *refs):
    n = len(pieces)
    given, out, sem = refs[:n], refs[n:2 * n], refs[2 * n]
    steps = [(i, p) for i in range(n) for p in range(pieces[i])]

    def move(at, i, p):
        span = given[i].shape[0] // pieces[i]
        rows = pl.ds(p * span, span)
        return pltpu.make_async_copy(given[i].at[rows], out[i].at[rows], sem.at[at])

    for at, (i, p) in enumerate(steps):
        move(at, i, p).start()
    for at, (i, p) in enumerate(steps):
        move(at, i, p).wait()


def shapes_of(rows, block, out_block, resident, rank):
    return (
        jax.ShapeDtypeStruct((rows, out_block), BF16),
        jax.ShapeDtypeStruct((rows, block), BF16),
        jax.ShapeDtypeStruct((resident, rank, block), F32),
        jax.ShapeDtypeStruct((resident, rank, out_block), F32),
    )


def direct(dp_count, tensor_count, tok, w, down, up, cot, seq_index, storage):
    resident, rank, block = down.shape
    out_block = up.shape[2]
    rows = tok.shape[0]
    seqs = seq_index.shape[0] // dp_count
    length = rows // seqs
    groups = len(slot_groups(dp_count))
    anywhere = pl.BlockSpec(memory_space=pl.ANY)
    wide = block + out_block
    vmem = pl.BlockSpec(memory_space=pltpu.VMEM)
    smem = pl.BlockSpec(memory_space=pltpu.SMEM)
    dma = pltpu.SemaphoreType.DMA
    table, weights = pl.pallas_call(
        functools.partial(routes, dp_count, seqs, resident),
        out_shape=(
            jax.ShapeDtypeStruct((2 * dp_count + seqs,), jnp.int32),
            jax.ShapeDtypeStruct((resident * dp_count + resident,), F32),
        ),
        in_specs=[smem, smem],
        out_specs=(smem, smem),
    )(seq_index, storage)
    return pl.pallas_call(
        functools.partial(kernel, dp_count, tensor_count),
        out_shape=shapes_of(rows, block, out_block, resident, rank),
        in_specs=[smem, smem, vmem, anywhere, anywhere, anywhere, vmem, vmem],
        out_specs=(vmem, vmem, anywhere, anywhere),
        scratch_shapes=[
            pltpu.VMEM(down.shape, BF16),
            pltpu.VMEM(up.shape, BF16),
            pltpu.VMEM(down.shape, F32),
            pltpu.VMEM(up.shape, F32),
            pltpu.VMEM((tensor_count, w.shape[0], out_block), BF16),
            pltpu.VMEM((dp_count * length, wide), BF16),
            pltpu.VMEM((dp_count * length, wide), BF16),
            pltpu.VMEM((dp_count, length, wide), BF16),
            pltpu.VMEM((dp_count, length, wide), BF16),
            pltpu.VMEM((tensor_count, rows, out_block), BF16),
            pltpu.VMEM((tensor_count, rows, out_block), BF16),
            pltpu.VMEM((tensor_count, rows, out_block), BF16),
            pltpu.VMEM((tensor_count, dp_count * length, 2 * rank), BF16),
            pltpu.VMEM((resident, dp_count * length, rank), BF16),
            pltpu.VMEM((resident, dp_count * length, rank), BF16),
            pltpu.VMEM((rows, block), F32),
            dma((tensor_count,)),
            dma((4,)),
            dma((dp_count,)),
            dma((dp_count,)),
            dma((dp_count,)),
            dma((dp_count,)),
            dma((tensor_count,)),
            dma((tensor_count,)),
            dma((tensor_count,)),
            dma((tensor_count,)),
            dma((groups, tensor_count)),
            dma((groups, tensor_count)),
        ],
        compiler_params=pltpu.CompilerParams(
            collective_id=1, has_side_effects=True, vmem_limit_bytes=60 * 1024 * 1024
        ),
    )(
        table, weights, tok.reshape(seqs, length, block), w, down, up, cot,
        cot.reshape(seqs, length, out_block))


def relayed(dp_count, tensor_count, table, weights, tok, w, down, up, cot, seqs):
    resident, rank, block = down.shape
    out_block = up.shape[2]
    rows = tok.shape[0]
    length = rows // seqs
    half = dp_count // 2
    anywhere = pl.BlockSpec(memory_space=pl.ANY)
    wide = block + out_block
    vmem = pl.BlockSpec(memory_space=pltpu.VMEM)
    smem = pl.BlockSpec(memory_space=pltpu.SMEM)
    dma = pltpu.SemaphoreType.DMA

    def slots(*lead):
        return pltpu.VMEM(lead + (length, wide), BF16)

    return pl.pallas_call(
        functools.partial(relay_kernel, dp_count, tensor_count),
        out_shape=shapes_of(rows, block, out_block, resident, rank),
        in_specs=[smem, smem] + [anywhere] * 5,
        out_specs=(vmem, vmem, anywhere, anywhere),
        scratch_shapes=[
            pltpu.VMEM(down.shape, BF16),
            pltpu.VMEM(up.shape, BF16),
            pltpu.VMEM(down.shape, F32),
            pltpu.VMEM(up.shape, F32),
            pltpu.VMEM((seqs, length, block), BF16),
            pltpu.VMEM((seqs, length, out_block), BF16),
            pltpu.VMEM((tensor_count, w.shape[0], out_block), BF16),
            slots(half - 1),
            slots(half - 1),
            slots(half - 1),
            pltpu.VMEM((dp_count * length, wide), BF16),
            slots(2, half - 2),
            slots(dp_count + 6 * half - 6),
            slots(dp_count - 1),
            pltpu.VMEM((tensor_count, seqs, length, out_block), BF16),
            pltpu.VMEM((tensor_count, rows, out_block), BF16),
            pltpu.VMEM((tensor_count, rows, out_block), BF16),
            pltpu.VMEM((dp_count * length, 2 * rank), BF16),
            pltpu.VMEM((tensor_count - 1, dp_count * length, 2 * rank), BF16),
            pltpu.VMEM((resident, dp_count * length, rank), BF16),
            pltpu.VMEM((resident, dp_count * length, rank), BF16),
            pltpu.VMEM((rows, block), F32),
            dma((tensor_count,)),
            dma((6,)),
            dma,
            dma,
            dma((half, 2)),
            dma((2, half - 1, 2)),
            dma((half - 1, 2)),
            dma((2, half - 1, 2)),
            dma,
            dma,
            dma,
            dma,
            dma,
            dma,
            dma((5,)),
        ],
        compiler_params=pltpu.CompilerParams(
            collective_id=0, has_side_effects=True, vmem_limit_bytes=60 * 1024 * 1024
        ),
    )(
        table, weights, tok.reshape(seqs, length, block), w, down, up, cot.reshape(seqs, length, out_block))


def on_device(dp_count, tensor_count, tok, w, down, up, cot, seq_index, storage):
    resident = down.shape[0]
    seqs = seq_index.shape[0] // dp_count
    anywhere = pl.BlockSpec(memory_space=pl.ANY)
    vmem = pl.BlockSpec(memory_space=pltpu.VMEM)
    smem = pl.BlockSpec(memory_space=pltpu.SMEM)
    dma = pltpu.SemaphoreType.DMA
    args = (tok, w, down, up, cot)
    if relay_fits(dp_count, seqs):
        table, weights, fits = pl.pallas_call(
            functools.partial(relay_routes, dp_count, seqs, resident),
            out_shape=(
                jax.ShapeDtypeStruct((32,), jnp.int32),
                jax.ShapeDtypeStruct((resident * dp_count + resident,), F32),
                jax.ShapeDtypeStruct((1,), jnp.int32),
            ),
            in_specs=[smem, smem],
            out_specs=(smem,) * 3,
        )(seq_index, storage)
        results = lax.cond(
            fits.reshape(()) > 0,
            lambda: relayed(dp_count, tensor_count, table, weights, *args, seqs),
            lambda: direct(dp_count, tensor_count, *args, seq_index, storage),
        )
    else:
        results = direct(dp_count, tensor_count, *args, seq_index, storage)
    pieces = (1, 2, resident, 1)
    return pl.pallas_call(
        functools.partial(finish, pieces),
        out_shape=tuple(jax.ShapeDtypeStruct(r.shape, r.dtype) for r in results),
        in_specs=[vmem] * 4,
        out_specs=(anywhere,) * 4,
        scratch_shapes=[dma((sum(pieces),))],
    )(*results)


def solution(mesh):
    in_specs = (
        P("dp", "tensor"),
        P("tensor", None),
        P("dp", None, "tensor"),
        P("dp", None, "tensor"),
        P("dp", "tensor"),
        P(),
        P(),
    )
    out_specs = (
        P("dp", "tensor"),
        P("dp", "tensor"),
        P("dp", None, "tensor"),
        P("dp", None, "tensor"),
    )
    return jax.shard_map(
        functools.partial(on_device, mesh.shape["dp"], mesh.shape["tensor"]),
        mesh=mesh, in_specs=in_specs, out_specs=out_specs, check_vma=False,
    )
```
